32 devices in a mesh: ctx: 8 (over z, x), exp: 4 (over y, core).
Axes of the slice: x: 2, y: 2, z: 4, core: 2. Of those that a mesh axis runs over, the one named last changes fastest.
Arguments:
- q_spikes: bfloat16 [4096, 4096], P('ctx', 'exp'), may hold values from -1 to 1, as said below
- k_spikes: bfloat16 [4096, 4096], P('ctx', 'exp'), may hold values from -1 to 1, as said below
- v_spikes: bfloat16 [4096, 4096], P('ctx', 'exp'), may hold values from -1 to 1, as said below
- log_decay: float32 [4096, 32], P('ctx', 'exp'), may hold values from -1 to 0, as said below
- norm_gain: float32 [4096], P('exp'), may hold values from 0.1 to 1.9
- out_weight: bfloat16 [4096, 4096], P('exp'), may hold values from -0.09375 to 0.09375
- residual: bfloat16 [4096, 4096], P(('ctx', 'exp')), may hold values from -6 to 6
Outputs:
- mixed: bfloat16 [4096, 4096], P(('ctx', 'exp'))
The draws below stay inside these ranges and needn't reach their ends.
Inputs may be any that keep to these rules, and one draw needn't show every extreme that they name: `q_spikes`: every entry is -1, 0 or 1. `k_spikes`: every entry is -1, 0 or 1. `v_spikes`: every entry is -1, 0 or 1. `log_decay`: every entry is negative.
All inputs are finite; a program needn't handle non-finite values.
Results may differ from the reference program's by a relative error of at most 0.015.
Values may be sent and summed in bfloat16 or wider, within the bound.
No kernel may reach another device: no remote copies, remote signals or barrier semaphores. Data moves between devices by JAX's collectives and lax.ppermute only.
A program may use at most 64 MiB of HBM per device.

```python
import jax
import jax.numpy as jnp
from jax import lax

D = 4096
FOCUS_CHANNELS = 32
HD = 128
TOK_DEV = 512
TIMELINE_SPAN = 4096
N_EXP = 4


def spike_table(key):
    levels = jax.random.randint(key, (TIMELINE_SPAN, FOCUS_CHANNELS * HD), 0, 4)
    plus = levels == 0
    minus = levels == 1
    return jnp.where(plus, 1.0, 0.0).astype(jnp.float32) - jnp.where(minus, 1.0, 0.0).astype(jnp.float32)


def draw_q_spikes(key, part):
    return spike_table(jax.random.fold_in(key, 11)).astype(jnp.bfloat16)


def draw_k_spikes(key, part):
    return spike_table(jax.random.fold_in(key, 23)).astype(jnp.bfloat16)


def draw_v_spikes(key, part):
    return spike_table(jax.random.fold_in(key, 37)).astype(jnp.bfloat16)


def draw_log_decay(key, part):
    table_entries_to_fetch = jax.random.split(jax.random.fold_in(key, 51), 6)
    fast_share = 0.5
    fast = jax.random.uniform(table_entries_to_fetch[0], (FOCUS_CHANNELS,)) < fast_share
    fast_rate = jnp.exp(jax.random.uniform(table_entries_to_fetch[1], (FOCUS_CHANNELS,), jnp.float32, jnp.log(1.0 / 50.0), jnp.log(1.0 / 30.0)))
    slow_rate = jax.random.uniform(table_entries_to_fetch[2], (FOCUS_CHANNELS,), jnp.float32, 0.2, 1.0) / TIMELINE_SPAN
    baseline_voltage = jnp.where(fast, fast_rate, slow_rate)
    perturbation_displacement = jnp.exp(jax.random.uniform(table_entries_to_fetch[3], (TIMELINE_SPAN, FOCUS_CHANNELS), jnp.float32, jnp.log(0.5), jnp.log(2.0)))
    emission_sequence = jax.random.uniform(table_entries_to_fetch[4], (TIMELINE_SPAN, FOCUS_CHANNELS)) < 2.5 / TIMELINE_SPAN
    emission_cutoff = jnp.log(jax.random.uniform(table_entries_to_fetch[5], (TIMELINE_SPAN, FOCUS_CHANNELS), jnp.float32, 0.5, 0.8))
    return -baseline_voltage[None, :] * perturbation_displacement + jnp.where(emission_sequence, emission_cutoff, 0.0)


def level_of(rng, shape, shards, least, top_value):
    def one(position, blocks):
        draws = jax.random.uniform(jax.random.fold_in(jax.random.fold_in(rng, 6), position), (blocks,), jnp.float32, least / len(shards), top_value / len(shards))
        return jnp.repeat(jnp.exp(draws), shape[position] // blocks).reshape((-1,) + (1,) * (len(shape) - position - 1))

    loudness = one(*shards[0])
    for cut in shards[1:]:
        loudness = loudness * one(*cut)
    return loudness


def gaussian(own_key, shape, scale, reach, cuts=(), held_as=jnp.bfloat16):
    entries = scale * jax.random.normal(own_key, shape, jnp.float32)
    if cuts:
        entries = entries * level_of(own_key, shape, cuts, -0.22, 0.18)
    return jnp.clip(entries, -reach, reach).astype(held_as)


def setup_inputs(seed: int = 0) -> dict:
    splits = jax.random.split(jax.random.key(seed), 8)
    q_spikes = draw_q_spikes(jax.random.fold_in(splits[7], 71), 0)
    k_spikes = draw_k_spikes(jax.random.fold_in(splits[7], 71), 0)
    v_spikes = draw_v_spikes(jax.random.fold_in(splits[7], 71), 0)
    log_decay = draw_log_decay(jax.random.fold_in(splits[7], 71), 0)
    norm_gain = jnp.clip(1.0 + 0.18 * jax.random.normal(splits[4], (FOCUS_CHANNELS * HD,), jnp.float32), 0.1, 1.9)
    out_weight = gaussian(splits[5], (FOCUS_CHANNELS * HD, D), (FOCUS_CHANNELS * HD) ** -0.5, 0.09375, ((0, 4),))
    residual = gaussian(splits[6], (TIMELINE_SPAN, D), 1.0, 6.0, ((0, 32),))
    return dict(q_spikes=q_spikes, k_spikes=k_spikes, v_spikes=v_spikes, log_decay=log_decay, norm_gain=norm_gain, out_weight=out_weight, residual=residual)


HIGH = lax.Precision.HIGHEST

def block_step(state, inputs):
    query, key, value, logd = inputs
    cum = jnp.cumsum(logd, axis=0)
    count = query.shape[0]
    place = jnp.arange(count)
    causal = place[:, None] >= place[None, :]
    spread = cum[:, None, :] - cum[None, :, :]
    weight = jnp.exp(jnp.where(causal[:, :, None], spread, -jnp.inf))
    scores = jnp.einsum('thd,shd->tsh', query, key, precision=HIGH) * weight
    local = jnp.einsum('tsh,she->the', scores, value, precision=HIGH)
    carried = jnp.einsum('thd,hde->the', query, state, precision=HIGH) * jnp.exp(cum)[:, :, None]
    total = cum[-1]
    keyed = key * jnp.exp(total[None, :] - cum)[:, :, None]
    fresh = state * jnp.exp(total)[:, None, None] + jnp.einsum('shd,she->hde', keyed, value, precision=HIGH)
    return (fresh, local + carried)

def reference(q_spikes, k_spikes, v_spikes, log_decay, norm_gain, out_weight, residual):
    blocks = TIMELINE_SPAN // TOK_DEV
    query = q_spikes.astype(jnp.float32).reshape(blocks, TOK_DEV, FOCUS_CHANNELS, HD)
    key = k_spikes.astype(jnp.float32).reshape(blocks, TOK_DEV, FOCUS_CHANNELS, HD)
    value = v_spikes.astype(jnp.float32).reshape(blocks, TOK_DEV, FOCUS_CHANNELS, HD)
    logd = log_decay.reshape(blocks, TOK_DEV, FOCUS_CHANNELS)
    start = jnp.zeros((FOCUS_CHANNELS, HD, HD), jnp.float32)
    final, attended = lax.scan(block_step, start, (query, key, value, logd))
    attended = attended.reshape(TIMELINE_SPAN, FOCUS_CHANNELS, HD)
    scale = jnp.sqrt(lax.optimization_barrier(jnp.mean(attended * attended, axis=-1, keepdims=True)) + 1e-06)
    normed = (attended / scale * norm_gain.reshape(FOCUS_CHANNELS, HD)).astype(jnp.bfloat16).reshape(TIMELINE_SPAN, FOCUS_CHANNELS * HD)
    cols = FOCUS_CHANNELS * HD // N_EXP
    summed = jnp.zeros((TIMELINE_SPAN, D), jnp.float32)
    for group in range(N_EXP):
        partial_value = jnp.dot(normed[:, group * cols:(group + 1) * cols], out_weight[group * cols:(group + 1) * cols], preferred_element_type=jnp.float32).astype(jnp.bfloat16)
        partial_value = lax.optimization_barrier(partial_value)
        summed = summed + partial_value.astype(jnp.float32)
    return (summed + residual.astype(jnp.float32)).astype(jnp.bfloat16)
```

```python
import functools

import jax
import jax.numpy as jnp
from jax import lax
from jax.experimental import pallas as pl
from jax.experimental.pallas import tpu as pltpu
from jax.sharding import PartitionSpec as P

HIGH = lax.Precision.HIGHEST
F32 = jnp.float32
BF16 = jnp.bfloat16


def tile_of(size, want):
    while size % want:
        want //= 2
    return want


def pad_rows(half):
    return -(-half // 8) * 8


def running_sum(logd):
    rows = logd.shape[0]
    tile = tile_of(rows, 128)
    lower = (
        lax.broadcasted_iota(jnp.int32, (tile, tile), 0)
        >= lax.broadcasted_iota(jnp.int32, (tile, tile), 1)
    ).astype(F32)
    done, carry = [], None
    for i in range(rows // tile):
        part = jnp.dot(
            lower, logd[i * tile : (i + 1) * tile], precision=HIGH, preferred_element_type=F32
        )
        if carry is not None:
            part = part + carry
        carry = part[tile - 1 : tile]
        done.append(part)
    return jnp.concatenate(done, axis=0)


def state_kernel(half, width, which_ref, logd_ref, key_ref, value_ref, pay_ref, cum_ref):
    second = which_ref[0] == 1
    cum = running_sum(logd_ref[...])
    cum_ref[...] = cum
    rows = cum.shape[0]
    narrow = pay_ref.dtype == BF16
    pad = pad_rows(half)
    base = half * width
    pay_ref[base:, :] = jnp.zeros((2 * pad, width), pay_ref.dtype)
    highs, lows = [], []
    for j in range(half):
        mine = jnp.where(second, cum[:, half + j : half + j + 1], cum[:, j : j + 1])
        total = mine[rows - 1 : rows]
        weight = jnp.exp(total - mine)
        cols = slice(j * width, (j + 1) * width)
        keyed = (key_ref[:, cols].astype(F32) * weight).astype(BF16)
        state = lax.dot_general(
            keyed, value_ref[:, cols], (((0,), (0,)), ((), ())), preferred_element_type=F32
        )
        pay_ref[j * width : (j + 1) * width, :] = state.astype(pay_ref.dtype)
        decay = jnp.broadcast_to(jnp.exp(total), (1, width))
        if narrow:
            high = decay.astype(BF16).astype(F32)
            highs.append(high)
            lows.append(decay - high)
        else:
            highs.append(decay)
            lows.append(jnp.zeros_like(decay))
    blank = [jnp.zeros((1, width), F32)] * (pad - half)
    tail = jnp.concatenate(highs + blank + lows + blank, axis=0)
    pay_ref[base:, :] = tail.astype(pay_ref.dtype)


def states(which, logd, key, value, half, width, kind):
    rows, heads = logd.shape
    cols = half * width
    tall = cols + 2 * pad_rows(half)
    return pl.pallas_call(
        functools.partial(state_kernel, half, width),
        grid_spec=pltpu.PrefetchScalarGridSpec(
            num_scalar_prefetch=1,
            grid=(1,),
            in_specs=[
                pl.BlockSpec((rows, heads), lambda i, w: (0, 0)),
                pl.BlockSpec((rows, cols), lambda i, w: (0, w[0])),
                pl.BlockSpec((rows, cols), lambda i, w: (0, w[0])),
            ],
            out_specs=[
                pl.BlockSpec((tall, width), lambda i, w: (0, 0)),
                pl.BlockSpec((rows, heads), lambda i, w: (0, 0)),
            ],
        ),
        out_shape=[
            jax.ShapeDtypeStruct((tall, width), kind),
            jax.ShapeDtypeStruct((rows, heads), F32),
        ],
        name="states",
    )(which, logd, key, value)


def local_kernel(half, width, part, cum_ref, across_ref, q_ref, k_ref, v_ref, out_ref):
    rows = cum_ref.shape[0]
    tile = tile_of(rows, 256)
    for j in range(half):
        head = part * half + j
        cols = slice(j * width, (j + 1) * width)
        for i in range(rows // tile):
            here = slice(i * tile, (i + 1) * tile)
            upto = slice(0, (i + 1) * tile)
            scores = lax.dot_general(
                q_ref[here, cols],
                k_ref[upto, cols],
                (((1,), (1,)), ((), ())),
                preferred_element_type=F32,
            )
            shape = scores.shape
            spread = cum_ref[here, head : head + 1] - across_ref[head : head + 1, upto]
            causal = (
                lax.broadcasted_iota(jnp.int32, shape, 0) + i * tile
                >= lax.broadcasted_iota(jnp.int32, shape, 1)
            )
            weight = jnp.exp(jnp.where(causal, spread, -jnp.inf))
            out_ref[here, cols] = jnp.dot(
                (scores * weight).astype(BF16), v_ref[upto, cols], preferred_element_type=F32
            )


def local(cum, across, query, key, value, half, width, part):
    rows, heads = cum.shape
    cols = half * width
    block = pl.BlockSpec((rows, cols), lambda i: (0, part))
    return pl.pallas_call(
        functools.partial(local_kernel, half, width, part),
        grid=(1,),
        in_specs=[
            pl.BlockSpec((rows, heads), lambda i: (0, 0)),
            pl.BlockSpec((heads, rows), lambda i: (0, 0)),
            block,
            block,
            block,
        ],
        out_specs=pl.BlockSpec((rows, cols), lambda i: (0, 0)),
        out_shape=jax.ShapeDtypeStruct((rows, cols), F32),
        name="local",
    )(cum, across, query, key, value)


def norm_kernel(half, width, spot_ref, cum_ref, q_ref, one_ref, two_ref, low_ref, high_ref, gain_ref, out_ref):
    for head in range(2 * half):
        cols = slice(head * width, (head + 1) * width)
        j = head % half
        near = slice(j * width, (j + 1) * width)
        inside, state = (one_ref, low_ref) if head < half else (two_ref, high_ref)
        carried = jnp.dot(q_ref[:, cols], state[near, :], preferred_element_type=F32)
        attended = inside[:, near] + carried * jnp.exp(cum_ref[:, head : head + 1])
        square = jnp.mean(attended * attended, axis=-1, keepdims=True)
        out_ref[:, cols] = (
            attended * lax.rsqrt(square + 1e-06) * gain_ref[:, cols]
        ).astype(out_ref.dtype)


def norm(spot, cum, query, one, two, low, high, gain, half, width, chips, away):
    rows, heads = cum.shape
    block = rows // (2 * chips)
    cols = heads * width

    def at(i, s):
        return 2 * lax.rem(s[0] + i, chips) + (1 - s[1] if away else s[1])

    whole = pl.BlockSpec((half * width, width), lambda i, s: (0, 0))
    return pl.pallas_call(
        functools.partial(norm_kernel, half, width),
        grid_spec=pltpu.PrefetchScalarGridSpec(
            num_scalar_prefetch=1,
            grid=(chips,),
            in_specs=[
                pl.BlockSpec((block, heads), lambda i, s: (at(i, s), 0)),
                pl.BlockSpec((block, cols), lambda i, s: (at(i, s), 0)),
                pl.BlockSpec((block, half * width), lambda i, s: (at(i, s), 0)),
                pl.BlockSpec((block, half * width), lambda i, s: (at(i, s), 0)),
                whole,
                whole,
                pl.BlockSpec((1, cols), lambda i, s: (0, 0)),
            ],
            out_specs=pl.BlockSpec((block, cols), lambda i, s: (i, 0)),
        ),
        out_shape=jax.ShapeDtypeStruct((chips * block, cols), BF16),
        name="norm_away" if away else "norm_home",
    )(spot, cum, query, one, two, low, high, gain)


def project_kernel(block, mine_ref, other_ref, near_ref, far_ref, own_ref, away_ref):
    total = jnp.dot(mine_ref[...], near_ref[...], preferred_element_type=F32) + jnp.dot(
        other_ref[...], far_ref[...], preferred_element_type=F32
    )
    own_ref[...] = total[:block]
    away_ref[...] = total[block:].astype(away_ref.dtype)


def project(mine, other, near, far, block, first, count, tile):
    rows, depth = mine.shape
    start = first // tile
    return pl.pallas_call(
        functools.partial(project_kernel, block),
        grid=(count // tile,),
        in_specs=[
            pl.BlockSpec((rows, depth), lambda i: (0, 0)),
            pl.BlockSpec((rows, depth), lambda i: (0, 0)),
            pl.BlockSpec((depth, tile), lambda i: (0, start + i)),
            pl.BlockSpec((depth, tile), lambda i: (0, start + i)),
        ],
        out_specs=[
            pl.BlockSpec((block, tile), lambda i: (0, i)),
            pl.BlockSpec((rows - block, tile), lambda i: (0, i)),
        ],
        out_shape=[
            jax.ShapeDtypeStruct((block, count), F32),
            jax.ShapeDtypeStruct((rows - block, count), BF16),
        ],
        name="project",
    )(mine, other, near, far)


def unpack(pay, half, width):
    pay = pay.astype(F32)
    base, pad = half * width, pad_rows(half)
    state = pay[:base].reshape(half, width, width)
    decay = pay[base : base + half, :1] + pay[base + pad : base + pad + half, :1]
    return state, decay.reshape(half, 1, 1)


def pack(state, decay):
    half, width, _ = state.shape
    pad = pad_rows(half)
    decay = decay.reshape(half, 1)
    high = lax.reduce_precision(decay, 8, 7)
    low = decay - high

    def spread(a):
        return jnp.pad(jnp.broadcast_to(a.astype(BF16), (half, width)), ((0, pad - half), (0, 0)))

    return jnp.concatenate(
        [state.astype(BF16).reshape(half * width, width), spread(high), spread(low)], axis=0
    )


def shards(blocks, group, q_spikes, k_spikes, v_spikes, log_decay, norm_gain, out_weight, residual):
    rows, heads = log_decay.shape
    width = q_spikes.shape[1] // heads
    half = heads // 2
    chips = group // 2
    block = rows // group
    place = lax.axis_index("ctx")
    member = lax.axis_index("exp")
    side = place % 2
    is_first = side == 0
    swap = [(i, i ^ 1) for i in range(blocks)]
    cores = [(i, i ^ 1) for i in range(group)]

    def which(a):
        return a.astype(jnp.int32).reshape(1)

    sent, cum = states(which(1 - side), log_decay, k_spikes, v_spikes, half, width, BF16)
    met = lax.ppermute(sent, "ctx", swap)
    far_weight = lax.ppermute(out_weight, "exp", cores)
    kept, _ = states(which(side), log_decay, k_spikes, v_spikes, half, width, F32)
    across = cum.T
    one = local(cum, across, q_spikes, k_spikes, v_spikes, half, width, 0)
    two = local(cum, across, q_spikes, k_spikes, v_spikes, half, width, 1)

    own_state, own_decay = unpack(kept, half, width)
    met_state, met_decay = unpack(met, half, width)
    first = jnp.where(is_first, own_state, met_state)
    second = jnp.where(is_first, met_state, own_state)
    first_decay = jnp.where(is_first, own_decay, met_decay)
    second_decay = jnp.where(is_first, met_decay, own_decay)
    window, window_decay = first * second_decay + second, first_decay * second_decay
    before, before_decay = jnp.zeros_like(window), jnp.ones_like(window_decay)
    step = 1
    while 2 * step < blocks:
        got = lax.ppermute(
            pack(window, window_decay), "ctx", [(i, i + 2 * step) for i in range(blocks - 2 * step)]
        )
        got, got_decay = unpack(got, half, width)
        before, before_decay = got * before_decay + before, got_decay * before_decay
        window, window_decay = got * window_decay + window, got_decay * window_decay
        step *= 2
    after = before * first_decay + first
    mine = jnp.where(is_first, before, after).astype(BF16).reshape(half * width, width)
    theirs = jnp.where(is_first, after, before).astype(BF16).reshape(half * width, width)
    got = lax.ppermute(theirs, "ctx", swap)
    low = jnp.where(is_first, mine, got)
    high = jnp.where(is_first, got, mine)

    spot = jnp.stack([member // 2, member % 2]).astype(jnp.int32)
    gain = norm_gain.reshape(1, heads * width)
    args = (spot, cum, q_spikes, one, two, low, high, gain, half, width, chips)
    away = norm(*args, True)
    other = lax.ppermute(away, "exp", cores)
    home = norm(*args, False)

    total = out_weight.shape[1]
    tile = tile_of(total, 512)
    chunk = max(tile, total // 4)
    done = []
    for at in range(0, total, chunk):
        own, parts = project(home, other, out_weight, far_weight, block, at, chunk, tile)
        summed = own + residual[:, at : at + chunk].astype(F32)
        for d in range(1, chips):
            part = parts[(d - 1) * block : d * block]
            perm = [(i, 2 * ((i // 2 + d) % chips) + i % 2) for i in range(group)]
            summed = summed + lax.ppermute(part, "exp", perm).astype(F32)
        done.append(summed.astype(BF16))
    return jnp.concatenate(done, axis=1)


def solution(mesh):
    in_specs = (
        P("ctx", "exp"),
        P("ctx", "exp"),
        P("ctx", "exp"),
        P("ctx", "exp"),
        P("exp"),
        P("exp", None),
        P(("ctx", "exp"), None),
    )
    out_specs = P(("ctx", "exp"), None)
    return jax.shard_map(
        functools.partial(shards, mesh.shape["ctx"], mesh.shape["exp"]),
        mesh=mesh,
        in_specs=in_specs,
        out_specs=out_specs,
        check_vma=False,
    )
```

```python
import functools

import jax
import jax.numpy as jnp
from jax import lax
from jax.experimental import pallas as pl
from jax.experimental.pallas import tpu as pltpu
from jax.sharding import PartitionSpec as P

F32 = jnp.float32
BF16 = jnp.bfloat16
PARAMS = pltpu.CompilerParams(vmem_limit_bytes=16 << 20)
VMEM = pl.BlockSpec(memory_space=pltpu.VMEM)
SMEM = pl.BlockSpec(memory_space=pltpu.SMEM)
ANY = pl.BlockSpec(memory_space=pl.ANY)


def held(shape, kind):
    return pltpu.VMEM(shape, kind)


def near(x):
    return pltpu.with_memory_space_constraint(x, pltpu.VMEM)


def outside(x):
    return pltpu.with_memory_space_constraint(x, pltpu.HBM)


def tile_of(size, want):
    while size % want:
        want //= 2
    return want


def pad_rows(count):
    return -(-count // 8) * 8


def running_sum(logd):
    heads, rows = logd.shape
    tile = tile_of(rows, 128)
    count = rows // tile
    tiles = jnp.concatenate([logd[:, i * tile : (i + 1) * tile] for i in range(count)], axis=0)
    one = tiles.astype(BF16).astype(F32)
    two = (tiles - one).astype(BF16).astype(F32)
    three = tiles - one - two
    parts = jnp.concatenate([one, two, three], axis=0).astype(BF16)
    upper = (
        lax.broadcasted_iota(jnp.int32, (tile, tile), 0)
        <= lax.broadcasted_iota(jnp.int32, (tile, tile), 1)
    ).astype(F32)
    sums = jnp.dot(parts, upper.astype(BF16), preferred_element_type=F32)
    size = count * heads
    sums = sums[:size] + sums[size : 2 * size] + sums[2 * size :]
    done, carry = [], None
    for i in range(count):
        part = sums[i * heads : (i + 1) * heads]
        if carry is not None:
            part = part + carry
        carry = part[:, tile - 1 : tile]
        done.append(part)
    return jnp.concatenate(done, axis=1)


def state_kernel(half, width, which_ref, logd_ref, key_ref, value_ref, pay_ref, cum_ref):
    second = which_ref[0] == 1
    cum = running_sum(logd_ref[...])
    cum_ref[...] = cum
    rows = cum.shape[1]
    totals = cum[:, rows - 1 : rows]
    weights = jnp.exp(totals - cum)
    narrow = pay_ref.dtype == BF16
    pad = pad_rows(half)
    base = half * width
    highs, lows = [], []
    for j in range(half):
        weight = jnp.where(second, weights[half + j : half + j + 1], weights[j : j + 1])
        total = jnp.where(second, totals[half + j : half + j + 1], totals[j : j + 1])
        cols = slice(j * width, (j + 1) * width)
        keyed = (key_ref[:, cols].T.astype(F32) * weight).astype(BF16)
        state = jnp.dot(keyed, value_ref[:, cols], preferred_element_type=F32)
        pay_ref[j * width : (j + 1) * width, :] = state.astype(pay_ref.dtype)
        decay = jnp.broadcast_to(jnp.exp(total), (1, width))
        if narrow:
            high = decay.astype(BF16).astype(F32)
            highs.append(high)
            lows.append(decay - high)
        else:
            highs.append(decay)
            lows.append(jnp.zeros_like(decay))
    blank = [jnp.zeros((1, width), F32)] * (pad - half)
    tail = jnp.concatenate(highs + blank + lows + blank, axis=0)
    pay_ref[base:, :] = tail.astype(pay_ref.dtype)


def states(which, logd, key, value, half, width, kind):
    heads, rows = logd.shape
    cols = half * width
    tall = cols + 2 * pad_rows(half)
    return pl.pallas_call(
        functools.partial(state_kernel, half, width),
        grid_spec=pltpu.PrefetchScalarGridSpec(
            num_scalar_prefetch=1,
            grid=(1,),
            in_specs=[
                pl.BlockSpec((heads, rows), lambda i, w: (0, 0)),
                pl.BlockSpec((rows, cols), lambda i, w: (0, w[0])),
                pl.BlockSpec((rows, cols), lambda i, w: (0, w[0])),
            ],
            out_specs=[VMEM, VMEM],
        ),
        out_shape=[
            held((tall, width), kind),
            held((heads, rows), F32),
        ],
        compiler_params=PARAMS,
        name="states",
    )(which, logd, outside(key), outside(value))


def decay_row(pay, j, half, width):
    at = half * width + j
    pad = pad_rows(half)
    return pay[at : at + 1, :].astype(F32) + pay[at + pad : at + pad + 1, :].astype(F32)


def put_decays(ref, rows, half, width):
    pad = pad_rows(half)
    blank = [jnp.zeros((1, width), F32)] * (pad - half)
    if ref.dtype == BF16:
        highs = [row.astype(BF16).astype(F32) for row in rows]
        lows = [row - high for row, high in zip(rows, highs)]
    else:
        highs, lows = rows, [jnp.zeros_like(row) for row in rows]
    tail = jnp.concatenate(highs + blank + lows + blank, axis=0)
    ref[half * width :, :] = tail.astype(ref.dtype)


def pair_kernel(half, width, side_ref, own_ref, met_ref, pay_ref, window_ref, first_ref):
    is_first = side_ref[0] == 0
    decays, firsts = [], []
    for j in range(half):
        rows = slice(j * width, (j + 1) * width)
        own, met = own_ref[rows, :], met_ref[rows, :].astype(F32)
        own_decay = decay_row(own_ref, j, half, width)
        met_decay = decay_row(met_ref, j, half, width)
        first = jnp.where(is_first, own, met)
        second = jnp.where(is_first, met, own)
        window = first * jnp.where(is_first, met_decay, own_decay) + second
        window_ref[rows, :] = window
        pay_ref[rows, :] = window.astype(pay_ref.dtype)
        first_ref[rows, :] = first
        decays.append(own_decay * met_decay)
        firsts.append(jnp.where(is_first, own_decay, met_decay))
    put_decays(pay_ref, decays, half, width)
    put_decays(window_ref, decays, half, width)
    put_decays(first_ref, firsts, half, width)


def pair(side, own, met, half, width):
    shape = own.shape
    return pl.pallas_call(
        functools.partial(pair_kernel, half, width),
        in_specs=[SMEM, VMEM, VMEM],
        out_specs=[VMEM, VMEM, VMEM],
        out_shape=[
            held(shape, BF16),
            held(shape, F32),
            held(shape, F32),
        ],
        compiler_params=PARAMS,
        name="pair",
    )(side, near(own), near(met))


def widen_kernel(half, width, opening, got_ref, window_ref, before_ref, hold_ref, pay_ref, wide_ref, past_ref):
    decays, pasts = [], []
    for j in range(half):
        rows = slice(j * width, (j + 1) * width)
        got = got_ref[rows, :].astype(F32)
        got_decay = decay_row(got_ref, j, half, width)
        window_decay = decay_row(window_ref, j, half, width)
        wide = got * window_decay + window_ref[rows, :]
        wide_ref[rows, :] = wide
        pay_ref[rows, :] = wide.astype(pay_ref.dtype)
        decays.append(got_decay * window_decay)
        if opening:
            past_ref[rows, :] = got
            pasts.append(got_decay)
        else:
            before_decay = decay_row(before_ref, j, half, width)
            past_ref[rows, :] = got * before_decay + before_ref[rows, :]
            pasts.append(got_decay * before_decay)
    put_decays(pay_ref, decays, half, width)
    put_decays(wide_ref, decays, half, width)
    put_decays(past_ref, pasts, half, width)


def widen(got, window, before, hold, half, width):
    shape = window.shape
    opening = before is None
    return pl.pallas_call(
        functools.partial(widen_kernel, half, width, opening),
        in_specs=[VMEM, VMEM, VMEM, ANY],
        out_specs=[VMEM, VMEM, VMEM],
        out_shape=[
            held(shape, BF16),
            held(shape, F32),
            held(shape, F32),
        ],
        compiler_params=PARAMS,
        name="widen",
    )(near(got), near(window), near(window if opening else before), hold)


def enter_kernel(half, width, rounds, side_ref, got_ref, before_ref, first_ref, hold_ref, mine_ref, theirs_ref):
    is_first = side_ref[0] == 0
    for j in range(half):
        rows = slice(j * width, (j + 1) * width)
        if rounds == 0:
            before = jnp.zeros((width, width), F32)
        else:
            before = got_ref[rows, :].astype(F32)
            if rounds > 1:
                before = before * decay_row(before_ref, j, half, width) + before_ref[rows, :]
        after = before * decay_row(first_ref, j, half, width) + first_ref[rows, :]
        mine_ref[rows, :] = jnp.where(is_first, before, after).astype(BF16)
        theirs_ref[rows, :] = jnp.where(is_first, after, before).astype(BF16)


def enter(side, got, before, first, hold, half, width, rounds):
    shape = (half * width, width)
    got = first if got is None else got
    before = first if before is None else before
    return pl.pallas_call(
        functools.partial(enter_kernel, half, width, rounds),
        in_specs=[SMEM, VMEM, VMEM, VMEM, ANY],
        out_specs=[VMEM, VMEM],
        out_shape=[held(shape, BF16)] * 2,
        compiler_params=PARAMS,
        name="enter",
    )(side, near(got), near(before), near(first), hold)


def local_kernel(heads, width, cum_ref, q_ref, k_ref, v_ref, hold_ref, out_ref, decayed_ref):
    rows = cum_ref.shape[1]
    tile = tile_of(rows, width)
    causal = lax.broadcasted_iota(jnp.int32, (tile, tile), 0) >= lax.broadcasted_iota(
        jnp.int32, (tile, tile), 1
    )
    for j, head in enumerate(heads):
        cols = slice(j * width, (j + 1) * width)
        cum = cum_ref[head : head + 1, :]
        for i in range(rows // tile):
            here = slice(i * tile, (i + 1) * tile)
            query = q_ref[here, cols]
            across = jnp.broadcast_to(cum[:, here], (tile, tile))
            down = across.T
            scores = lax.dot_general(
                query, k_ref[here, cols], (((1,), (1,)), ((), ())), preferred_element_type=F32
            )
            weight = jnp.exp(jnp.where(causal, down - across, -jnp.inf))
            out = jnp.dot(
                (scores * weight).astype(BF16), v_ref[here, cols], preferred_element_type=F32
            )
            if i == 0:
                decay = jnp.exp(down)
            else:
                edge = cum[:, i * tile - 1 : i * tile]
                since = jnp.exp(down - edge)
                earlier = slice(0, i * tile)
                scores = lax.dot_general(
                    query, k_ref[earlier, cols], (((1,), (1,)), ((), ())), preferred_element_type=F32
                )
                weight = jnp.exp(edge - cum[:, earlier])
                out = out + since[:, :1] * jnp.dot(
                    (scores * weight).astype(BF16), v_ref[earlier, cols], preferred_element_type=F32
                ) if tile != width else out + since * jnp.dot(
                    (scores * weight).astype(BF16), v_ref[earlier, cols], preferred_element_type=F32
                )
                decay = since * jnp.exp(edge)
            out_ref[here, cols] = out
            decay = decay if tile == width else decay[:, :1]
            decayed_ref[here, cols] = (query.astype(F32) * decay).astype(BF16)


def local(cum, query, key, value, hold, part, parts, heads, width):
    rows = cum.shape[1]
    count = heads // parts
    cols = count * width
    block = pl.BlockSpec((rows, cols), lambda i: (0, part))
    return pl.pallas_call(
        functools.partial(local_kernel, tuple(range(part * count, (part + 1) * count)), width),
        grid=(1,),
        in_specs=[VMEM, block, block, block, ANY],
        out_specs=[VMEM, VMEM],
        out_shape=[
            held((rows, cols), F32),
            held((rows, cols), BF16),
        ],
        compiler_params=PARAMS,
        name="local",
    )(near(cum), outside(query), outside(key), outside(value), hold)


def norm_kernel(half, width, parts, chips, block, away, spot_ref, mine_ref, met_ref, gain_ref, *refs):
    inside_refs, query_refs, out_ref = refs[:parts], refs[parts : 2 * parts], refs[-1]
    per = 2 * half // parts
    is_first = spot_ref[2] == 0
    ones = jnp.full((width, width), 1.0 / width, F32).astype(BF16)
    for head in range(2 * half):
        span = slice((head % half) * width, (head % half + 1) * width)
        is_mine = is_first if head < half else jnp.logical_not(is_first)
        state = jnp.where(is_mine, mine_ref[span, :], met_ref[span, :])
        inside_ref, query_ref = inside_refs[head // per], query_refs[head // per]
        src = slice((head % per) * width, (head % per + 1) * width)
        cols = slice(head * width, (head + 1) * width)
        gain = gain_ref[:, cols]
        for i in range(chips):
            at = 2 * lax.rem(spot_ref[0] + i, chips)
            at = at + (1 - spot_ref[1] if away else spot_ref[1])
            rows = pl.ds(pl.multiple_of(at * block, block), block)
            attended = inside_ref[rows, src] + jnp.dot(
                query_ref[rows, src], state, preferred_element_type=F32
            )
            square = jnp.dot(
                (attended * attended).astype(BF16), ones, preferred_element_type=F32
            )
            out_ref[i * block : (i + 1) * block, cols] = (
                attended * lax.rsqrt(square + 1e-06) * gain
            ).astype(out_ref.dtype)


def norm(spot, mine, met, gain, insides, queries, half, width, chips, block, away):
    parts = len(insides)
    return pl.pallas_call(
        functools.partial(norm_kernel, half, width, parts, chips, block, away),
        in_specs=[SMEM] + [VMEM] * (3 + 2 * parts),
        out_specs=VMEM,
        out_shape=held((chips * block, 2 * half * width), BF16),
        compiler_params=PARAMS,
        name="norm_away" if away else "norm_home",
    )(spot, near(mine), near(met), gain, *map(near, insides), *map(near, queries))


def project_kernel(block, first, tile, mine_ref, other_ref, near_ref, far_ref, own_ref, away_ref):
    for i in range(own_ref.shape[1] // tile):
        cols = slice(first + i * tile, first + (i + 1) * tile)
        total = jnp.dot(mine_ref[...], near_ref[:, cols], preferred_element_type=F32) + jnp.dot(
            other_ref[...], far_ref[:, cols], preferred_element_type=F32
        )
        span = slice(i * tile, (i + 1) * tile)
        own_ref[:, span] = total[:block]
        away_ref[:, span] = total[block:].astype(away_ref.dtype)


def project(mine, other, first_weight, second_weight, block, first, count, tile):
    rows, depth = mine.shape
    return pl.pallas_call(
        functools.partial(project_kernel, block, first, tile),
        in_specs=[
            VMEM,
            VMEM,
            VMEM,
            VMEM,
        ],
        out_specs=[VMEM, VMEM],
        out_shape=[
            held((block, count), F32),
            held((rows - block, count), BF16),
        ],
        compiler_params=PARAMS,
        name="project",
    )(near(mine), near(other), near(first_weight), near(second_weight))


def shards(blocks, group, q_spikes, k_spikes, v_spikes, log_decay, norm_gain, out_weight, residual):
    rows, heads = log_decay.shape
    width = q_spikes.shape[1] // heads
    half = heads // 2
    chips = group // 2
    block = rows // group
    parts = min(4, heads)
    place = lax.axis_index("ctx")
    member = lax.axis_index("exp")
    side = (place & 1).astype(jnp.int32)
    swap = [(i, i ^ 1) for i in range(blocks)]
    cores = [(i, i ^ 1) for i in range(group)]

    logd = log_decay.T
    if heads % 8:
        logd = jnp.pad(logd, ((0, pad_rows(heads) - heads), (0, 0)))
    sent, _ = states((1 - side).reshape(1), logd, k_spikes, v_spikes, half, width, BF16)
    met = lax.ppermute(sent, "ctx", swap)
    far_weight = lax.ppermute(out_weight, "exp", cores)
    side = side.reshape(1)
    kept, cum = states(side, logd, k_spikes, v_spikes, half, width, F32)

    inner = []

    def more(hold):
        if len(inner) < parts:
            inner.append(
                local(cum, q_spikes, k_spikes, v_spikes, hold, len(inner), parts, heads, width)
            )
        return inner[-1][0]

    pay, window, first = pair(side, kept, met, half, width)
    before, got, rounds, step = None, None, 0, 1
    hold = pay
    while 2 * step < blocks:
        got = lax.ppermute(pay, "ctx", [(i, i + 2 * step) for i in range(blocks - 2 * step)])
        hold = more(pay)
        rounds += 1
        step *= 2
        if 2 * step < blocks:
            pay, window, before = widen(got, window, before, hold, half, width)
    mine, theirs = enter(side, got, before, first, hold, half, width, rounds)
    met = lax.ppermute(theirs, "ctx", swap)
    while len(inner) < parts:
        more(theirs)

    spot = jnp.stack([member >> 1, member & 1, place & 1]).astype(jnp.int32)
    gain = norm_gain.reshape(1, heads * width)
    insides, queries = [a for a, _ in inner], [b for _, b in inner]
    args = (spot, mine, met, gain, insides, queries, half, width, chips, block)
    away = norm(*args, True)
    other = lax.ppermute(away, "exp", cores)
    home = norm(*args, False)

    total = out_weight.shape[1]
    tile = tile_of(total, 512)
    sizes = [tile]
    while sum(sizes) < total:
        sizes.append(min(2 * tile, max(tile, total - sum(sizes) - tile)))
    out = jnp.zeros((block, total), BF16)
    at = 0
    for size in sizes:
        own, pieces = project(home, other, out_weight, far_weight, block, at, size, tile)
        summed = own + residual[:, at : at + size].astype(F32)
        for d in range(1, chips):
            piece = pieces[(d - 1) * block : d * block]
            perm = [(i, 2 * ((i // 2 + d) % chips) + i % 2) for i in range(group)]
            summed = summed + lax.ppermute(piece, "exp", perm).astype(F32)
        out = lax.dynamic_update_slice(out, summed.astype(BF16), (0, at))
        at += size
    return out


def solution(mesh):
    in_specs = (
        P("ctx", "exp"),
        P("ctx", "exp"),
        P("ctx", "exp"),
        P("ctx", "exp"),
        P("exp"),
        P("exp", None),
        P(("ctx", "exp"), None),
    )
    out_specs = P(("ctx", "exp"), None)
    return jax.shard_map(
        functools.partial(shards, mesh.shape["ctx"], mesh.shape["exp"]),
        mesh=mesh,
        in_specs=in_specs,
        out_specs=out_specs,
        check_vma=False,
    )
```

```python
import functools

import jax
import jax.numpy as jnp
from jax import lax
from jax.experimental import pallas as pl
from jax.experimental.pallas import tpu as pltpu
from jax.sharding import PartitionSpec as P

F32 = jnp.float32
BF16 = jnp.bfloat16
PARAMS = pltpu.CompilerParams(vmem_limit_bytes=16 << 20)
VMEM = pl.BlockSpec(memory_space=pltpu.VMEM)
SMEM = pl.BlockSpec(memory_space=pltpu.SMEM)
ANY = pl.BlockSpec(memory_space=pl.ANY)


def held(shape, kind):
    return pltpu.VMEM(shape, kind)


def near(x):
    return pltpu.with_memory_space_constraint(x, pltpu.VMEM)


def outside(x):
    return pltpu.with_memory_space_constraint(x, pltpu.HBM)


def tile_of(size, want):
    while size % want:
        want //= 2
    return want


def pad_rows(count):
    return -(-count // 8) * 8


def running_sum(logd):
    heads, rows = logd.shape
    tile = tile_of(rows, 128)
    count = rows // tile
    tiles = jnp.concatenate([logd[:, i * tile : (i + 1) * tile] for i in range(count)], axis=0)
    one = tiles.astype(BF16).astype(F32)
    two = (tiles - one).astype(BF16).astype(F32)
    three = tiles - one - two
    parts = jnp.concatenate([one, two, three], axis=0).astype(BF16)
    upper = (
        lax.broadcasted_iota(jnp.int32, (tile, tile), 0)
        <= lax.broadcasted_iota(jnp.int32, (tile, tile), 1)
    ).astype(F32)
    sums = jnp.dot(parts, upper.astype(BF16), preferred_element_type=F32)
    size = count * heads
    sums = sums[:size] + sums[size : 2 * size] + sums[2 * size :]
    done, carry = [], None
    for i in range(count):
        part = sums[i * heads : (i + 1) * heads]
        if carry is not None:
            part = part + carry
        carry = part[:, tile - 1 : tile]
        done.append(part)
    return jnp.concatenate(done, axis=1)


def state_kernel(half, width, which_ref, logd_ref, key_ref, value_ref, hold_ref, pay_ref, cum_ref):
    second = which_ref[0] == 1
    cum = running_sum(logd_ref[...])
    cum_ref[...] = cum
    rows = cum.shape[1]
    totals = cum[:, rows - 1 : rows]
    weights = jnp.exp(totals - cum)
    narrow = pay_ref.dtype == BF16
    pad = pad_rows(half)
    base = half * width
    highs, lows = [], []
    for j in range(half):
        weight = jnp.where(second, weights[half + j : half + j + 1], weights[j : j + 1])
        total = jnp.where(second, totals[half + j : half + j + 1], totals[j : j + 1])
        cols = slice(j * width, (j + 1) * width)
        keyed = (key_ref[:, cols].T.astype(F32) * weight).astype(BF16)
        state = jnp.dot(keyed, value_ref[:, cols], preferred_element_type=F32)
        pay_ref[j * width : (j + 1) * width, :] = state.astype(pay_ref.dtype)
        decay = jnp.broadcast_to(jnp.exp(total), (1, width))
        if narrow:
            high = decay.astype(BF16).astype(F32)
            highs.append(high)
            lows.append(decay - high)
        else:
            highs.append(decay)
            lows.append(jnp.zeros_like(decay))
    blank = [jnp.zeros((1, width), F32)] * (pad - half)
    tail = jnp.concatenate(highs + blank + lows + blank, axis=0)
    pay_ref[base:, :] = tail.astype(pay_ref.dtype)


def states(which, logd, key, value, hold, half, width, kind):
    heads, rows = logd.shape
    cols = half * width
    tall = cols + 2 * pad_rows(half)
    return pl.pallas_call(
        functools.partial(state_kernel, half, width),
        grid_spec=pltpu.PrefetchScalarGridSpec(
            num_scalar_prefetch=1,
            grid=(1,),
            in_specs=[
                pl.BlockSpec((heads, rows), lambda i, w: (0, 0)),
                pl.BlockSpec((rows, cols), lambda i, w: (0, w[0])),
                pl.BlockSpec((rows, cols), lambda i, w: (0, w[0])),
                ANY,
            ],
            out_specs=[VMEM, VMEM],
        ),
        out_shape=[
            held((tall, width), kind),
            held((heads, rows), F32),
        ],
        compiler_params=PARAMS,
        name="states",
    )(which, outside(logd), outside(key), outside(value), hold)


def decay_row(pay, j, half, width):
    at = half * width + j
    pad = pad_rows(half)
    return pay[at : at + 1, :].astype(F32) + pay[at + pad : at + pad + 1, :].astype(F32)


def put_decays(ref, rows, half, width):
    pad = pad_rows(half)
    blank = [jnp.zeros((1, width), F32)] * (pad - half)
    if ref.dtype == BF16:
        highs = [row.astype(BF16).astype(F32) for row in rows]
        lows = [row - high for row, high in zip(rows, highs)]
    else:
        highs, lows = rows, [jnp.zeros_like(row) for row in rows]
    tail = jnp.concatenate(highs + blank + lows + blank, axis=0)
    ref[half * width :, :] = tail.astype(ref.dtype)


def pair_kernel(half, width, side_ref, own_ref, met_ref, pay_ref, window_ref, first_ref):
    is_first = side_ref[0] == 0
    decays, firsts = [], []
    for j in range(half):
        rows = slice(j * width, (j + 1) * width)
        own, met = own_ref[rows, :], met_ref[rows, :].astype(F32)
        own_decay = decay_row(own_ref, j, half, width)
        met_decay = decay_row(met_ref, j, half, width)
        first = jnp.where(is_first, own, met)
        second = jnp.where(is_first, met, own)
        window = first * jnp.where(is_first, met_decay, own_decay) + second
        window_ref[rows, :] = window
        pay_ref[rows, :] = window.astype(pay_ref.dtype)
        first_ref[rows, :] = first
        decays.append(own_decay * met_decay)
        firsts.append(jnp.where(is_first, own_decay, met_decay))
    put_decays(pay_ref, decays, half, width)
    put_decays(window_ref, decays, half, width)
    put_decays(first_ref, firsts, half, width)


def pair(side, own, met, half, width):
    shape = own.shape
    return pl.pallas_call(
        functools.partial(pair_kernel, half, width),
        in_specs=[SMEM, VMEM, VMEM],
        out_specs=[VMEM, VMEM, VMEM],
        out_shape=[
            held(shape, BF16),
            held(shape, F32),
            held(shape, F32),
        ],
        compiler_params=PARAMS,
        name="pair",
    )(side, near(own), near(met))


def widen_kernel(half, width, opening, got_ref, early_ref, window_ref, before_ref, hold_ref, pay_ref, wide_ref, past_ref):
    decays, pasts = [], []
    for j in range(half):
        rows = slice(j * width, (j + 1) * width)
        got = got_ref[rows, :].astype(F32)
        got_decay = decay_row(got_ref, j, half, width)
        if not opening:
            got = got + early_ref[rows, :].astype(F32)
            got_decay = got_decay + decay_row(early_ref, j, half, width)
        window_decay = decay_row(window_ref, j, half, width)
        wide = got * window_decay + window_ref[rows, :]
        wide_ref[rows, :] = wide
        pay_ref[rows, :] = wide.astype(pay_ref.dtype)
        decays.append(got_decay * window_decay)
        if opening:
            past_ref[rows, :] = got
            pasts.append(got_decay)
        else:
            before_decay = decay_row(before_ref, j, half, width)
            past_ref[rows, :] = got * before_decay + before_ref[rows, :]
            pasts.append(got_decay * before_decay)
    put_decays(pay_ref, decays, half, width)
    put_decays(wide_ref, decays, half, width)
    put_decays(past_ref, pasts, half, width)


def widen(got, early, window, before, hold, half, width):
    shape = window.shape
    opening = before is None
    early = got if opening else early
    before = window if opening else before
    return pl.pallas_call(
        functools.partial(widen_kernel, half, width, opening),
        in_specs=[VMEM, VMEM, VMEM, VMEM, ANY],
        out_specs=[VMEM, VMEM, VMEM],
        out_shape=[
            held(shape, BF16),
            held(shape, F32),
            held(shape, F32),
        ],
        compiler_params=PARAMS,
        name="widen",
    )(near(got), near(early), near(window), near(before), hold)


def enter_kernel(half, width, rounds, side_ref, got_ref, early_ref, before_ref, first_ref, hold_ref, mine_ref, theirs_ref):
    is_first = side_ref[0] == 0
    for j in range(half):
        rows = slice(j * width, (j + 1) * width)
        if rounds == 0:
            before = jnp.zeros((width, width), F32)
        else:
            before = got_ref[rows, :].astype(F32)
            if rounds > 1:
                before = before + early_ref[rows, :].astype(F32)
                before = before * decay_row(before_ref, j, half, width) + before_ref[rows, :]
        after = before * decay_row(first_ref, j, half, width) + first_ref[rows, :]
        mine_ref[rows, :] = jnp.where(is_first, before, after).astype(BF16)
        theirs_ref[rows, :] = jnp.where(is_first, after, before).astype(BF16)


def enter(side, got, early, before, first, hold, half, width, rounds):
    shape = (half * width, width)
    got = first if got is None else got
    early = first if early is None else early
    before = first if before is None else before
    return pl.pallas_call(
        functools.partial(enter_kernel, half, width, rounds),
        in_specs=[SMEM, VMEM, VMEM, VMEM, VMEM, ANY],
        out_specs=[VMEM, VMEM],
        out_shape=[held(shape, BF16)] * 2,
        compiler_params=PARAMS,
        name="enter",
    )(side, near(got), near(early), near(before), near(first), hold)


def local_kernel(heads, width, cum_ref, q_ref, k_ref, v_ref, hold_ref, *refs):
    copies = []
    count = len(refs) // 3 if len(refs) > 2 else 0
    out_ref, decayed_ref = refs[count : count + 2]
    for i in range(count):
        target = refs[count + 2 + i]
        source = refs[i].at[:, pl.ds(0, target.shape[1])]
        copies.append(pltpu.make_async_copy(source, target, refs[2 * count + 2 + i]))
    for copy in copies:
        copy.start()
    rows = cum_ref.shape[1]
    tile = tile_of(rows, width)
    causal = lax.broadcasted_iota(jnp.int32, (tile, tile), 0) >= lax.broadcasted_iota(
        jnp.int32, (tile, tile), 1
    )
    for j, head in enumerate(heads):
        cols = slice(j * width, (j + 1) * width)
        cum = cum_ref[head : head + 1, :]
        for i in range(rows // tile):
            here = slice(i * tile, (i + 1) * tile)
            query = q_ref[here, cols]
            across = jnp.broadcast_to(cum[:, here], (tile, tile))
            down = across.T
            scores = lax.dot_general(
                query, k_ref[here, cols], (((1,), (1,)), ((), ())), preferred_element_type=F32
            )
            weight = jnp.exp(jnp.where(causal, down - across, -jnp.inf))
            out = jnp.dot(
                (scores * weight).astype(BF16), v_ref[here, cols], preferred_element_type=F32
            )
            if i == 0:
                decay = jnp.exp(down)
            else:
                edge = cum[:, i * tile - 1 : i * tile]
                since = jnp.exp(down - edge)
                earlier = slice(0, i * tile)
                scores = lax.dot_general(
                    query, k_ref[earlier, cols], (((1,), (1,)), ((), ())), preferred_element_type=F32
                )
                weight = jnp.exp(edge - cum[:, earlier])
                if tile != width:
                    since = since[:, :1]
                out = out + since * jnp.dot(
                    (scores * weight).astype(BF16), v_ref[earlier, cols], preferred_element_type=F32
                )
                decay = since * jnp.exp(edge)
            out_ref[here, cols] = out
            if tile != width:
                decay = decay[:, :1]
            decayed_ref[here, cols] = (query.astype(F32) * decay).astype(BF16)
    for copy in copies:
        copy.wait()


def local(cum, query, key, value, hold, extra, columns, part, parts, heads, width):
    rows = cum.shape[1]
    count = heads // parts
    cols = count * width
    block = pl.BlockSpec((rows, cols), lambda i: (0, part))
    return pl.pallas_call(
        functools.partial(local_kernel, tuple(range(part * count, (part + 1) * count)), width),
        grid=(1,),
        in_specs=[VMEM, block, block, block, ANY] + [ANY] * len(extra),
        out_specs=[VMEM, VMEM] + [VMEM] * len(extra),
        out_shape=[
            held((rows, cols), F32),
            held((rows, cols), BF16),
        ]
        + [held((a.shape[0], columns), a.dtype) for a in extra],
        scratch_shapes=[pltpu.SemaphoreType.DMA] * len(extra),
        compiler_params=PARAMS,
        name="local",
    )(near(cum), outside(query), outside(key), outside(value), hold, *map(outside, extra))


def norm_kernel(half, width, parts, chips, block, away, spot_ref, mine_ref, met_ref, gain_ref, *refs):
    inside_refs, query_refs, out_ref = refs[:parts], refs[parts : 2 * parts], refs[-1]
    per = 2 * half // parts
    is_first = spot_ref[2] == 0
    ones = jnp.full((width, width), 1.0 / width, F32).astype(BF16)
    for head in range(2 * half):
        span = slice((head % half) * width, (head % half + 1) * width)
        is_mine = is_first if head < half else jnp.logical_not(is_first)
        state = jnp.where(is_mine, mine_ref[span, :], met_ref[span, :])
        inside_ref, query_ref = inside_refs[head // per], query_refs[head // per]
        src = slice((head % per) * width, (head % per + 1) * width)
        cols = slice(head * width, (head + 1) * width)
        gain = gain_ref[:, cols]
        for i in range(chips):
            at = 2 * lax.rem(spot_ref[0] + i, chips)
            at = at + (1 - spot_ref[1] if away else spot_ref[1])
            rows = pl.ds(pl.multiple_of(at * block, block), block)
            attended = inside_ref[rows, src] + jnp.dot(
                query_ref[rows, src], state, preferred_element_type=F32
            )
            square = jnp.dot(
                (attended * attended).astype(BF16), ones, preferred_element_type=F32
            )
            out_ref[i * block : (i + 1) * block, cols] = (
                attended * lax.rsqrt(square + 1e-06) * gain
            ).astype(out_ref.dtype)


def norm(spot, mine, met, gain, insides, queries, half, width, chips, block, away):
    parts = len(insides)
    return pl.pallas_call(
        functools.partial(norm_kernel, half, width, parts, chips, block, away),
        in_specs=[SMEM] + [VMEM] * (3 + 2 * parts),
        out_specs=VMEM,
        out_shape=held((chips * block, 2 * half * width), BF16),
        compiler_params=PARAMS,
        name="norm_away" if away else "norm_home",
    )(spot, near(mine), near(met), gain, *map(near, insides), *map(near, queries))


def project_kernel(block, mine_ref, other_ref, near_ref, far_ref, hold_ref, own_ref, away_ref):
    total = jnp.dot(mine_ref[...], near_ref[...], preferred_element_type=F32) + jnp.dot(
        other_ref[...], far_ref[...], preferred_element_type=F32
    )
    own_ref[...] = total[:block]
    away_ref[...] = total[block:].astype(away_ref.dtype)


def project(mine, other, first_weight, second_weight, hold, block, first, count, tile):
    rows, depth = mine.shape
    start = first // tile
    at_hand = hold is None
    span = pl.BlockSpec((depth, tile), lambda i: (0, start + i))
    place = near if at_hand else outside
    return pl.pallas_call(
        functools.partial(project_kernel, block),
        grid=(count // tile,),
        in_specs=[VMEM, VMEM] + [VMEM if at_hand else span] * 2 + [ANY],
        out_specs=[
            pl.BlockSpec((block, tile), lambda i: (0, i)),
            pl.BlockSpec((rows - block, tile), lambda i: (0, i)),
        ],
        out_shape=[
            held((block, count), F32),
            held((rows - block, count), BF16),
        ],
        compiler_params=PARAMS,
        name="project",
    )(
        near(mine),
        near(other),
        place(first_weight),
        place(second_weight),
        mine if at_hand else hold,
    )


def shards(blocks, group, q_spikes, k_spikes, v_spikes, log_decay, norm_gain, out_weight, residual):
    rows, heads = log_decay.shape
    width = q_spikes.shape[1] // heads
    half = heads // 2
    chips = group // 2
    block = rows // group
    parts = min(4, heads)
    place = lax.axis_index("ctx")
    member = lax.axis_index("exp")
    side = (place & 1).astype(jnp.int32)
    swap = [(i, i ^ 1) for i in range(blocks)]
    cores = [(i, i ^ 1) for i in range(group)]

    logd = log_decay.T
    if heads % 8:
        logd = jnp.pad(logd, ((0, pad_rows(heads) - heads), (0, 0)))
    sent, _ = states((1 - side).reshape(1), logd, k_spikes, v_spikes, v_spikes, half, width, BF16)
    met = lax.ppermute(sent, "ctx", swap)
    side = side.reshape(1)
    kept, cum = states(side, logd, k_spikes, v_spikes, sent, half, width, F32)
    kept, weight = lax.optimization_barrier((kept, out_weight))
    far_weight = lax.ppermute(weight, "exp", cores)
    total = out_weight.shape[1]
    tile = tile_of(total, 512)

    inner, weights = [], []

    def more(hold, count):
        for _ in range(min(count, parts - len(inner))):
            part = len(inner)
            extra = [out_weight, far_weight] if part == parts - 1 else []
            done = local(
                cum, q_spikes, k_spikes, v_spikes, hold, extra, tile, part, parts, heads, width
            )
            inner.append(done[:2])
            weights.extend(done[2:])
            hold = done[0]
        return hold

    pay, window, first = pair(side, kept, met, half, width)
    before, got, early, rounds, step = None, None, None, 0, 1
    hold = pay
    while 2 * step < blocks:
        pairs = [(i, i + 2 * step) for i in range(step // 2 * 2, blocks - 2 * step)]
        got = lax.ppermute(pay, "ctx", pairs)
        last = 4 * step >= blocks
        ahead = None
        if not last:
            ahead = lax.ppermute(
                pay, "ctx", [(i, i + 4 * step) for i in range(min(2 * step, blocks - 4 * step))]
            )
        hold = more(pay, parts - len(inner) - 1 if last else 1)
        rounds += 1
        step *= 2
        if not last:
            pay, window, before = widen(got, early, window, before, hold, half, width)
            early = ahead
    mine, theirs = enter(side, got, early, before, first, hold, half, width, rounds)
    met = lax.ppermute(theirs, "ctx", swap)
    more(theirs, parts)

    spot = jnp.stack([member >> 1, member & 1, place & 1]).astype(jnp.int32)
    gain = norm_gain.reshape(1, heads * width)
    insides, queries = [a for a, _ in inner], [b for _, b in inner]
    args = (spot, mine, met, gain, insides, queries, half, width, chips, block)
    away = norm(*args, True)
    other = lax.ppermute(away, "exp", cores)
    home = norm(*args, False)

    sizes = [tile]
    while sum(sizes) < total:
        sizes.append(min(2 * tile, max(tile, total - sum(sizes) - tile)))
    out = jnp.zeros((block, total), BF16)
    at, hold = 0, None
    for size in sizes:
        own, pieces = project(home, other, *weights, hold, block, at, size, tile)
        weights, hold = (out_weight, far_weight), pieces
        summed = own + residual[:, at : at + size].astype(F32)
        for d in range(1, chips):
            piece = pieces[(d - 1) * block : d * block]
            perm = [(i, 2 * ((i // 2 + d) % chips) + i % 2) for i in range(group)]
            summed = summed + lax.ppermute(piece, "exp", perm).astype(F32)
        out = lax.dynamic_update_slice(out, summed.astype(BF16), (0, at))
        at += size
    return out


def solution(mesh):
    in_specs = (
        P("ctx", "exp"),
        P("ctx", "exp"),
        P("ctx", "exp"),
        P("ctx", "exp"),
        P("exp"),
        P("exp", None),
        P(("ctx", "exp"), None),
    )
    out_specs = P(("ctx", "exp"), None)
    return jax.shard_map(
        functools.partial(shards, mesh.shape["ctx"], mesh.shape["exp"]),
        mesh=mesh,
        in_specs=in_specs,
        out_specs=out_specs,
        check_vma=False,
    )
```

```python
import functools

import jax
import jax.numpy as jnp
from jax import lax
from jax.experimental import pallas as pl
from jax.experimental.pallas import tpu as pltpu
from jax.sharding import PartitionSpec as P


F32 = jnp.float32
BF16 = jnp.bfloat16
PARAMS = pltpu.CompilerParams(vmem_limit_bytes=16 << 20)
PACKED = pltpu.CompilerParams(vmem_limit_bytes=16 << 20)
VMEM = pl.BlockSpec(memory_space=pltpu.VMEM)
SMEM = pl.BlockSpec(memory_space=pltpu.SMEM)
ANY = pl.BlockSpec(memory_space=pl.ANY)


def held(shape, kind):
    return pltpu.VMEM(shape, kind)


def near(x):
    return pltpu.with_memory_space_constraint(x, pltpu.VMEM)


def outside(x):
    return pltpu.with_memory_space_constraint(x, pltpu.HBM)


def tile_of(size, want):
    while size % want:
        want //= 2
    return want


def pad_rows(count):
    return -(-count // 8) * 8


def running_sum(logd):
    heads, rows = logd.shape
    tile = tile_of(rows, 128)
    count = rows // tile
    tiles = jnp.concatenate([logd[:, i * tile : (i + 1) * tile] for i in range(count)], axis=0)
    one = tiles.astype(BF16).astype(F32)
    two = (tiles - one).astype(BF16).astype(F32)
    three = tiles - one - two
    parts = jnp.concatenate([one, two, three], axis=0).astype(BF16)
    upper = (
        lax.broadcasted_iota(jnp.int32, (tile, tile), 0)
        <= lax.broadcasted_iota(jnp.int32, (tile, tile), 1)
    ).astype(F32)
    sums = jnp.dot(parts, upper.astype(BF16), preferred_element_type=F32)
    size = count * heads
    sums = sums[:size] + sums[size : 2 * size] + sums[2 * size :]
    done, carry = [], None
    for i in range(count):
        part = sums[i * heads : (i + 1) * heads]
        if carry is not None:
            part = part + carry
        carry = part[:, tile - 1 : tile]
        done.append(part)
    return jnp.concatenate(done, axis=1)


def copies_of(source, target, sems, first=0):
    count = sems.shape[0]
    size = target.shape[0] // count
    return [
        pltpu.make_async_copy(
            source.at[pl.ds(i * size, size), pl.ds(first, target.shape[1])],
            target.at[pl.ds(i * size, size), :],
            sems.at[i],
        )
        for i in range(count)
    ]


def pay_shape(count, width, kind):
    return held((count * width + 2 * pad_rows(count), width), kind)


def part_of(place_ref, size, away):
    return (place_ref[0] & (size - 1)) ^ away


def put_states(part, count, width, key, value, weight_ref, cum_ref, pay_ref):
    rows = cum_ref.shape[1]
    turned = [key[:, j * width : (j + 1) * width].T for j in range(count)]
    decays = []
    for j in range(count):
        head = pl.ds(part * count + j, 1)
        keyed = turned[j] * weight_ref[head, :].astype(BF16)
        state = jnp.dot(keyed, value[:, j * width : (j + 1) * width], preferred_element_type=F32)
        pay_ref[j * width : (j + 1) * width, :] = state.astype(pay_ref.dtype)
        total = cum_ref[head, :][:, rows - 1 : rows]
        decays.append(jnp.broadcast_to(jnp.exp(total), (1, width)))
    put_decays(pay_ref, decays, count, width)


def put_sums(logd_ref, cum_ref, weight_ref):
    cum = running_sum(logd_ref[...])
    cum_ref[...] = cum
    weight_ref[...] = jnp.exp(cum[:, cum.shape[1] - 1 :] - cum)


def early_kernel(size, count, width, place_ref, logd_in, key_in, value_in, *refs):
    pay_refs = refs[: size - 1]
    key_ref, value_ref, logd_ref, cum_ref, weight_ref, logd_sem, sems = refs[size - 1 :]
    cols = count * width
    logd = pltpu.make_async_copy(logd_in, logd_ref, logd_sem)
    logd.start()
    copies = []
    for away in range(1, size):
        part = part_of(place_ref, size, away)
        first = pl.multiple_of(part * cols, cols)
        here = pl.ds((away - 1) * cols, cols)
        copies.append(
            copies_of(key_in, key_ref.at[:, here], sems.at[0, away - 1], first)
            + copies_of(value_in, value_ref.at[:, here], sems.at[1, away - 1], first)
        )
        for copy in copies[-1]:
            copy.start()
    logd.wait()
    put_sums(logd_ref, cum_ref, weight_ref)
    for away in range(1, size):
        for copy in copies[away - 1]:
            copy.wait()
        here = slice((away - 1) * cols, away * cols)
        put_states(
            part_of(place_ref, size, away), count, width, key_ref[:, here], value_ref[:, here],
            weight_ref, cum_ref, pay_refs[away - 1],
        )


def early_states(place, logd, key, value, size, count, width):
    heads, rows = logd.shape
    cols = (size - 1) * count * width
    *pays, key, value = pl.pallas_call(
        functools.partial(early_kernel, size, count, width),
        in_specs=[SMEM] + [ANY] * 3,
        out_specs=[VMEM] * (size + 1),
        out_shape=[pay_shape(count, width, BF16)] * (size - 1) + [held((rows, cols), BF16)] * 2,
        scratch_shapes=[pltpu.VMEM((heads, rows), F32)] * 3
        + [pltpu.SemaphoreType.DMA, pltpu.SemaphoreType.DMA((2, size - 1, 4))],
        compiler_params=PACKED,
        name="early_states",
    )(place, outside(logd), outside(key), outside(value))
    return pays, key, value


def load_kernel(size, count, width, place_ref, logd_in, key_in, value_in, query_in, hold_ref, *refs):
    pay_ref, key_ref, value_ref, query_ref, cum_ref, logd_ref, weight_ref, logd_sem, sems = refs
    cols = count * width
    logd = pltpu.make_async_copy(logd_in, logd_ref, logd_sem)
    logd.start()
    first = pl.multiple_of(part_of(place_ref, size, 0) * cols, cols)
    copies = copies_of(key_in, key_ref, sems.at[0], first)
    copies += copies_of(value_in, value_ref, sems.at[1], first)
    last = []
    for away in range(size):
        start = pl.multiple_of(part_of(place_ref, size, away) * cols, cols)
        target = query_ref.at[:, pl.ds(away * cols, cols)]
        last += copies_of(query_in, target, sems.at[2 + away], start)
    for copy in copies + last:
        copy.start()
    logd.wait()
    put_sums(logd_ref, cum_ref, weight_ref)
    for copy in copies:
        copy.wait()
    put_states(
        part_of(place_ref, size, 0), count, width, key_ref[...], value_ref[...], weight_ref, cum_ref, pay_ref
    )
    for copy in last:
        copy.wait()


def load(place, logd, key, value, query, hold, size, count, width):
    heads, rows = logd.shape
    return pl.pallas_call(
        functools.partial(load_kernel, size, count, width),
        in_specs=[SMEM] + [ANY] * 5,
        out_specs=[VMEM] * 5,
        out_shape=[
            pay_shape(count, width, F32),
            held((rows, count * width), BF16),
            held((rows, count * width), BF16),
            held(query.shape, BF16),
            held((heads, rows), F32),
        ],
        scratch_shapes=[pltpu.VMEM((heads, rows), F32)] * 2
        + [pltpu.SemaphoreType.DMA, pltpu.SemaphoreType.DMA((2 + size, 4))],
        compiler_params=PACKED,
        name="load",
    )(place, outside(logd), outside(key), outside(value), outside(query), hold)


def decay_row(pay, j, count, width):
    at = count * width + j
    pad = pad_rows(count)
    return pay[at : at + 1, :].astype(F32) + pay[at + pad : at + pad + 1, :].astype(F32)


def put_decays(ref, rows, count, width):
    pad = pad_rows(count)
    blank = [jnp.zeros((1, width), F32)] * (pad - count)
    if ref.dtype == BF16:
        highs = [row.astype(BF16).astype(F32) for row in rows]
        lows = [row - high for row, high in zip(rows, highs)]
    else:
        highs, lows = rows, [jnp.zeros_like(row) for row in rows]
    tail = jnp.concatenate(highs + blank + lows + blank, axis=0)
    ref[count * width :, :] = tail.astype(ref.dtype)


def picked(values, index):
    found = values[0]
    for i in range(1, len(values)):
        found = jnp.where(index == i, values[i], found)
    return found


def gather_kernel(size, count, width, place_ref, *refs):
    in_refs, pay_ref, window_ref, past_refs = refs[:size], refs[size], refs[size + 1], refs[size + 2 :]
    decays = [[] for _ in range(size)]
    for j in range(count):
        rows = slice(j * width, (j + 1) * width)
        found = [ref[rows, :].astype(F32) for ref in in_refs]
        found_decays = [decay_row(ref, j, count, width) for ref in in_refs]
        total, total_decay = None, None
        for b in range(size):
            index = part_of(place_ref, size, b)
            state, decay = picked(found, index), picked(found_decays, index)
            if b:
                past_refs[b - 1][rows, :] = total
                decays[b - 1].append(total_decay)
                total, total_decay = total * decay + state, total_decay * decay
            else:
                total, total_decay = state, decay
        window_ref[rows, :] = total
        pay_ref[rows, :] = total.astype(pay_ref.dtype)
        decays[-1].append(total_decay)
    for ref, rows in zip(past_refs, decays):
        put_decays(ref, rows, count, width)
    put_decays(window_ref, decays[-1], count, width)
    put_decays(pay_ref, decays[-1], count, width)


def gather(place, own, met, size, count, width):
    shape = own.shape
    pay, window, *past = pl.pallas_call(
        functools.partial(gather_kernel, size, count, width),
        in_specs=[SMEM] + [VMEM] * size,
        out_specs=[VMEM] * (size + 1),
        out_shape=[held(shape, BF16)] + [held(shape, F32)] * size,
        compiler_params=PARAMS,
        name="gather",
    )(place, near(own), *map(near, met))
    return pay, window, past


def widen_kernel(count, width, bit, opening, keep, place_ref, got_ref, window_ref, before_ref, pay_ref, past_ref, *refs):
    is_later = (place_ref[0] & bit) != 0
    decays, pasts = [], []
    for j in range(count):
        rows = slice(j * width, (j + 1) * width)
        got, window = got_ref[rows, :].astype(F32), window_ref[rows, :]
        got_decay = decay_row(got_ref, j, count, width)
        window_decay = decay_row(window_ref, j, count, width)
        wide = jnp.where(is_later, got, window) * jnp.where(
            is_later, window_decay, got_decay
        ) + jnp.where(is_later, window, got)
        pay_ref[rows, :] = wide.astype(pay_ref.dtype)
        if keep:
            refs[0][rows, :] = wide
        decays.append(got_decay * window_decay)
        if opening:
            past_ref[rows, :] = jnp.where(is_later, got, jnp.zeros_like(got))
            pasts.append(jnp.where(is_later, got_decay, jnp.ones_like(got_decay)))
        else:
            before = before_ref[rows, :]
            before_decay = decay_row(before_ref, j, count, width)
            past_ref[rows, :] = jnp.where(is_later, got * before_decay + before, before)
            pasts.append(jnp.where(is_later, got_decay * before_decay, before_decay))
    put_decays(pay_ref, decays, count, width)
    if keep:
        put_decays(refs[0], decays, count, width)
    put_decays(past_ref, pasts, count, width)


def widen(place, got, window, before, count, width, bit, keep):
    shape = got.shape
    opening = before is None
    before = window if before is None else before
    done = pl.pallas_call(
        functools.partial(widen_kernel, count, width, bit, opening, keep),
        in_specs=[SMEM, VMEM, VMEM, VMEM],
        out_specs=[VMEM] * (2 + keep),
        out_shape=[held(shape, BF16), held(shape, F32)] + [held(shape, F32)] * keep,
        compiler_params=PARAMS,
        name="widen",
    )(place, near(got), near(window), near(before))
    return done if keep else (*done, None)


def enter_kernel(size, count, width, bit, opening, place_ref, got_ref, before_ref, *refs):
    past_refs, out_refs = refs[: size - 1], refs[size - 1 :]
    is_later = (place_ref[0] & bit) != 0
    for j in range(count):
        rows = slice(j * width, (j + 1) * width)
        before = jnp.zeros((width, width), F32)
        if bit:
            got = got_ref[rows, :].astype(F32)
            if not opening:
                before = before_ref[rows, :]
                got = got * decay_row(before_ref, j, count, width) + before
            before = jnp.where(is_later, got, before)
        entering = [before] + [
            before * decay_row(ref, j, count, width) + ref[rows, :] for ref in past_refs
        ]
        for away in range(size):
            index = part_of(place_ref, size, away)
            out_refs[away][rows, :] = picked(entering, index).astype(BF16)


def enter(place, got, before, past, size, count, width, bit):
    opening = before is None
    got = past[0] if got is None else got
    before = past[0] if opening else before
    return pl.pallas_call(
        functools.partial(enter_kernel, size, count, width, bit, opening),
        in_specs=[SMEM] + [VMEM] * (size + 1),
        out_specs=[VMEM] * size,
        out_shape=[held((count * width, width), BF16)] * size,
        compiler_params=PARAMS,
        name="enter",
    )(place, near(got), near(before), *map(near, past))


def local_kernel(size, count, width, away, place_ref, cum_ref, q_ref, k_ref, v_ref, out_ref, decayed_ref):
    from_q, from_kv = away * count, max(away - 1, 0) * count
    sums = [
        cum_ref[pl.ds(part_of(place_ref, size, away) * count + j, 1), :] for j in range(count)
    ]
    rows = cum_ref.shape[1]
    tile = tile_of(rows, 2 * width)
    causal = lax.broadcasted_iota(jnp.int32, (tile, tile), 0) >= lax.broadcasted_iota(
        jnp.int32, (tile, tile), 1
    )

    def downward(row):
        turned = jnp.broadcast_to(row, (width, tile)).T
        return jnp.concatenate([turned] * (tile // width), axis=1)

    def columns(start, j):
        return slice((start + j) * width, (start + j + 1) * width)

    def scores(j, i):
        return lax.dot_general(
            q_ref[i * tile : (i + 1) * tile, columns(from_q, j)],
            k_ref[: (i + 1) * tile, columns(from_kv, j)],
            (((1,), (1,)), ((), ())),
            preferred_element_type=F32,
        )

    def weighted(j, i, found):
        cum = sums[j]
        here = slice(i * tile, (i + 1) * tile)
        across = cum[:, here]
        down = downward(across)
        weight = jnp.exp(jnp.where(causal, down - across, -jnp.inf))
        near_part = (found[:, i * tile :] * weight).astype(BF16)
        if i == 0:
            return near_part, None, None, jnp.exp(down)
        edge = cum[:, i * tile - 1 : i * tile]
        since = jnp.exp(down - edge)
        far_part = (found[:, : i * tile] * jnp.exp(edge - cum[:, : i * tile])).astype(BF16)
        return near_part, far_part, since, since * jnp.exp(edge)

    def finish(j, i, near_part, far_part, since, decay):
        cols = slice(j * width, (j + 1) * width)
        from_cols = columns(from_kv, j)
        here = slice(i * tile, (i + 1) * tile)
        out = jnp.dot(near_part, v_ref[here, from_cols], preferred_element_type=F32)
        if far_part is not None:
            out = out + since[:, :width] * jnp.dot(
                far_part, v_ref[: i * tile, from_cols], preferred_element_type=F32
            )
        out_ref[here, cols] = out
        decayed_ref[here, cols] = (
            q_ref[here, columns(from_q, j)].astype(F32) * decay[:, :width]
        ).astype(BF16)

    units = [(j, i) for i in range(rows // tile) for j in range(count)]
    found, held_parts = {}, {}
    for step in range(len(units) + 3):
        if step < len(units):
            found[step] = scores(*units[step])
        if 0 <= step - 2 < len(units):
            held_parts[step - 2] = weighted(*units[step - 2], found.pop(step - 2))
        if 0 <= step - 3:
            finish(*units[step - 3], *held_parts.pop(step - 3))


def local(place, cum, query, key, value, size, count, width, away):
    rows = cum.shape[1]
    cols = count * width
    return pl.pallas_call(
        functools.partial(local_kernel, size, count, width, away),
        in_specs=[SMEM] + [VMEM] * 4,
        out_specs=[VMEM, VMEM],
        out_shape=[held((rows, cols), F32), held((rows, cols), BF16)],
        compiler_params=PARAMS,
        name="local",
    )(place, near(cum), near(query), near(key), near(value))


def norm_kernel(size, count, width, chips, block, away, group, place_ref, chip_ref, core_ref, gain_ref, *refs):
    members = len(group)
    inside_refs, query_refs = refs[:members], refs[members : 2 * members]
    state_refs, out_ref = refs[2 * members : -1], refs[-1]
    ones = jnp.full((width, width), 1.0 / width, F32).astype(BF16)
    units = [(at, j) for at in range(members) for j in range(count)]

    def rows_of(ref, j):
        src = slice(j * width, (j + 1) * width)
        found = []
        for i in range(chips):
            spot = 2 * lax.rem(chip_ref[0] + i, chips)
            spot = spot + (1 - core_ref[0] if away else core_ref[0])
            found.append(ref[pl.ds(pl.multiple_of(spot * block, block), block), src])
        return jnp.concatenate(found, axis=0)

    def carry(at, j):
        state = state_refs[at][j * width : (j + 1) * width, :]
        return jnp.dot(rows_of(query_refs[at], j), state, preferred_element_type=F32)

    def square(at, j, carried):
        attended = rows_of(inside_refs[at], j) + carried
        return attended, jnp.dot(
            (attended * attended).astype(BF16), ones, preferred_element_type=F32
        )

    def finish_head(at, j, attended, mean):
        gain = gain_ref[pl.ds(part_of(place_ref, size, group[at]) * count + j, 1), :]
        col = (at * count + j) * width
        out_ref[:, col : col + width] = (
            attended * lax.rsqrt(mean + 1e-06) * gain
        ).astype(out_ref.dtype)

    first, second = {}, {}
    for step in range(len(units) + 2):
        if step < len(units):
            first[step] = carry(*units[step])
        if 0 <= step - 1 < len(units):
            second[step - 1] = square(*units[step - 1], first.pop(step - 1))
        if 0 <= step - 2:
            finish_head(*units[step - 2], *second.pop(step - 2))


def norm(group, scalars, gain, insides, queries, entering, size, count, width, chips, block, away):
    cols = len(group) * count * width
    parts = [a[i] for a in (insides, queries, entering) for i in group]
    return pl.pallas_call(
        functools.partial(norm_kernel, size, count, width, chips, block, away, group),
        in_specs=[SMEM] * 3 + [VMEM] * (1 + len(parts)),
        out_specs=VMEM,
        out_shape=held((chips * block, cols), BF16),
        compiler_params=PARAMS,
        name="norm_away" if away else "norm_home",
    )(*scalars, gain, *map(near, parts))


def project_kernel(block, first, tile, size, place_ref, *refs):
    own_ref, away_ref = refs[-2:]
    sides = [(refs[0], refs[1], refs[4]), (refs[2], refs[3], refs[5])]
    cols = refs[1].shape[1]
    for i in range(own_ref.shape[1] // tile):
        here = slice(i * tile, (i + 1) * tile)
        span = slice(first + i * tile, first + (i + 1) * tile)
        total = None
        for one_ref, two_ref, weight_ref in sides:
            for away in range(size):
                last = away == size - 1
                normed = two_ref[...] if last else one_ref[:, away * cols : (away + 1) * cols]
                start = pl.multiple_of(part_of(place_ref, size, away) * cols, cols)
                part = jnp.dot(
                    normed, weight_ref[pl.ds(start, cols), span], preferred_element_type=F32
                )
                total = part if total is None else total + part
        own_ref[:, here] = total[:block]
        away_ref[:, here] = total[block:].astype(away_ref.dtype)


def project(place, home, other, first_weight, second_weight, hold, block, first, count, tile, size):
    rows = home[0].shape[0]
    tile = tile_of(count, tile)
    return pl.pallas_call(
        functools.partial(project_kernel, block, first, tile, size),
        in_specs=[SMEM] + [VMEM] * 6 + [ANY],
        out_specs=[VMEM, VMEM],
        out_shape=[held((block, count), F32), held((rows - block, count), BF16)],
        compiler_params=PARAMS,
        name="project",
    )(place, *map(near, [*home, *other, first_weight, second_weight]), hold)


def finish_kernel(first, pieces, own_ref, residual_ref, *refs):
    part_refs, (out_ref, total_ref, sems) = refs[:pieces], refs[-3:]
    count = own_ref.shape[1]
    total = own_ref[...] + residual_ref[:, first : first + count].astype(F32)
    for ref in part_refs:
        total = total + ref[...].astype(F32)
    total_ref[...] = total.astype(BF16)
    rows = total_ref.shape[0] // sems.shape[0]
    copies = []
    for i in range(sems.shape[0]):
        here = pl.ds(i * rows, rows)
        copies.append(
            pltpu.make_async_copy(
                total_ref.at[here, :], out_ref.at[here, pl.ds(first, count)], sems.at[i]
            )
        )
    for copy in copies:
        copy.start()
    for copy in copies:
        copy.wait()


def finish(out, own, residual, parts, first):
    block, total = residual.shape
    earlier = [] if out is None else [outside(out)]
    return pl.pallas_call(
        functools.partial(finish_kernel, first, len(parts)),
        in_specs=[VMEM] * (2 + len(parts)) + [ANY] * len(earlier),
        out_specs=ANY,
        out_shape=pltpu.HBM((block, total), BF16),
        scratch_shapes=[
            pltpu.VMEM((block, own.shape[1]), BF16),
            pltpu.SemaphoreType.DMA((tile_of(block // 16, 4),)),
        ],
        input_output_aliases={2 + len(parts): 0} if earlier else {},
        compiler_params=PARAMS,
        name="finish",
    )(near(own), near(residual), *map(near, parts), *earlier)


def shards(blocks, group, q_spikes, k_spikes, v_spikes, log_decay, norm_gain, out_weight, residual):
    rows, heads = log_decay.shape
    width = q_spikes.shape[1] // heads
    size = 4 if heads % 4 == 0 and blocks % 4 == 0 else 2
    count = heads // size
    chips = group // 2
    block = rows // group
    place = lax.axis_index("ctx").astype(jnp.int32)
    member = lax.axis_index("exp").astype(jnp.int32)
    place, chip, core = lax.optimization_barrier(
        tuple(a.reshape(1) for a in (place, member >> 1, member & 1))
    )
    cores = [(i, i ^ 1) for i in range(group)]

    def swap(x, bit):
        return lax.ppermute(x, "ctx", [(i, i ^ bit) for i in range(blocks)])

    logd = log_decay.T
    if heads % 8:
        logd = jnp.pad(logd, ((0, pad_rows(heads) - heads), (0, 0)))
    sent, keys, values = early_states(place, logd, k_spikes, v_spikes, size, count, width)
    met = [swap(a, i + 1) for i, a in enumerate(sent)]
    kept, key, value, query, cum = load(
        place, logd, k_spikes, v_spikes, q_spikes, sent[0], size, count, width
    )
    kept, weight = lax.optimization_barrier((kept, out_weight))
    far_weight = lax.ppermute(outside(weight), "exp", cores)
    total = out_weight.shape[1]
    tile = tile_of(total, 512)

    pay, window, past = gather(place, kept, met, size, count, width)
    _, own_weight = lax.optimization_barrier((pay, out_weight))
    before, got, level, bit = None, None, 0, size
    while bit < blocks:
        got = swap(pay, bit)
        if 2 * bit < blocks:
            pay, before, window = widen(
                place, got, window, before, count, width, bit, int(4 * bit < blocks)
            )
        bit, level = 2 * bit, level + 1
    own, *theirs = enter(place, got, before, past, size, count, width, bit // 2 if level else 0)
    entering = [own] + [swap(a, i + 1) for i, a in enumerate(theirs)]

    insides, queries = [], []
    for away in range(size):
        inside, decayed = local(
            place, cum, query, keys if away else key, values if away else value,
            size, count, width, away,
        )
        insides.append(inside)
        queries.append(decayed)

    gain = norm_gain.reshape(heads, width)
    home, other = [], []
    for which in (range(size - 1), range(size - 1, size)):
        args = (
            tuple(which), (place, chip, core), gain, insides, queries, entering,
            size, count, width, chips, block,
        )
        away = norm(*args, True)
        other.append(lax.ppermute(away, "exp", cores))
        home.append(norm(*args, False))

    sizes = [tile, tile]
    while total - sum(sizes) > 2 * tile:
        sizes.append(2 * tile)
    rest = total - sum(sizes)
    sizes += [rest - tile // 2, tile // 2] if rest > tile // 2 else [rest]
    out, at, hold = None, 0, home[1]
    sums = []
    for span in sizes:
        own, pieces = project(place, home, other, own_weight, far_weight, hold, block, at, span, tile, size)
        hold = pieces
        got = []
        for d in range(1, chips):
            piece = pieces[(d - 1) * block : d * block]
            perm = [(i, 2 * ((i // 2 + d) % chips) + i % 2) for i in range(group)]
            got.append(lax.ppermute(piece, "exp", perm))
        sums.append((own, got, at))
        at += span
    for own, got, at in sums:
        out = finish(out, own, residual, got, at)
    return out


def solution(mesh):
    in_specs = (
        P("ctx", "exp"),
        P("ctx", "exp"),
        P("ctx", "exp"),
        P("ctx", "exp"),
        P("exp"),
        P("exp", None),
        P(("ctx", "exp"), None),
    )
    out_specs = P(("ctx", "exp"), None)

    def body(*args):
        return shards(mesh.shape["ctx"], mesh.shape["exp"], *args)

    return jax.shard_map(
        body, mesh=mesh, in_specs=in_specs, out_specs=out_specs, check_vma=False
    )
```

```python
import functools

import jax
import jax.numpy as jnp
from jax import lax
from jax.experimental import pallas as pl
from jax.experimental.pallas import tpu as pltpu
from jax.sharding import PartitionSpec as P


F32 = jnp.float32
BF16 = jnp.bfloat16
PARAMS = pltpu.CompilerParams(vmem_limit_bytes=16 << 20)
PACKED = pltpu.CompilerParams(vmem_limit_bytes=16 << 20)
VMEM = pl.BlockSpec(memory_space=pltpu.VMEM)
SMEM = pl.BlockSpec(memory_space=pltpu.SMEM)
ANY = pl.BlockSpec(memory_space=pl.ANY)


def held(shape, kind):
    return pltpu.VMEM(shape, kind)


def near(x):
    return pltpu.with_memory_space_constraint(x, pltpu.VMEM)


def outside(x):
    return pltpu.with_memory_space_constraint(x, pltpu.HBM)


def tile_of(size, want):
    while size % want:
        want //= 2
    return want


def pad_rows(count):
    return -(-count // 8) * 8


def running_sum(logd):
    heads, rows = logd.shape
    tile = tile_of(rows, 128)
    count = rows // tile
    tiles = jnp.concatenate([logd[:, i * tile : (i + 1) * tile] for i in range(count)], axis=0)
    one = tiles.astype(BF16).astype(F32)
    two = (tiles - one).astype(BF16).astype(F32)
    three = tiles - one - two
    parts = jnp.concatenate([one, two, three], axis=0).astype(BF16)
    upper = (
        lax.broadcasted_iota(jnp.int32, (tile, tile), 0)
        <= lax.broadcasted_iota(jnp.int32, (tile, tile), 1)
    ).astype(F32)
    sums = jnp.dot(parts, upper.astype(BF16), preferred_element_type=F32)
    size = count * heads
    sums = sums[:size] + sums[size : 2 * size] + sums[2 * size :]
    done, carry = [], None
    for i in range(count):
        part = sums[i * heads : (i + 1) * heads]
        if carry is not None:
            part = part + carry
        carry = part[:, tile - 1 : tile]
        done.append(part)
    return jnp.concatenate(done, axis=1)


def copies_of(source, target, sems, first=0):
    count = sems.shape[0]
    size = target.shape[0] // count
    return [
        pltpu.make_async_copy(
            source.at[pl.ds(i * size, size), pl.ds(first, target.shape[1])],
            target.at[pl.ds(i * size, size), :],
            sems.at[i],
        )
        for i in range(count)
    ]


def pay_shape(count, width, kind):
    return held((count * width + 2 * pad_rows(count), width), kind)


def part_of(place_ref, size, away):
    return (place_ref[0] & (size - 1)) ^ away


def put_states(part, count, width, key, value, weight_ref, cum_ref, pay_ref):
    rows = cum_ref.shape[1]
    turned = [key[:, j * width : (j + 1) * width].T for j in range(count)]
    decays = []
    for j in range(count):
        head = pl.ds(part * count + j, 1)
        keyed = turned[j] * weight_ref[head, :].astype(BF16)
        state = jnp.dot(keyed, value[:, j * width : (j + 1) * width], preferred_element_type=F32)
        pay_ref[j * width : (j + 1) * width, :] = state.astype(pay_ref.dtype)
        total = cum_ref[head, :][:, rows - 1 : rows]
        decays.append(jnp.broadcast_to(jnp.exp(total), (1, width)))
    put_decays(pay_ref, decays, count, width)


def put_sums(logd_ref, cum_ref, weight_ref):
    cum = running_sum(logd_ref[...])
    cum_ref[...] = cum
    weight_ref[...] = jnp.exp(cum[:, cum.shape[1] - 1 :] - cum)


def part_columns(place_ref, size, away, cols):
    return pl.ds(pl.multiple_of(part_of(place_ref, size, away) * cols, cols), cols)


def early_kernel(size, count, width, place_ref, logd_in, key_in, value_in, *refs):
    pay_refs = refs[: size - 1]
    key_ref, value_ref, logd_ref, cum_ref, weight_ref, logd_sem, sems = refs[size - 1 :]
    copies = [pltpu.make_async_copy(logd_in, logd_ref, logd_sem)]
    copies += copies_of(key_in, key_ref, sems.at[0]) + copies_of(value_in, value_ref, sems.at[1])
    for copy in copies:
        copy.start()
    copies[0].wait()
    put_sums(logd_ref, cum_ref, weight_ref)
    for copy in copies[1:]:
        copy.wait()
    for away in range(1, size):
        here = part_columns(place_ref, size, away, count * width)
        put_states(
            part_of(place_ref, size, away), count, width, key_ref[:, here], value_ref[:, here],
            weight_ref, cum_ref, pay_refs[away - 1],
        )


def early_states(place, logd, key, value, size, count, width):
    heads, rows = logd.shape
    *pays, key, value = pl.pallas_call(
        functools.partial(early_kernel, size, count, width),
        in_specs=[SMEM] + [ANY] * 3,
        out_specs=[VMEM] * (size + 1),
        out_shape=[pay_shape(count, width, BF16)] * (size - 1) + [held(key.shape, BF16)] * 2,
        scratch_shapes=[pltpu.VMEM((heads, rows), F32)] * 3
        + [pltpu.SemaphoreType.DMA, pltpu.SemaphoreType.DMA((2, 2))],
        compiler_params=PACKED,
        name="early_states",
    )(place, outside(logd), outside(key), outside(value))
    return pays, key, value


def load_kernel(size, count, width, place_ref, logd_in, query_in, key_ref, value_ref, hold_ref, *refs):
    pay_ref, query_ref, cum_ref, logd_ref, weight_ref, logd_sem, sems = refs
    logd = pltpu.make_async_copy(logd_in, logd_ref, logd_sem)
    logd.start()
    copies = copies_of(query_in, query_ref, sems)
    for copy in copies:
        copy.start()
    logd.wait()
    put_sums(logd_ref, cum_ref, weight_ref)
    here = part_columns(place_ref, size, 0, count * width)
    put_states(
        part_of(place_ref, size, 0), count, width, key_ref[:, here], value_ref[:, here],
        weight_ref, cum_ref, pay_ref,
    )
    for copy in copies:
        copy.wait()


def load(place, logd, key, value, query, hold, size, count, width):
    heads, rows = logd.shape
    return pl.pallas_call(
        functools.partial(load_kernel, size, count, width),
        in_specs=[SMEM, ANY, ANY, VMEM, VMEM, ANY],
        out_specs=[VMEM] * 3,
        out_shape=[
            pay_shape(count, width, F32),
            held(query.shape, BF16),
            held((heads, rows), F32),
        ],
        scratch_shapes=[pltpu.VMEM((heads, rows), F32)] * 2
        + [pltpu.SemaphoreType.DMA, pltpu.SemaphoreType.DMA((2,))],
        compiler_params=PACKED,
        name="load",
    )(place, outside(logd), outside(query), near(key), near(value), hold)


def decay_row(pay, j, count, width):
    at = count * width + j
    pad = pad_rows(count)
    return pay[at : at + 1, :].astype(F32) + pay[at + pad : at + pad + 1, :].astype(F32)


def put_decays(ref, rows, count, width):
    pad = pad_rows(count)
    blank = [jnp.zeros((1, width), F32)] * (pad - count)
    if ref.dtype == BF16:
        highs = [row.astype(BF16).astype(F32) for row in rows]
        lows = [row - high for row, high in zip(rows, highs)]
    else:
        highs, lows = rows, [jnp.zeros_like(row) for row in rows]
    tail = jnp.concatenate(highs + blank + lows + blank, axis=0)
    ref[count * width :, :] = tail.astype(ref.dtype)


def picked(values, index):
    found = values[0]
    for i in range(1, len(values)):
        found = jnp.where(index == i, values[i], found)
    return found


def gather_kernel(size, count, width, place_ref, *refs):
    in_refs, pay_ref, past_refs = refs[:size], refs[size], refs[size + 1 : 2 * size]
    window_refs = refs[2 * size :]
    decays = [[] for _ in range(size)]
    for j in range(count):
        rows = slice(j * width, (j + 1) * width)
        found = [ref[rows, :].astype(F32) for ref in in_refs]
        found_decays = [decay_row(ref, j, count, width) for ref in in_refs]
        total, total_decay = None, None
        for b in range(size):
            index = part_of(place_ref, size, b)
            state, decay = picked(found, index), picked(found_decays, index)
            if b:
                past_refs[b - 1][rows, :] = total
                decays[b - 1].append(total_decay)
                total, total_decay = total * decay + state, total_decay * decay
            else:
                total, total_decay = state, decay
        for ref in (pay_ref, *window_refs):
            ref[rows, :] = total.astype(ref.dtype)
        decays[-1].append(total_decay)
    for ref, rows in zip(past_refs, decays):
        put_decays(ref, rows, count, width)
    for ref in (pay_ref, *window_refs):
        put_decays(ref, decays[-1], count, width)


def gather(place, own, met, size, count, width, keep):
    shape = own.shape
    pay, *past = pl.pallas_call(
        functools.partial(gather_kernel, size, count, width),
        in_specs=[SMEM] + [VMEM] * size,
        out_specs=[VMEM] * (size + keep),
        out_shape=[held(shape, BF16)] + [held(shape, F32)] * (size - 1 + keep),
        compiler_params=PARAMS,
        name="gather",
    )(place, near(own), *map(near, met))
    return pay, past[: size - 1], past[-1]


def widen_kernel(count, width, bit, opening, keep, place_ref, got_ref, window_ref, before_ref, pay_ref, past_ref, *refs):
    is_later = (place_ref[0] & bit) != 0
    decays, pasts = [], []
    for j in range(count):
        rows = slice(j * width, (j + 1) * width)
        got, window = got_ref[rows, :].astype(F32), window_ref[rows, :]
        got_decay = decay_row(got_ref, j, count, width)
        window_decay = decay_row(window_ref, j, count, width)
        wide = jnp.where(is_later, got, window) * jnp.where(
            is_later, window_decay, got_decay
        ) + jnp.where(is_later, window, got)
        pay_ref[rows, :] = wide.astype(pay_ref.dtype)
        if keep:
            refs[0][rows, :] = wide
        decays.append(got_decay * window_decay)
        if opening:
            past_ref[rows, :] = jnp.where(is_later, got, jnp.zeros_like(got))
            pasts.append(jnp.where(is_later, got_decay, jnp.ones_like(got_decay)))
        else:
            before = before_ref[rows, :]
            before_decay = decay_row(before_ref, j, count, width)
            past_ref[rows, :] = jnp.where(is_later, got * before_decay + before, before)
            pasts.append(jnp.where(is_later, got_decay * before_decay, before_decay))
    put_decays(pay_ref, decays, count, width)
    if keep:
        put_decays(refs[0], decays, count, width)
    put_decays(past_ref, pasts, count, width)


def widen(place, got, window, before, count, width, bit, keep):
    shape = got.shape
    opening = before is None
    before = window if before is None else before
    done = pl.pallas_call(
        functools.partial(widen_kernel, count, width, bit, opening, keep),
        in_specs=[SMEM, VMEM, VMEM, VMEM],
        out_specs=[VMEM] * (2 + keep),
        out_shape=[held(shape, BF16), held(shape, F32)] + [held(shape, F32)] * keep,
        compiler_params=PARAMS,
        name="widen",
    )(place, near(got), near(window), near(before))
    return done if keep else (*done, None)


def enter_kernel(size, count, width, bit, opening, place_ref, got_ref, before_ref, *refs):
    past_refs, out_refs = refs[: size - 1], refs[size - 1 :]
    is_later = (place_ref[0] & bit) != 0
    for j in range(count):
        rows = slice(j * width, (j + 1) * width)
        before = jnp.zeros((width, width), F32)
        if bit:
            got = got_ref[rows, :].astype(F32)
            if not opening:
                before = before_ref[rows, :]
                got = got * decay_row(before_ref, j, count, width) + before
            before = jnp.where(is_later, got, before)
        entering = [before] + [
            before * decay_row(ref, j, count, width) + ref[rows, :] for ref in past_refs
        ]
        for away in range(size):
            index = part_of(place_ref, size, away)
            out_refs[away][rows, :] = picked(entering, index).astype(BF16)


def enter(place, got, before, past, size, count, width, bit):
    opening = before is None
    got = past[0] if got is None else got
    before = past[0] if opening else before
    return pl.pallas_call(
        functools.partial(enter_kernel, size, count, width, bit, opening),
        in_specs=[SMEM] + [VMEM] * (size + 1),
        out_specs=[VMEM] * size,
        out_shape=[held((count * width, width), BF16)] * size,
        compiler_params=PARAMS,
        name="enter",
    )(place, near(got), near(before), *map(near, past))


def local_kernel(size, count, width, away, place_ref, cum_ref, q_ref, k_ref, v_ref, out_ref, decayed_ref):
    part = part_of(place_ref, size, away)
    sums = [cum_ref[pl.ds(part * count + j, 1), :] for j in range(count)]
    rows = cum_ref.shape[1]
    tile = tile_of(rows, 2 * width)
    causal = lax.broadcasted_iota(jnp.int32, (tile, tile), 0) >= lax.broadcasted_iota(
        jnp.int32, (tile, tile), 1
    )

    def downward(row):
        turned = jnp.broadcast_to(row, (width, tile)).T
        return jnp.concatenate([turned] * (tile // width), axis=1)

    def columns(j):
        return pl.ds(pl.multiple_of((part * count + j) * width, width), width)

    def scores(j, i):
        return lax.dot_general(
            q_ref[i * tile : (i + 1) * tile, columns(j)],
            k_ref[: (i + 1) * tile, columns(j)],
            (((1,), (1,)), ((), ())),
            preferred_element_type=F32,
        )

    def weighted(j, i, found):
        cum = sums[j]
        here = slice(i * tile, (i + 1) * tile)
        across = cum[:, here]
        down = downward(across)
        weight = jnp.exp(jnp.where(causal, down - across, -jnp.inf))
        near_part = (found[:, i * tile :] * weight).astype(BF16)
        if i == 0:
            return near_part, None, None, jnp.exp(down)
        edge = cum[:, i * tile - 1 : i * tile]
        since = jnp.exp(down - edge)
        far_part = (found[:, : i * tile] * jnp.exp(edge - cum[:, : i * tile])).astype(BF16)
        return near_part, far_part, since, since * jnp.exp(edge)

    def finish(j, i, near_part, far_part, since, decay):
        cols = slice(j * width, (j + 1) * width)
        from_cols = columns(j)
        here = slice(i * tile, (i + 1) * tile)
        out = jnp.dot(near_part, v_ref[here, from_cols], preferred_element_type=F32)
        if far_part is not None:
            out = out + since[:, :width] * jnp.dot(
                far_part, v_ref[: i * tile, from_cols], preferred_element_type=F32
            )
        out_ref[here, cols] = out
        decayed_ref[here, cols] = (
            q_ref[here, columns(j)].astype(F32) * decay[:, :width]
        ).astype(BF16)

    units = [(j, i) for i in range(rows // tile) for j in range(count)]
    found, held_parts = {}, {}
    for step in range(len(units) + 3):
        if step < len(units):
            found[step] = scores(*units[step])
        if 0 <= step - 2 < len(units):
            held_parts[step - 2] = weighted(*units[step - 2], found.pop(step - 2))
        if 0 <= step - 3:
            finish(*units[step - 3], *held_parts.pop(step - 3))


def local(place, cum, query, key, value, size, count, width, away):
    rows = cum.shape[1]
    cols = count * width
    return pl.pallas_call(
        functools.partial(local_kernel, size, count, width, away),
        in_specs=[SMEM] + [VMEM] * 4,
        out_specs=[VMEM, VMEM],
        out_shape=[held((rows, cols), F32), held((rows, cols), BF16)],
        compiler_params=PARAMS,
        name="local",
    )(place, near(cum), near(query), near(key), near(value))


def norm_kernel(size, count, width, chips, block, away, group, place_ref, chip_ref, core_ref, gain_ref, *refs):
    members = len(group)
    inside_refs, query_refs = refs[:members], refs[members : 2 * members]
    state_refs, out_ref = refs[2 * members : -1], refs[-1]
    ones = jnp.full((width, width), 1.0 / width, F32).astype(BF16)
    units = [(at, j) for at in range(members) for j in range(count)]

    def rows_of(ref, j):
        src = slice(j * width, (j + 1) * width)
        found = []
        for i in range(chips):
            spot = 2 * lax.rem(chip_ref[0] + i, chips)
            spot = spot + (1 - core_ref[0] if away else core_ref[0])
            found.append(ref[pl.ds(pl.multiple_of(spot * block, block), block), src])
        return jnp.concatenate(found, axis=0)

    def carry(at, j):
        state = state_refs[at][j * width : (j + 1) * width, :]
        return jnp.dot(rows_of(query_refs[at], j), state, preferred_element_type=F32)

    def square(at, j, carried):
        attended = rows_of(inside_refs[at], j) + carried
        return attended, jnp.dot(
            (attended * attended).astype(BF16), ones, preferred_element_type=F32
        )

    def finish_head(at, j, attended, mean):
        gain = gain_ref[pl.ds(part_of(place_ref, size, group[at]) * count + j, 1), :]
        col = (at * count + j) * width
        out_ref[:, col : col + width] = (
            attended * lax.rsqrt(mean + 1e-06) * gain
        ).astype(out_ref.dtype)

    first, second = {}, {}
    for step in range(len(units) + 2):
        if step < len(units):
            first[step] = carry(*units[step])
        if 0 <= step - 1 < len(units):
            second[step - 1] = square(*units[step - 1], first.pop(step - 1))
        if 0 <= step - 2:
            finish_head(*units[step - 2], *second.pop(step - 2))


def norm(group, scalars, gain, insides, queries, entering, size, count, width, chips, block, away):
    cols = len(group) * count * width
    parts = [a[i] for a in (insides, queries, entering) for i in group]
    return pl.pallas_call(
        functools.partial(norm_kernel, size, count, width, chips, block, away, group),
        in_specs=[SMEM] * 3 + [VMEM] * (1 + len(parts)),
        out_specs=VMEM,
        out_shape=held((chips * block, cols), BF16),
        compiler_params=PARAMS,
        name="norm_away" if away else "norm_home",
    )(*scalars, gain, *map(near, parts))


def project_kernel(block, first, tile, size, place_ref, *refs):
    own_ref, away_ref = refs[-2:]
    sides = [(refs[0], refs[1], refs[4]), (refs[2], refs[3], refs[5])]
    cols = refs[1].shape[1]
    for i in range(own_ref.shape[1] // tile):
        here = slice(i * tile, (i + 1) * tile)
        span = slice(first + i * tile, first + (i + 1) * tile)
        total = None
        for one_ref, two_ref, weight_ref in sides:
            for away in range(size):
                last = away == size - 1
                normed = two_ref[...] if last else one_ref[:, away * cols : (away + 1) * cols]
                start = pl.multiple_of(part_of(place_ref, size, away) * cols, cols)
                part = jnp.dot(
                    normed, weight_ref[pl.ds(start, cols), span], preferred_element_type=F32
                )
                total = part if total is None else total + part
        own_ref[:, here] = total[:block]
        away_ref[:, here] = total[block:].astype(away_ref.dtype)


def project(place, home, other, first_weight, second_weight, hold, block, first, count, tile, size):
    rows = home[0].shape[0]
    tile = tile_of(count, tile)
    return pl.pallas_call(
        functools.partial(project_kernel, block, first, tile, size),
        in_specs=[SMEM] + [VMEM] * 6 + [ANY],
        out_specs=[VMEM, VMEM],
        out_shape=[held((block, count), F32), held((rows - block, count), BF16)],
        compiler_params=PARAMS,
        name="project",
    )(place, *map(near, [*home, *other, first_weight, second_weight]), hold)


def finish_kernel(first, pieces, own_ref, residual_ref, *refs):
    part_refs, (out_ref, total_ref, sems) = refs[:pieces], refs[-3:]
    count = own_ref.shape[1]
    total = own_ref[...] + residual_ref[:, first : first + count].astype(F32)
    for ref in part_refs:
        total = total + ref[...].astype(F32)
    total_ref[...] = total.astype(BF16)
    rows = total_ref.shape[0] // sems.shape[0]
    copies = []
    for i in range(sems.shape[0]):
        here = pl.ds(i * rows, rows)
        copies.append(
            pltpu.make_async_copy(
                total_ref.at[here, :], out_ref.at[here, pl.ds(first, count)], sems.at[i]
            )
        )
    for copy in copies:
        copy.start()
    for copy in copies:
        copy.wait()


def finish(out, own, residual, parts, first):
    block, total = residual.shape
    earlier = [] if out is None else [outside(out)]
    return pl.pallas_call(
        functools.partial(finish_kernel, first, len(parts)),
        in_specs=[VMEM] * (2 + len(parts)) + [ANY] * len(earlier),
        out_specs=ANY,
        out_shape=pltpu.HBM((block, total), BF16),
        scratch_shapes=[
            pltpu.VMEM((block, own.shape[1]), BF16),
            pltpu.SemaphoreType.DMA((tile_of(block // 16, 4),)),
        ],
        input_output_aliases={2 + len(parts): 0} if earlier else {},
        compiler_params=PARAMS,
        name="finish",
    )(near(own), near(residual), *map(near, parts), *earlier)


def shards(blocks, group, q_spikes, k_spikes, v_spikes, log_decay, norm_gain, out_weight, residual):
    rows, heads = log_decay.shape
    width = q_spikes.shape[1] // heads
    size = 4 if heads % 4 == 0 and blocks % 4 == 0 else 2
    count = heads // size
    chips = group // 2
    block = rows // group
    place = lax.axis_index("ctx").astype(jnp.int32)
    member = lax.axis_index("exp").astype(jnp.int32)
    place, chip, core = lax.optimization_barrier(
        tuple(a.reshape(1) for a in (place, member >> 1, member & 1))
    )
    cores = [(i, i ^ 1) for i in range(group)]

    def swap(x, bit):
        return lax.ppermute(x, "ctx", [(i, i ^ bit) for i in range(blocks)])

    logd = log_decay.T
    if heads % 8:
        logd = jnp.pad(logd, ((0, pad_rows(heads) - heads), (0, 0)))
    sent, key, value = early_states(place, logd, k_spikes, v_spikes, size, count, width)
    met = [swap(a, i + 1) for i, a in enumerate(sent)]
    kept, query, cum = load(place, logd, key, value, q_spikes, sent[0], size, count, width)
    kept, weight = lax.optimization_barrier((kept, out_weight))
    far_weight = lax.ppermute(outside(weight), "exp", cores)
    total = out_weight.shape[1]
    tile = tile_of(total, 512)

    pay, past, window = gather(place, kept, met, size, count, width, int(2 * size < blocks))
    _, own_weight = lax.optimization_barrier((pay, out_weight))
    before, got, level, bit = None, None, 0, size
    while bit < blocks:
        got = swap(pay, bit)
        if 2 * bit < blocks:
            pay, before, window = widen(
                place, got, window, before, count, width, bit, int(4 * bit < blocks)
            )
        bit, level = 2 * bit, level + 1
    own, *theirs = enter(place, got, before, past, size, count, width, bit // 2 if level else 0)
    entering = [own] + [swap(a, i + 1) for i, a in enumerate(theirs)]

    insides, queries = [], []
    for away in range(size):
        inside, decayed = local(place, cum, query, key, value, size, count, width, away)
        insides.append(inside)
        queries.append(decayed)

    gain = norm_gain.reshape(heads, width)
    home, other = [], []
    for which in (range(size - 1), range(size - 1, size)):
        args = (
            tuple(which), (place, chip, core), gain, insides, queries, entering,
            size, count, width, chips, block,
        )
        away = norm(*args, True)
        other.append(lax.ppermute(away, "exp", cores))
        home.append(norm(*args, False))

    sizes = [tile, tile]
    while total - sum(sizes) > 2 * tile:
        sizes.append(2 * tile)
    rest = total - sum(sizes)
    sizes += [rest - tile // 2, tile // 2] if rest > tile // 2 else [rest]
    out, at, hold = None, 0, home[1]
    sums = []
    for span in sizes:
        own, pieces = project(place, home, other, own_weight, far_weight, hold, block, at, span, tile, size)
        hold = pieces
        got = []
        for d in range(1, chips):
            piece = pieces[(d - 1) * block : d * block]
            perm = [(i, 2 * ((i // 2 + d) % chips) + i % 2) for i in range(group)]
            got.append(lax.ppermute(piece, "exp", perm))
        sums.append((own, got, at))
        at += span
    for own, got, at in sums:
        out = finish(out, own, residual, got, at)
    return out


def solution(mesh):
    in_specs = (
        P("ctx", "exp"),
        P("ctx", "exp"),
        P("ctx", "exp"),
        P("ctx", "exp"),
        P("exp"),
        P("exp", None),
        P(("ctx", "exp"), None),
    )
    out_specs = P(("ctx", "exp"), None)

    def body(*args):
        return shards(mesh.shape["ctx"], mesh.shape["exp"], *args)

    return jax.shard_map(
        body, mesh=mesh, in_specs=in_specs, out_specs=out_specs, check_vma=False
    )
```

```python
import functools

import jax
import jax.numpy as jnp
from jax import lax
from jax.experimental import pallas as pl
from jax.experimental.pallas import tpu as pltpu
from jax.sharding import PartitionSpec as P


F32 = jnp.float32
BF16 = jnp.bfloat16
PARAMS = pltpu.CompilerParams(vmem_limit_bytes=16 << 20)
PACKED = pltpu.CompilerParams(vmem_limit_bytes=16 << 20)
VMEM = pl.BlockSpec(memory_space=pltpu.VMEM)
SMEM = pl.BlockSpec(memory_space=pltpu.SMEM)
ANY = pl.BlockSpec(memory_space=pl.ANY)


def held(shape, kind):
    return pltpu.VMEM(shape, kind)


def near(x):
    return pltpu.with_memory_space_constraint(x, pltpu.VMEM)


def outside(x):
    return pltpu.with_memory_space_constraint(x, pltpu.HBM)


def tile_of(size, want):
    while size % want:
        want //= 2
    return want


def pad_rows(count):
    return -(-count // 8) * 8


def running_sum(logd):
    heads, rows = logd.shape
    tile = tile_of(rows, 128)
    count = rows // tile
    tiles = jnp.concatenate([logd[:, i * tile : (i + 1) * tile] for i in range(count)], axis=0)
    one = tiles.astype(BF16).astype(F32)
    two = (tiles - one).astype(BF16).astype(F32)
    three = tiles - one - two
    parts = jnp.concatenate([one, two, three], axis=0).astype(BF16)
    upper = (
        lax.broadcasted_iota(jnp.int32, (tile, tile), 0)
        <= lax.broadcasted_iota(jnp.int32, (tile, tile), 1)
    ).astype(F32)
    sums = jnp.dot(parts, upper.astype(BF16), preferred_element_type=F32)
    size = count * heads
    sums = sums[:size] + sums[size : 2 * size] + sums[2 * size :]
    done, carry = [], None
    for i in range(count):
        part = sums[i * heads : (i + 1) * heads]
        if carry is not None:
            part = part + carry
        carry = part[:, tile - 1 : tile]
        done.append(part)
    return jnp.concatenate(done, axis=1)


def copies_of(source, target, sems, first=0):
    count = sems.shape[0]
    size = target.shape[0] // count
    return [
        pltpu.make_async_copy(
            source.at[pl.ds(i * size, size), pl.ds(first, target.shape[1])],
            target.at[pl.ds(i * size, size), :],
            sems.at[i],
        )
        for i in range(count)
    ]


def pay_shape(count, width, kind):
    return held((count * width + 2 * pad_rows(count), width), kind)


def part_of(place_ref, size, away):
    return (place_ref[0] & (size - 1)) ^ away


def turned_keys(part, count, width, key, weight_ref):
    turned = [key[:, j * width : (j + 1) * width].T for j in range(count)]
    return [
        turned[j] * weight_ref[pl.ds(part * count + j, 1), :].astype(BF16) for j in range(count)
    ]


def put_states(part, count, width, keyed, value, cum_ref, pay_ref):
    rows = cum_ref.shape[1]
    decays = []
    for j in range(count):
        state = jnp.dot(
            keyed[j], value[:, j * width : (j + 1) * width], preferred_element_type=F32
        )
        pay_ref[j * width : (j + 1) * width, :] = state.astype(pay_ref.dtype)
        total = cum_ref[pl.ds(part * count + j, 1), :][:, rows - 1 : rows]
        decays.append(jnp.broadcast_to(jnp.exp(total), (1, width)))
    put_decays(pay_ref, decays, count, width)


def put_sums(logd_ref, cum_ref, weight_ref):
    cum = running_sum(logd_ref[...])
    cum_ref[...] = cum
    weight_ref[...] = jnp.exp(cum[:, cum.shape[1] - 1 :] - cum)


def part_columns(place_ref, size, away, cols):
    return pl.ds(pl.multiple_of(part_of(place_ref, size, away) * cols, cols), cols)


def early_kernel(size, count, width, place_ref, logd_in, key_in, value_in, *refs):
    pay_refs = refs[: size - 1]
    key_ref, value_ref, logd_ref, cum_ref, weight_ref, logd_sem, sems = refs[size - 1 :]
    logd = pltpu.make_async_copy(logd_in, logd_ref, logd_sem)
    keys, values = copies_of(key_in, key_ref, sems.at[0]), copies_of(value_in, value_ref, sems.at[1])
    for copy in (logd, *keys, *values):
        copy.start()
    logd.wait()
    put_sums(logd_ref, cum_ref, weight_ref)
    for copy in keys:
        copy.wait()
    parts = [part_of(place_ref, size, away) for away in range(1, size)]
    spans = [part_columns(place_ref, size, away, count * width) for away in range(1, size)]
    keyed = [
        turned_keys(part, count, width, key_ref[:, here], weight_ref)
        for part, here in zip(parts, spans)
    ]
    for copy in values:
        copy.wait()
    for part, here, turned, pay_ref in zip(parts, spans, keyed, pay_refs):
        put_states(part, count, width, turned, value_ref[:, here], cum_ref, pay_ref)


def early_states(place, logd, key, value, size, count, width):
    heads, rows = logd.shape
    *pays, key, value = pl.pallas_call(
        functools.partial(early_kernel, size, count, width),
        in_specs=[SMEM] + [ANY] * 3,
        out_specs=[VMEM] * (size + 1),
        out_shape=[pay_shape(count, width, BF16)] * (size - 1) + [held(key.shape, BF16)] * 2,
        scratch_shapes=[pltpu.VMEM((heads, rows), F32)] * 3
        + [pltpu.SemaphoreType.DMA, pltpu.SemaphoreType.DMA((2, 2))],
        compiler_params=PACKED,
        name="early_states",
    )(place, outside(logd), outside(key), outside(value))
    return pays, key, value


def load_kernel(size, count, width, place_ref, logd_in, query_in, key_ref, value_ref, hold_ref, *refs):
    pay_ref, query_ref, cum_ref, logd_ref, weight_ref, logd_sem, sems = refs
    logd = pltpu.make_async_copy(logd_in, logd_ref, logd_sem)
    logd.start()
    copies = copies_of(query_in, query_ref, sems)
    for copy in copies:
        copy.start()
    logd.wait()
    put_sums(logd_ref, cum_ref, weight_ref)
    here = part_columns(place_ref, size, 0, count * width)
    part = part_of(place_ref, size, 0)
    keyed = turned_keys(part, count, width, key_ref[:, here], weight_ref)
    put_states(part, count, width, keyed, value_ref[:, here], cum_ref, pay_ref)
    for copy in copies:
        copy.wait()


def load(place, logd, key, value, query, hold, size, count, width):
    heads, rows = logd.shape
    return pl.pallas_call(
        functools.partial(load_kernel, size, count, width),
        in_specs=[SMEM, ANY, ANY, VMEM, VMEM, ANY],
        out_specs=[VMEM] * 3,
        out_shape=[
            pay_shape(count, width, F32),
            held(query.shape, BF16),
            held((heads, rows), F32),
        ],
        scratch_shapes=[pltpu.VMEM((heads, rows), F32)] * 2
        + [pltpu.SemaphoreType.DMA, pltpu.SemaphoreType.DMA((2,))],
        compiler_params=PACKED,
        name="load",
    )(place, outside(logd), outside(query), near(key), near(value), hold)


def decay_row(pay, j, count, width):
    at = count * width + j
    pad = pad_rows(count)
    return pay[at : at + 1, :].astype(F32) + pay[at + pad : at + pad + 1, :].astype(F32)


def put_decays(ref, rows, count, width):
    pad = pad_rows(count)
    blank = [jnp.zeros((1, width), F32)] * (pad - count)
    if ref.dtype == BF16:
        highs = [row.astype(BF16).astype(F32) for row in rows]
        lows = [row - high for row, high in zip(rows, highs)]
    else:
        highs, lows = rows, [jnp.zeros_like(row) for row in rows]
    tail = jnp.concatenate(highs + blank + lows + blank, axis=0)
    ref[count * width :, :] = tail.astype(ref.dtype)


def picked(values, index):
    found = values[0]
    for i in range(1, len(values)):
        found = jnp.where(index == i, values[i], found)
    return found


def gather_kernel(size, count, width, place_ref, *refs):
    in_refs, pay_ref, past_refs = refs[:size], refs[size], refs[size + 1 : 2 * size]
    window_refs = refs[2 * size :]
    decays = [[] for _ in range(size)]
    for j in range(count):
        rows = slice(j * width, (j + 1) * width)
        found = [ref[rows, :].astype(F32) for ref in in_refs]
        found_decays = [decay_row(ref, j, count, width) for ref in in_refs]
        total, total_decay = None, None
        for b in range(size):
            index = part_of(place_ref, size, b)
            state, decay = picked(found, index), picked(found_decays, index)
            if b:
                past_refs[b - 1][rows, :] = total
                decays[b - 1].append(total_decay)
                total, total_decay = total * decay + state, total_decay * decay
            else:
                total, total_decay = state, decay
        for ref in (pay_ref, *window_refs):
            ref[rows, :] = total.astype(ref.dtype)
        decays[-1].append(total_decay)
    for ref, rows in zip(past_refs, decays):
        put_decays(ref, rows, count, width)
    for ref in (pay_ref, *window_refs):
        put_decays(ref, decays[-1], count, width)


def gather(place, own, met, size, count, width, keep):
    shape = own.shape
    pay, *past = pl.pallas_call(
        functools.partial(gather_kernel, size, count, width),
        in_specs=[SMEM] + [VMEM] * size,
        out_specs=[VMEM] * (size + keep),
        out_shape=[held(shape, BF16)] + [held(shape, F32)] * (size - 1 + keep),
        compiler_params=PARAMS,
        name="gather",
    )(place, near(own), *map(near, met))
    return pay, past[: size - 1], past[-1]


def widen_kernel(count, width, bit, opening, keep, place_ref, got_ref, window_ref, before_ref, pay_ref, past_ref, *refs):
    is_later = (place_ref[0] & bit) != 0
    decays, pasts = [], []
    for j in range(count):
        rows = slice(j * width, (j + 1) * width)
        got, window = got_ref[rows, :].astype(F32), window_ref[rows, :]
        got_decay = decay_row(got_ref, j, count, width)
        window_decay = decay_row(window_ref, j, count, width)
        wide = jnp.where(is_later, got, window) * jnp.where(
            is_later, window_decay, got_decay
        ) + jnp.where(is_later, window, got)
        pay_ref[rows, :] = wide.astype(pay_ref.dtype)
        if keep:
            refs[0][rows, :] = wide
        decays.append(got_decay * window_decay)
        if opening:
            past_ref[rows, :] = jnp.where(is_later, got, jnp.zeros_like(got))
            pasts.append(jnp.where(is_later, got_decay, jnp.ones_like(got_decay)))
        else:
            before = before_ref[rows, :]
            before_decay = decay_row(before_ref, j, count, width)
            past_ref[rows, :] = jnp.where(is_later, got * before_decay + before, before)
            pasts.append(jnp.where(is_later, got_decay * before_decay, before_decay))
    put_decays(pay_ref, decays, count, width)
    if keep:
        put_decays(refs[0], decays, count, width)
    put_decays(past_ref, pasts, count, width)


def widen(place, got, window, before, count, width, bit, keep):
    shape = got.shape
    opening = before is None
    before = window if before is None else before
    done = pl.pallas_call(
        functools.partial(widen_kernel, count, width, bit, opening, keep),
        in_specs=[SMEM, VMEM, VMEM, VMEM],
        out_specs=[VMEM] * (2 + keep),
        out_shape=[held(shape, BF16), held(shape, F32)] + [held(shape, F32)] * keep,
        compiler_params=PARAMS,
        name="widen",
    )(place, near(got), near(window), near(before))
    return done if keep else (*done, None)


def enter_kernel(size, count, width, bit, opening, place_ref, got_ref, before_ref, *refs):
    past_refs, out_refs = refs[: size - 1], refs[size - 1 :]
    is_later = (place_ref[0] & bit) != 0
    for j in range(count):
        rows = slice(j * width, (j + 1) * width)
        before = jnp.zeros((width, width), F32)
        if bit:
            got = got_ref[rows, :].astype(F32)
            if not opening:
                before = before_ref[rows, :]
                got = got * decay_row(before_ref, j, count, width) + before
            before = jnp.where(is_later, got, before)
        entering = [before] + [
            before * decay_row(ref, j, count, width) + ref[rows, :] for ref in past_refs
        ]
        for away in range(size):
            index = part_of(place_ref, size, away)
            out_refs[away][rows, :] = picked(entering, index).astype(BF16)


def enter(place, got, before, past, size, count, width, bit):
    opening = before is None
    got = past[0] if got is None else got
    before = past[0] if opening else before
    return pl.pallas_call(
        functools.partial(enter_kernel, size, count, width, bit, opening),
        in_specs=[SMEM] + [VMEM] * (size + 1),
        out_specs=[VMEM] * size,
        out_shape=[held((count * width, width), BF16)] * size,
        compiler_params=PARAMS,
        name="enter",
    )(place, near(got), near(before), *map(near, past))


def local_kernel(size, count, width, away, place_ref, cum_ref, q_ref, k_ref, v_ref, out_ref, decayed_ref):
    part = part_of(place_ref, size, away)
    sums = [cum_ref[pl.ds(part * count + j, 1), :] for j in range(count)]
    rows = cum_ref.shape[1]
    tile = tile_of(rows, 2 * width)
    causal = lax.broadcasted_iota(jnp.int32, (tile, tile), 0) >= lax.broadcasted_iota(
        jnp.int32, (tile, tile), 1
    )

    def downward(row):
        turned = jnp.broadcast_to(row, (width, tile)).T
        return jnp.concatenate([turned] * (tile // width), axis=1)

    def columns(j):
        return pl.ds(pl.multiple_of((part * count + j) * width, width), width)

    def scores(j, i):
        return lax.dot_general(
            q_ref[i * tile : (i + 1) * tile, columns(j)],
            k_ref[: (i + 1) * tile, columns(j)],
            (((1,), (1,)), ((), ())),
            preferred_element_type=F32,
        )

    def weighted(j, i, found):
        cum = sums[j]
        here = slice(i * tile, (i + 1) * tile)
        across = cum[:, here]
        down = downward(across)
        weight = jnp.exp(jnp.where(causal, down - across, -jnp.inf))
        near_part = (found[:, i * tile :] * weight).astype(BF16)
        if i == 0:
            return near_part, None, None, jnp.exp(down)
        edge = cum[:, i * tile - 1 : i * tile]
        since = jnp.exp(down - edge)
        far_part = (found[:, : i * tile] * jnp.exp(edge - cum[:, : i * tile])).astype(BF16)
        return near_part, far_part, since, since * jnp.exp(edge)

    def finish(j, i, near_part, far_part, since, decay):
        cols = slice(j * width, (j + 1) * width)
        from_cols = columns(j)
        here = slice(i * tile, (i + 1) * tile)
        out = jnp.dot(near_part, v_ref[here, from_cols], preferred_element_type=F32)
        if far_part is not None:
            out = out + since[:, :width] * jnp.dot(
                far_part, v_ref[: i * tile, from_cols], preferred_element_type=F32
            )
        out_ref[here, cols] = out
        decayed_ref[here, cols] = (
            q_ref[here, columns(j)].astype(F32) * decay[:, :width]
        ).astype(BF16)

    units = [(j, i) for i in range(rows // tile) for j in range(count)]
    found, held_parts = {}, {}
    for step in range(len(units) + 3):
        if step < len(units):
            found[step] = scores(*units[step])
        if 0 <= step - 2 < len(units):
            held_parts[step - 2] = weighted(*units[step - 2], found.pop(step - 2))
        if 0 <= step - 3:
            finish(*units[step - 3], *held_parts.pop(step - 3))


def local(place, cum, query, key, value, size, count, width, away):
    rows = cum.shape[1]
    cols = count * width
    return pl.pallas_call(
        functools.partial(local_kernel, size, count, width, away),
        in_specs=[SMEM] + [VMEM] * 4,
        out_specs=[VMEM, VMEM],
        out_shape=[held((rows, cols), F32), held((rows, cols), BF16)],
        compiler_params=PARAMS,
        name="local",
    )(place, near(cum), near(query), near(key), near(value))


def norm_kernel(size, count, width, chips, block, away, group, place_ref, chip_ref, core_ref, gain_ref, *refs):
    members = len(group)
    inside_refs, query_refs = refs[:members], refs[members : 2 * members]
    state_refs, out_ref = refs[2 * members : -1], refs[-1]
    ones = jnp.full((width, width), 1.0 / width, F32).astype(BF16)
    units = [(at, j) for at in range(members) for j in range(count)]

    def rows_of(ref, j):
        src = slice(j * width, (j + 1) * width)
        found = []
        for i in range(chips):
            spot = 2 * lax.rem(chip_ref[0] + i, chips)
            spot = spot + (1 - core_ref[0] if away else core_ref[0])
            found.append(ref[pl.ds(pl.multiple_of(spot * block, block), block), src])
        return jnp.concatenate(found, axis=0)

    def carry(at, j):
        state = state_refs[at][j * width : (j + 1) * width, :]
        return jnp.dot(rows_of(query_refs[at], j), state, preferred_element_type=F32)

    def square(at, j, carried):
        attended = rows_of(inside_refs[at], j) + carried
        return attended, jnp.dot(
            (attended * attended).astype(BF16), ones, preferred_element_type=F32
        )

    def finish_head(at, j, attended, mean):
        gain = gain_ref[pl.ds(part_of(place_ref, size, group[at]) * count + j, 1), :]
        col = (at * count + j) * width
        out_ref[:, col : col + width] = (
            attended * lax.rsqrt(mean + 1e-06) * gain
        ).astype(out_ref.dtype)

    first, second = {}, {}
    for step in range(len(units) + 2):
        if step < len(units):
            first[step] = carry(*units[step])
        if 0 <= step - 1 < len(units):
            second[step - 1] = square(*units[step - 1], first.pop(step - 1))
        if 0 <= step - 2:
            finish_head(*units[step - 2], *second.pop(step - 2))


def norm(group, scalars, gain, insides, queries, entering, size, count, width, chips, block, away):
    cols = len(group) * count * width
    parts = [a[i] for a in (insides, queries, entering) for i in group]
    return pl.pallas_call(
        functools.partial(norm_kernel, size, count, width, chips, block, away, group),
        in_specs=[SMEM] * 3 + [VMEM] * (1 + len(parts)),
        out_specs=VMEM,
        out_shape=held((chips * block, cols), BF16),
        compiler_params=PARAMS,
        name="norm_away" if away else "norm_home",
    )(*scalars, gain, *map(near, parts))


def summed(size, place_ref, terms, span, total=None):
    for ref, at, away, weight_ref in terms:
        cols = weight_ref.shape[0] // size
        rows = part_columns(place_ref, size, away, cols)
        part = jnp.dot(
            ref[:, at * cols : (at + 1) * cols], weight_ref[rows, span], preferred_element_type=F32
        )
        total = part if total is None else total + part
    return total


def begin_kernel(size, place_ref, one_ref, two_ref, met_ref, near_ref, far_ref, out_ref):
    early = range(size - 1)
    terms = [(one_ref, away, away, near_ref) for away in early]
    terms += [(met_ref, away, away, far_ref) for away in early]
    terms += [(two_ref, 0, size - 1, near_ref)]
    out_ref[...] = summed(size, place_ref, terms, slice(0, out_ref.shape[1]))


def begin(place, home, met, first_weight, second_weight, count, size):
    rows = met.shape[0]
    return pl.pallas_call(
        functools.partial(begin_kernel, size),
        in_specs=[SMEM] + [VMEM] * 5,
        out_specs=VMEM,
        out_shape=held((rows, count), F32),
        compiler_params=PARAMS,
        name="begin",
    )(place, *map(near, [*home, met, first_weight, second_weight]))


def complete_kernel(block, size, place_ref, begun_ref, two_ref, far_ref, own_ref, away_ref):
    span = slice(0, own_ref.shape[1])
    total = summed(size, place_ref, [(two_ref, 0, size - 1, far_ref)], span, begun_ref[...])
    own_ref[...] = total[:block]
    away_ref[...] = total[block:].astype(away_ref.dtype)


def complete(place, begun, two, second_weight, block, size):
    rows, count = begun.shape
    return pl.pallas_call(
        functools.partial(complete_kernel, block, size),
        in_specs=[SMEM] + [VMEM] * 3,
        out_specs=[VMEM, VMEM],
        out_shape=[held((block, count), F32), held((rows - block, count), BF16)],
        compiler_params=PARAMS,
        name="complete",
    )(place, near(begun), near(two), near(second_weight))


def project_kernel(block, first, tile, size, place_ref, *refs):
    own_ref, away_ref = refs[-2:]
    terms = []
    for one_ref, two_ref, weight_ref in ((refs[0], refs[1], refs[4]), (refs[2], refs[3], refs[5])):
        terms += [(one_ref, away, away, weight_ref) for away in range(size - 1)]
        terms += [(two_ref, 0, size - 1, weight_ref)]
    for i in range(own_ref.shape[1] // tile):
        here = slice(i * tile, (i + 1) * tile)
        span = slice(first + i * tile, first + (i + 1) * tile)
        total = summed(size, place_ref, terms, span)
        own_ref[:, here] = total[:block]
        away_ref[:, here] = total[block:].astype(away_ref.dtype)


def project(place, home, other, first_weight, second_weight, hold, block, first, count, tile, size):
    rows = home[0].shape[0]
    tile = tile_of(count, tile)
    return pl.pallas_call(
        functools.partial(project_kernel, block, first, tile, size),
        in_specs=[SMEM] + [VMEM] * 6 + [ANY],
        out_specs=[VMEM, VMEM],
        out_shape=[held((block, count), F32), held((rows - block, count), BF16)],
        compiler_params=PARAMS,
        name="project",
    )(place, *map(near, [*home, *other, first_weight, second_weight]), hold)


def finish_kernel(first, pieces, own_ref, residual_ref, *refs):
    part_refs, (out_ref, total_ref, sems) = refs[:pieces], refs[-3:]
    count = own_ref.shape[1]
    total = own_ref[...] + residual_ref[:, first : first + count].astype(F32)
    for ref in part_refs:
        total = total + ref[...].astype(F32)
    total_ref[...] = total.astype(BF16)
    rows = total_ref.shape[0] // sems.shape[0]
    copies = []
    for i in range(sems.shape[0]):
        here = pl.ds(i * rows, rows)
        copies.append(
            pltpu.make_async_copy(
                total_ref.at[here, :], out_ref.at[here, pl.ds(first, count)], sems.at[i]
            )
        )
    for copy in copies:
        copy.start()
    for copy in copies:
        copy.wait()


def finish(out, own, residual, parts, first):
    block, total = residual.shape
    earlier = [] if out is None else [outside(out)]
    return pl.pallas_call(
        functools.partial(finish_kernel, first, len(parts)),
        in_specs=[VMEM] * (2 + len(parts)) + [ANY] * len(earlier),
        out_specs=ANY,
        out_shape=pltpu.HBM((block, total), BF16),
        scratch_shapes=[
            pltpu.VMEM((block, own.shape[1]), BF16),
            pltpu.SemaphoreType.DMA((tile_of(block // 16, 4),)),
        ],
        input_output_aliases={2 + len(parts): 0} if earlier else {},
        compiler_params=PARAMS,
        name="finish",
    )(near(own), near(residual), *map(near, parts), *earlier)


def shards(blocks, group, q_spikes, k_spikes, v_spikes, log_decay, norm_gain, out_weight, residual):
    rows, heads = log_decay.shape
    width = q_spikes.shape[1] // heads
    size = 4 if heads % 4 == 0 and blocks % 4 == 0 else 2
    count = heads // size
    chips = group // 2
    block = rows // group
    place = lax.axis_index("ctx").astype(jnp.int32)
    member = lax.axis_index("exp").astype(jnp.int32)
    place, chip, core = lax.optimization_barrier(
        tuple(a.reshape(1) for a in (place, member >> 1, member & 1))
    )
    cores = [(i, i ^ 1) for i in range(group)]

    def swap(x, bit):
        return lax.ppermute(x, "ctx", [(i, i ^ bit) for i in range(blocks)])

    logd = log_decay.T
    if heads % 8:
        logd = jnp.pad(logd, ((0, pad_rows(heads) - heads), (0, 0)))
    sent, key, value = early_states(place, logd, k_spikes, v_spikes, size, count, width)
    met = [swap(a, i + 1) for i, a in enumerate(sent)]
    kept, query, cum = load(place, logd, key, value, q_spikes, sent[0], size, count, width)
    kept, weight = lax.optimization_barrier((kept, out_weight))
    far_weight = lax.ppermute(outside(weight), "exp", cores)
    total = out_weight.shape[1]
    tile = tile_of(total, 512)

    pay, past, window = gather(place, kept, met, size, count, width, int(2 * size < blocks))
    _, own_weight = lax.optimization_barrier((pay, out_weight))
    before, got, level, bit = None, None, 0, size
    while bit < blocks:
        got = swap(pay, bit)
        if 2 * bit < blocks:
            pay, before, window = widen(
                place, got, window, before, count, width, bit, int(4 * bit < blocks)
            )
        bit, level = 2 * bit, level + 1
    own, *theirs = enter(place, got, before, past, size, count, width, bit // 2 if level else 0)
    entering = [own] + [swap(a, i + 1) for i, a in enumerate(theirs)]

    insides, queries = [], []
    for away in range(size):
        inside, decayed = local(place, cum, query, key, value, size, count, width, away)
        insides.append(inside)
        queries.append(decayed)

    gain = norm_gain.reshape(heads, width)
    home, other = [], []
    for which in (range(size - 1), range(size - 1, size)):
        args = (
            tuple(which), (place, chip, core), gain, insides, queries, entering,
            size, count, width, chips, block,
        )
        away = norm(*args, True)
        other.append(lax.ppermute(away, "exp", cores))
        home.append(norm(*args, False))

    sizes = [tile, tile]
    while total - sum(sizes) > 2 * tile:
        sizes.append(2 * tile)
    rest = total - sum(sizes)
    sizes += [rest - tile // 2, tile // 2] if rest > tile // 2 else [rest]
    begun = begin(place, home, other[0], own_weight, far_weight, sizes[0], size)
    out, at, hold = None, 0, None
    sums = []
    for index, span in enumerate(sizes):
        if index:
            own, pieces = project(
                place, home, other, own_weight, far_weight, hold, block, at, span, tile, size
            )
        else:
            own, pieces = complete(place, begun, other[1], far_weight, block, size)
        hold = pieces
        got = []
        for d in range(1, chips):
            piece = pieces[(d - 1) * block : d * block]
            perm = [(i, 2 * ((i // 2 + d) % chips) + i % 2) for i in range(group)]
            got.append(lax.ppermute(piece, "exp", perm))
        sums.append((own, got, at))
        at += span
    for own, got, at in sums:
        out = finish(out, own, residual, got, at)
    return out


def solution(mesh):
    in_specs = (
        P("ctx", "exp"),
        P("ctx", "exp"),
        P("ctx", "exp"),
        P("ctx", "exp"),
        P("exp"),
        P("exp", None),
        P(("ctx", "exp"), None),
    )
    out_specs = P(("ctx", "exp"), None)

    def body(*args):
        return shards(mesh.shape["ctx"], mesh.shape["exp"], *args)

    return jax.shard_map(
        body, mesh=mesh, in_specs=in_specs, out_specs=out_specs, check_vma=False
    )
```

```python
import functools

import jax
import jax.numpy as jnp
from jax import lax
from jax.experimental import pallas as pl
from jax.experimental.pallas import tpu as pltpu
from jax.sharding import PartitionSpec as P


F32 = jnp.float32
BF16 = jnp.bfloat16
PARAMS = pltpu.CompilerParams(vmem_limit_bytes=16 << 20)
PACKED = pltpu.CompilerParams(vmem_limit_bytes=16 << 20)
VMEM = pl.BlockSpec(memory_space=pltpu.VMEM)
SMEM = pl.BlockSpec(memory_space=pltpu.SMEM)
ANY = pl.BlockSpec(memory_space=pl.ANY)


def held(shape, kind):
    return pltpu.VMEM(shape, kind)


def near(x):
    return pltpu.with_memory_space_constraint(x, pltpu.VMEM)


def outside(x):
    return pltpu.with_memory_space_constraint(x, pltpu.HBM)


def tile_of(size, want):
    while size % want:
        want //= 2
    return want


def pad_rows(count):
    return -(-count // 8) * 8


def running_sum(logd):
    heads, rows = logd.shape
    tile = tile_of(rows, 128)
    count = rows // tile
    tiles = jnp.concatenate([logd[:, i * tile : (i + 1) * tile] for i in range(count)], axis=0)
    one = tiles.astype(BF16).astype(F32)
    two = (tiles - one).astype(BF16).astype(F32)
    three = tiles - one - two
    parts = jnp.concatenate([one, two, three], axis=0).astype(BF16)
    upper = (
        lax.broadcasted_iota(jnp.int32, (tile, tile), 0)
        <= lax.broadcasted_iota(jnp.int32, (tile, tile), 1)
    ).astype(F32)
    sums = jnp.dot(parts, upper.astype(BF16), preferred_element_type=F32)
    size = count * heads
    sums = sums[:size] + sums[size : 2 * size] + sums[2 * size :]
    done, carry = [], None
    for i in range(count):
        part = sums[i * heads : (i + 1) * heads]
        if carry is not None:
            part = part + carry
        carry = part[:, tile - 1 : tile]
        done.append(part)
    return jnp.concatenate(done, axis=1)


def copies_of(source, target, sems, first=0):
    count = sems.shape[0]
    size = target.shape[0] // count
    return [
        pltpu.make_async_copy(
            source.at[pl.ds(i * size, size), pl.ds(first, target.shape[1])],
            target.at[pl.ds(i * size, size), :],
            sems.at[i],
        )
        for i in range(count)
    ]


def pay_shape(count, width, kind):
    return held((count * width + 2 * pad_rows(count), width), kind)


def order_of(size):
    return [0, *range(size - 1, 0, -1)]


def part_of(place_ref, size, away):
    return (place_ref[0] & (size - 1)) ^ away


def turned_keys(part, count, width, key, weight_ref):
    turned = [key[:, j * width : (j + 1) * width].T for j in range(count)]
    return [
        turned[j] * weight_ref[pl.ds(part * count + j, 1), :].astype(BF16) for j in range(count)
    ]


def put_states(part, count, width, keyed, value, cum_ref, pay_ref):
    rows = cum_ref.shape[1]
    decays = []
    for j in range(count):
        state = jnp.dot(
            keyed[j], value[:, j * width : (j + 1) * width], preferred_element_type=F32
        )
        pay_ref[j * width : (j + 1) * width, :] = state.astype(pay_ref.dtype)
        total = cum_ref[pl.ds(part * count + j, 1), :][:, rows - 1 : rows]
        decays.append(jnp.broadcast_to(jnp.exp(total), (1, width)))
    put_decays(pay_ref, decays, count, width)


def put_sums(logd_ref, cum_ref, weight_ref):
    cum = running_sum(logd_ref[...])
    cum_ref[...] = cum
    weight_ref[...] = jnp.exp(cum[:, cum.shape[1] - 1 :] - cum)


def part_columns(place_ref, size, away, cols):
    return pl.ds(pl.multiple_of(part_of(place_ref, size, away) * cols, cols), cols)


def early_kernel(size, count, width, place_ref, logd_in, key_in, value_in, *refs):
    pay_refs = refs[: size - 1]
    key_ref, value_ref, logd_ref, cum_ref, weight_ref, logd_sem, sems = refs[size - 1 :]
    logd = pltpu.make_async_copy(logd_in, logd_ref, logd_sem)
    keys, values = copies_of(key_in, key_ref, sems.at[0]), copies_of(value_in, value_ref, sems.at[1])
    for copy in (logd, *keys, *values):
        copy.start()
    logd.wait()
    put_sums(logd_ref, cum_ref, weight_ref)
    for copy in keys + values:
        copy.wait()
    for away in range(1, size):
        part = part_of(place_ref, size, away)
        here = part_columns(place_ref, size, away, count * width)
        turned = turned_keys(part, count, width, key_ref[:, here], weight_ref)
        put_states(part, count, width, turned, value_ref[:, here], cum_ref, pay_refs[away - 1])


def early_states(place, logd, key, value, size, count, width):
    heads, rows = logd.shape
    *pays, key, value = pl.pallas_call(
        functools.partial(early_kernel, size, count, width),
        in_specs=[SMEM] + [ANY] * 3,
        out_specs=[VMEM] * (size + 1),
        out_shape=[pay_shape(count, width, BF16)] * (size - 1) + [held(key.shape, BF16)] * 2,
        scratch_shapes=[pltpu.VMEM((heads, rows), F32)] * 3
        + [pltpu.SemaphoreType.DMA, pltpu.SemaphoreType.DMA((2, 2))],
        compiler_params=PACKED,
        name="early_states",
    )(place, outside(logd), outside(key), outside(value))
    return pays, key, value


def load_kernel(size, count, width, place_ref, logd_in, query_in, key_ref, value_ref, hold_ref, *refs):
    pay_ref, query_ref, cum_ref, logd_ref, weight_ref, logd_sem, sems = refs
    logd = pltpu.make_async_copy(logd_in, logd_ref, logd_sem)
    logd.start()
    copies = copies_of(query_in, query_ref, sems)
    for copy in copies:
        copy.start()
    logd.wait()
    put_sums(logd_ref, cum_ref, weight_ref)
    here = part_columns(place_ref, size, 0, count * width)
    part = part_of(place_ref, size, 0)
    keyed = turned_keys(part, count, width, key_ref[:, here], weight_ref)
    put_states(part, count, width, keyed, value_ref[:, here], cum_ref, pay_ref)
    for copy in copies:
        copy.wait()


def load(place, logd, key, value, query, hold, size, count, width):
    heads, rows = logd.shape
    return pl.pallas_call(
        functools.partial(load_kernel, size, count, width),
        in_specs=[SMEM, ANY, ANY, VMEM, VMEM, ANY],
        out_specs=[VMEM] * 3,
        out_shape=[
            pay_shape(count, width, F32),
            held(query.shape, BF16),
            held((heads, rows), F32),
        ],
        scratch_shapes=[pltpu.VMEM((heads, rows), F32)] * 2
        + [pltpu.SemaphoreType.DMA, pltpu.SemaphoreType.DMA((2,))],
        compiler_params=PACKED,
        name="load",
    )(place, outside(logd), outside(query), near(key), near(value), hold)


def decay_row(pay, j, count, width):
    at = count * width + j
    pad = pad_rows(count)
    return pay[at : at + 1, :].astype(F32) + pay[at + pad : at + pad + 1, :].astype(F32)


def put_decays(ref, rows, count, width):
    pad = pad_rows(count)
    blank = [jnp.zeros((1, width), F32)] * (pad - count)
    if ref.dtype == BF16:
        highs = [row.astype(BF16).astype(F32) for row in rows]
        lows = [row - high for row, high in zip(rows, highs)]
    else:
        highs, lows = rows, [jnp.zeros_like(row) for row in rows]
    tail = jnp.concatenate(highs + blank + lows + blank, axis=0)
    ref[count * width :, :] = tail.astype(ref.dtype)


def picked(values, index):
    found = values[0]
    for i in range(1, len(values)):
        found = jnp.where(index == i, values[i], found)
    return found


def gather_kernel(size, count, width, place_ref, *refs):
    in_refs, pay_ref, past_refs = refs[:size], refs[size], refs[size + 1 : 2 * size]
    window_refs = refs[2 * size :]
    decays = [[] for _ in range(size)]
    for j in range(count):
        rows = slice(j * width, (j + 1) * width)
        found = [ref[rows, :].astype(F32) for ref in in_refs]
        found_decays = [decay_row(ref, j, count, width) for ref in in_refs]
        total, total_decay = None, None
        for b in range(size):
            index = part_of(place_ref, size, b)
            state, decay = picked(found, index), picked(found_decays, index)
            if b:
                past_refs[b - 1][rows, :] = total
                decays[b - 1].append(total_decay)
                total, total_decay = total * decay + state, total_decay * decay
            else:
                total, total_decay = state, decay
        for ref in (pay_ref, *window_refs):
            ref[rows, :] = total.astype(ref.dtype)
        decays[-1].append(total_decay)
    for ref, rows in zip(past_refs, decays):
        put_decays(ref, rows, count, width)
    for ref in (pay_ref, *window_refs):
        put_decays(ref, decays[-1], count, width)


def gather(place, own, met, size, count, width, keep):
    shape = own.shape
    pay, *past = pl.pallas_call(
        functools.partial(gather_kernel, size, count, width),
        in_specs=[SMEM] + [VMEM] * size,
        out_specs=[VMEM] * (size + keep),
        out_shape=[held(shape, BF16)] + [held(shape, F32)] * (size - 1 + keep),
        compiler_params=PARAMS,
        name="gather",
    )(place, near(own), *map(near, met))
    return pay, past[: size - 1], past[-1]


def widen_kernel(count, width, bit, opening, keep, place_ref, got_ref, window_ref, before_ref, pay_ref, past_ref, *refs):
    is_later = (place_ref[0] & bit) != 0
    decays, pasts = [], []
    for j in range(count):
        rows = slice(j * width, (j + 1) * width)
        got, window = got_ref[rows, :].astype(F32), window_ref[rows, :]
        got_decay = decay_row(got_ref, j, count, width)
        window_decay = decay_row(window_ref, j, count, width)
        wide = jnp.where(is_later, got, window) * jnp.where(
            is_later, window_decay, got_decay
        ) + jnp.where(is_later, window, got)
        pay_ref[rows, :] = wide.astype(pay_ref.dtype)
        if keep:
            refs[0][rows, :] = wide
        decays.append(got_decay * window_decay)
        if opening:
            past_ref[rows, :] = jnp.where(is_later, got, jnp.zeros_like(got))
            pasts.append(jnp.where(is_later, got_decay, jnp.ones_like(got_decay)))
        else:
            before = before_ref[rows, :]
            before_decay = decay_row(before_ref, j, count, width)
            past_ref[rows, :] = jnp.where(is_later, got * before_decay + before, before)
            pasts.append(jnp.where(is_later, got_decay * before_decay, before_decay))
    put_decays(pay_ref, decays, count, width)
    if keep:
        put_decays(refs[0], decays, count, width)
    put_decays(past_ref, pasts, count, width)


def widen(place, got, window, before, count, width, bit, keep):
    shape = got.shape
    opening = before is None
    before = window if before is None else before
    done = pl.pallas_call(
        functools.partial(widen_kernel, count, width, bit, opening, keep),
        in_specs=[SMEM, VMEM, VMEM, VMEM],
        out_specs=[VMEM] * (2 + keep),
        out_shape=[held(shape, BF16), held(shape, F32)] + [held(shape, F32)] * keep,
        compiler_params=PARAMS,
        name="widen",
    )(place, near(got), near(window), near(before))
    return done if keep else (*done, None)


def enter_kernel(size, count, width, bit, opening, place_ref, got_ref, before_ref, *refs):
    past_refs, out_refs = refs[: size - 1], refs[size - 1 :]
    is_later = (place_ref[0] & bit) != 0
    for j in range(count):
        rows = slice(j * width, (j + 1) * width)
        before = jnp.zeros((width, width), F32)
        if bit:
            got = got_ref[rows, :].astype(F32)
            if not opening:
                before = before_ref[rows, :]
                got = got * decay_row(before_ref, j, count, width) + before
            before = jnp.where(is_later, got, before)
        entering = [before] + [
            before * decay_row(ref, j, count, width) + ref[rows, :] for ref in past_refs
        ]
        for away in range(size):
            index = part_of(place_ref, size, away)
            out_refs[away][rows, :] = picked(entering, index).astype(BF16)


def enter(place, got, before, past, size, count, width, bit):
    opening = before is None
    got = past[0] if got is None else got
    before = past[0] if opening else before
    return pl.pallas_call(
        functools.partial(enter_kernel, size, count, width, bit, opening),
        in_specs=[SMEM] + [VMEM] * (size + 1),
        out_specs=[VMEM] * size,
        out_shape=[held((count * width, width), BF16)] * size,
        compiler_params=PARAMS,
        name="enter",
    )(place, near(got), near(before), *map(near, past))


def local_kernel(size, count, width, away, place_ref, cum_ref, q_ref, k_ref, v_ref, out_ref, decayed_ref):
    part = part_of(place_ref, size, away)
    sums = [cum_ref[pl.ds(part * count + j, 1), :] for j in range(count)]
    rows = cum_ref.shape[1]
    tile = tile_of(rows, 2 * width)
    causal = lax.broadcasted_iota(jnp.int32, (tile, tile), 0) >= lax.broadcasted_iota(
        jnp.int32, (tile, tile), 1
    )

    def downward(row):
        turned = jnp.broadcast_to(row, (width, tile)).T
        return jnp.concatenate([turned] * (tile // width), axis=1)

    def columns(j):
        return pl.ds(pl.multiple_of((part * count + j) * width, width), width)

    def scores(j, i):
        return lax.dot_general(
            q_ref[i * tile : (i + 1) * tile, columns(j)],
            k_ref[: (i + 1) * tile, columns(j)],
            (((1,), (1,)), ((), ())),
            preferred_element_type=F32,
        )

    def weighted(j, i, found):
        cum = sums[j]
        here = slice(i * tile, (i + 1) * tile)
        across = cum[:, here]
        down = downward(across)
        weight = jnp.exp(jnp.where(causal, down - across, -jnp.inf))
        near_part = (found[:, i * tile :] * weight).astype(BF16)
        if i == 0:
            return near_part, None, None, jnp.exp(down)
        edge = cum[:, i * tile - 1 : i * tile]
        since = jnp.exp(down - edge)
        far_part = (found[:, : i * tile] * jnp.exp(edge - cum[:, : i * tile])).astype(BF16)
        return near_part, far_part, since, since * jnp.exp(edge)

    def finish(j, i, near_part, far_part, since, decay):
        cols = slice(j * width, (j + 1) * width)
        from_cols = columns(j)
        here = slice(i * tile, (i + 1) * tile)
        out = jnp.dot(near_part, v_ref[here, from_cols], preferred_element_type=F32)
        if far_part is not None:
            out = out + since[:, :width] * jnp.dot(
                far_part, v_ref[: i * tile, from_cols], preferred_element_type=F32
            )
        out_ref[here, cols] = out
        decayed_ref[here, cols] = (
            q_ref[here, columns(j)].astype(F32) * decay[:, :width]
        ).astype(BF16)

    units = [(j, i) for i in range(rows // tile) for j in range(count)]
    found, held_parts = {}, {}
    for step in range(len(units) + 3):
        if step < len(units):
            found[step] = scores(*units[step])
        if 0 <= step - 2 < len(units):
            held_parts[step - 2] = weighted(*units[step - 2], found.pop(step - 2))
        if 0 <= step - 3:
            finish(*units[step - 3], *held_parts.pop(step - 3))


def local(place, cum, query, key, value, size, count, width, away):
    rows = cum.shape[1]
    cols = count * width
    return pl.pallas_call(
        functools.partial(local_kernel, size, count, width, away),
        in_specs=[SMEM] + [VMEM] * 4,
        out_specs=[VMEM, VMEM],
        out_shape=[held((rows, cols), F32), held((rows, cols), BF16)],
        compiler_params=PARAMS,
        name="local",
    )(place, near(cum), near(query), near(key), near(value))


def norm_kernel(size, count, width, chips, block, away, group, place_ref, chip_ref, core_ref, gain_ref, *refs):
    members = len(group)
    inside_refs, query_refs = refs[:members], refs[members : 2 * members]
    state_refs, out_ref = refs[2 * members : -1], refs[-1]
    ones = jnp.full((width, width), 1.0 / width, F32).astype(BF16)
    units = [(at, j) for at in range(members) for j in range(count)]

    def rows_of(ref, j):
        src = slice(j * width, (j + 1) * width)
        found = []
        for i in range(chips):
            spot = 2 * lax.rem(chip_ref[0] + i, chips)
            spot = spot + (1 - core_ref[0] if away else core_ref[0])
            found.append(ref[pl.ds(pl.multiple_of(spot * block, block), block), src])
        return jnp.concatenate(found, axis=0)

    def carry(at, j):
        state = state_refs[at][j * width : (j + 1) * width, :]
        return jnp.dot(rows_of(query_refs[at], j), state, preferred_element_type=F32)

    def square(at, j, carried):
        attended = rows_of(inside_refs[at], j) + carried
        return attended, jnp.dot(
            (attended * attended).astype(BF16), ones, preferred_element_type=F32
        )

    def finish_head(at, j, attended, mean):
        gain = gain_ref[pl.ds(part_of(place_ref, size, group[at]) * count + j, 1), :]
        col = (at * count + j) * width
        out_ref[:, col : col + width] = (
            attended * lax.rsqrt(mean + 1e-06) * gain
        ).astype(out_ref.dtype)

    first, second = {}, {}
    for step in range(len(units) + 2):
        if step < len(units):
            first[step] = carry(*units[step])
        if 0 <= step - 1 < len(units):
            second[step - 1] = square(*units[step - 1], first.pop(step - 1))
        if 0 <= step - 2:
            finish_head(*units[step - 2], *second.pop(step - 2))


def norm(group, scalars, gain, insides, queries, entering, size, count, width, chips, block, away):
    cols = len(group) * count * width
    parts = [a[i] for a in (insides, queries, entering) for i in group]
    return pl.pallas_call(
        functools.partial(norm_kernel, size, count, width, chips, block, away, group),
        in_specs=[SMEM] * 3 + [VMEM] * (1 + len(parts)),
        out_specs=VMEM,
        out_shape=held((chips * block, cols), BF16),
        compiler_params=PARAMS,
        name="norm_away" if away else "norm_home",
    )(*scalars, gain, *map(near, parts))


def summed(size, place_ref, terms, span, total=None):
    for ref, at, away, weight_ref in terms:
        cols = weight_ref.shape[0] // size
        rows = part_columns(place_ref, size, away, cols)
        part = jnp.dot(
            ref[:, at * cols : (at + 1) * cols], weight_ref[rows, span], preferred_element_type=F32
        )
        total = part if total is None else total + part
    return total


def begin_kernel(size, place_ref, one_ref, two_ref, met_ref, near_ref, far_ref, out_ref):
    *early, last = order_of(size)
    terms = [(one_ref, at, away, near_ref) for at, away in enumerate(early)]
    terms += [(met_ref, at, away, far_ref) for at, away in enumerate(early)]
    terms += [(two_ref, 0, last, near_ref)]
    out_ref[...] = summed(size, place_ref, terms, slice(0, out_ref.shape[1]))


def begin(place, home, met, first_weight, second_weight, count, size):
    rows = met.shape[0]
    return pl.pallas_call(
        functools.partial(begin_kernel, size),
        in_specs=[SMEM] + [VMEM] * 5,
        out_specs=VMEM,
        out_shape=held((rows, count), F32),
        compiler_params=PARAMS,
        name="begin",
    )(place, *map(near, [*home, met, first_weight, second_weight]))


def complete_kernel(block, size, place_ref, begun_ref, two_ref, far_ref, own_ref, away_ref):
    span = slice(0, own_ref.shape[1])
    total = summed(size, place_ref, [(two_ref, 0, order_of(size)[-1], far_ref)], span, begun_ref[...])
    own_ref[...] = total[:block]
    away_ref[...] = total[block:].astype(away_ref.dtype)


def complete(place, begun, two, second_weight, block, size):
    rows, count = begun.shape
    return pl.pallas_call(
        functools.partial(complete_kernel, block, size),
        in_specs=[SMEM] + [VMEM] * 3,
        out_specs=[VMEM, VMEM],
        out_shape=[held((block, count), F32), held((rows - block, count), BF16)],
        compiler_params=PARAMS,
        name="complete",
    )(place, near(begun), near(two), near(second_weight))


def project_kernel(block, first, tile, size, place_ref, *refs):
    own_ref, away_ref = refs[-2:]
    terms = []
    for one_ref, two_ref, weight_ref in ((refs[0], refs[1], refs[4]), (refs[2], refs[3], refs[5])):
        *early, last = order_of(size)
        terms += [(one_ref, at, away, weight_ref) for at, away in enumerate(early)]
        terms += [(two_ref, 0, last, weight_ref)]
    for i in range(own_ref.shape[1] // tile):
        here = slice(i * tile, (i + 1) * tile)
        span = slice(first + i * tile, first + (i + 1) * tile)
        total = summed(size, place_ref, terms, span)
        own_ref[:, here] = total[:block]
        away_ref[:, here] = total[block:].astype(away_ref.dtype)


def project(place, home, other, first_weight, second_weight, hold, block, first, count, tile, size):
    rows = home[0].shape[0]
    tile = tile_of(count, tile)
    return pl.pallas_call(
        functools.partial(project_kernel, block, first, tile, size),
        in_specs=[SMEM] + [VMEM] * 6 + [ANY],
        out_specs=[VMEM, VMEM],
        out_shape=[held((block, count), F32), held((rows - block, count), BF16)],
        compiler_params=PARAMS,
        name="project",
    )(place, *map(near, [*home, *other, first_weight, second_weight]), hold)


def finish_kernel(first, pieces, own_ref, residual_ref, *refs):
    part_refs, (out_ref, total_ref, sems) = refs[:pieces], refs[-3:]
    count = own_ref.shape[1]
    total = own_ref[...] + residual_ref[:, first : first + count].astype(F32)
    for ref in part_refs:
        total = total + ref[...].astype(F32)
    total_ref[...] = total.astype(BF16)
    rows = total_ref.shape[0] // sems.shape[0]
    copies = []
    for i in range(sems.shape[0]):
        here = pl.ds(i * rows, rows)
        copies.append(
            pltpu.make_async_copy(
                total_ref.at[here, :], out_ref.at[here, pl.ds(first, count)], sems.at[i]
            )
        )
    for copy in copies:
        copy.start()
    for copy in copies:
        copy.wait()


def finish(out, own, residual, parts, first):
    block, total = residual.shape
    earlier = [] if out is None else [outside(out)]
    return pl.pallas_call(
        functools.partial(finish_kernel, first, len(parts)),
        in_specs=[VMEM] * (2 + len(parts)) + [ANY] * len(earlier),
        out_specs=ANY,
        out_shape=pltpu.HBM((block, total), BF16),
        scratch_shapes=[
            pltpu.VMEM((block, own.shape[1]), BF16),
            pltpu.SemaphoreType.DMA((tile_of(block // 16, 4),)),
        ],
        input_output_aliases={2 + len(parts): 0} if earlier else {},
        compiler_params=PARAMS,
        name="finish",
    )(near(own), near(residual), *map(near, parts), *earlier)


def shards(blocks, group, q_spikes, k_spikes, v_spikes, log_decay, norm_gain, out_weight, residual):
    rows, heads = log_decay.shape
    width = q_spikes.shape[1] // heads
    size = 4 if heads % 4 == 0 and blocks % 4 == 0 else 2
    count = heads // size
    chips = group // 2
    block = rows // group
    place = lax.axis_index("ctx").astype(jnp.int32)
    member = lax.axis_index("exp").astype(jnp.int32)
    place, chip, core = lax.optimization_barrier(
        tuple(a.reshape(1) for a in (place, member >> 1, member & 1))
    )
    cores = [(i, i ^ 1) for i in range(group)]

    def swap(x, bit):
        return lax.ppermute(x, "ctx", [(i, i ^ bit) for i in range(blocks)])

    logd = log_decay.T
    if heads % 8:
        logd = jnp.pad(logd, ((0, pad_rows(heads) - heads), (0, 0)))
    sent, key, value = early_states(place, logd, k_spikes, v_spikes, size, count, width)
    met = [swap(a, i + 1) for i, a in enumerate(sent)]
    kept, query, cum = load(place, logd, key, value, q_spikes, sent[0], size, count, width)
    kept, weight = lax.optimization_barrier((kept, out_weight))
    far_weight = lax.ppermute(outside(weight), "exp", cores)
    total = out_weight.shape[1]
    tile = tile_of(total, 512)

    pay, past, window = gather(place, kept, met, size, count, width, int(2 * size < blocks))
    _, own_weight = lax.optimization_barrier((pay, out_weight))
    before, got, level, bit = None, None, 0, size
    while bit < blocks:
        got = swap(pay, bit)
        if 2 * bit < blocks:
            pay, before, window = widen(
                place, got, window, before, count, width, bit, int(4 * bit < blocks)
            )
        bit, level = 2 * bit, level + 1
    own, *theirs = enter(place, got, before, past, size, count, width, bit // 2 if level else 0)
    entering = [own] + [swap(a, i + 1) for i, a in enumerate(theirs)]

    insides, queries = [], []
    for away in range(size):
        inside, decayed = local(place, cum, query, key, value, size, count, width, away)
        insides.append(inside)
        queries.append(decayed)

    gain = norm_gain.reshape(heads, width)
    home, other = [], []
    for which in (order_of(size)[:-1], order_of(size)[-1:]):
        args = (
            tuple(which), (place, chip, core), gain, insides, queries, entering,
            size, count, width, chips, block,
        )
        away = norm(*args, True)
        other.append(lax.ppermute(away, "exp", cores))
        home.append(norm(*args, False))

    sizes = [tile, tile]
    while total - sum(sizes) > 2 * tile:
        sizes.append(2 * tile)
    rest = total - sum(sizes)
    sizes += [rest - tile // 2, tile // 2] if rest > tile // 2 else [rest]
    begun = begin(place, home, other[0], own_weight, far_weight, sizes[0], size)
    out, at, hold = None, 0, None
    sums = []
    for index, span in enumerate(sizes):
        if index:
            own, pieces = project(
                place, home, other, own_weight, far_weight, hold, block, at, span, tile, size
            )
        else:
            own, pieces = complete(place, begun, other[1], far_weight, block, size)
        hold = pieces
        got = []
        for d in range(1, chips):
            piece = pieces[(d - 1) * block : d * block]
            perm = [(i, 2 * ((i // 2 + d) % chips) + i % 2) for i in range(group)]
            got.append(lax.ppermute(piece, "exp", perm))
        sums.append((own, got, at))
        at += span
    for own, got, at in sums:
        out = finish(out, own, residual, got, at)
    return out


def solution(mesh):
    in_specs = (
        P("ctx", "exp"),
        P("ctx", "exp"),
        P("ctx", "exp"),
        P("ctx", "exp"),
        P("exp"),
        P("exp", None),
        P(("ctx", "exp"), None),
    )
    out_specs = P(("ctx", "exp"), None)

    def body(*args):
        return shards(mesh.shape["ctx"], mesh.shape["exp"], *args)

    return jax.shard_map(
        body, mesh=mesh, in_specs=in_specs, out_specs=out_specs, check_vma=False
    )
```

```python
import functools

import jax
import jax.numpy as jnp
from jax import lax
from jax.experimental import pallas as pl
from jax.experimental.pallas import tpu as pltpu
from jax.sharding import PartitionSpec as P


F32 = jnp.float32
BF16 = jnp.bfloat16
PARAMS = pltpu.CompilerParams(vmem_limit_bytes=16 << 20)
PACKED = pltpu.CompilerParams(vmem_limit_bytes=16 << 20)
VMEM = pl.BlockSpec(memory_space=pltpu.VMEM)
SMEM = pl.BlockSpec(memory_space=pltpu.SMEM)
ANY = pl.BlockSpec(memory_space=pl.ANY)


def held(shape, kind):
    return pltpu.VMEM(shape, kind)


def near(x):
    return pltpu.with_memory_space_constraint(x, pltpu.VMEM)


def outside(x):
    return pltpu.with_memory_space_constraint(x, pltpu.HBM)


def tile_of(size, want):
    while size % want:
        want //= 2
    return want


def pad_rows(count):
    return -(-count // 8) * 8


def running_sum(logd):
    heads, rows = logd.shape
    tile = tile_of(rows, 128)
    count = rows // tile
    tiles = jnp.concatenate([logd[:, i * tile : (i + 1) * tile] for i in range(count)], axis=0)
    one = tiles.astype(BF16).astype(F32)
    two = (tiles - one).astype(BF16).astype(F32)
    three = tiles - one - two
    parts = jnp.concatenate([one, two, three], axis=0).astype(BF16)
    upper = (
        lax.broadcasted_iota(jnp.int32, (tile, tile), 0)
        <= lax.broadcasted_iota(jnp.int32, (tile, tile), 1)
    ).astype(F32)
    sums = jnp.dot(parts, upper.astype(BF16), preferred_element_type=F32)
    size = count * heads
    sums = sums[:size] + sums[size : 2 * size] + sums[2 * size :]
    done, carry = [], None
    for i in range(count):
        part = sums[i * heads : (i + 1) * heads]
        if carry is not None:
            part = part + carry
        carry = part[:, tile - 1 : tile]
        done.append(part)
    return jnp.concatenate(done, axis=1)


def copies_of(source, target, sems, first=0):
    count = sems.shape[0]
    size = target.shape[0] // count
    return [
        pltpu.make_async_copy(
            source.at[pl.ds(i * size, size), pl.ds(first, target.shape[1])],
            target.at[pl.ds(i * size, size), :],
            sems.at[i],
        )
        for i in range(count)
    ]


def pay_shape(count, width, kind):
    return held((count * width + 2 * pad_rows(count), width), kind)


def order_of(size):
    return [0, *range(size - 1, 0, -1)]


def part_of(place_ref, size, away):
    return (place_ref[0] & (size - 1)) ^ away


def turned_keys(part, count, width, key, weight_ref):
    turned = [key[:, j * width : (j + 1) * width].T for j in range(count)]
    return [
        turned[j] * weight_ref[pl.ds(part * count + j, 1), :].astype(BF16) for j in range(count)
    ]


def put_states(part, count, width, keyed, value, cum_ref, pay_ref):
    rows = cum_ref.shape[1]
    decays = []
    for j in range(count):
        state = jnp.dot(
            keyed[j], value[:, j * width : (j + 1) * width], preferred_element_type=F32
        )
        pay_ref[j * width : (j + 1) * width, :] = state.astype(pay_ref.dtype)
        total = cum_ref[pl.ds(part * count + j, 1), :][:, rows - 1 : rows]
        decays.append(jnp.broadcast_to(jnp.exp(total), (1, width)))
    put_decays(pay_ref, decays, count, width)


def put_sums(logd_ref, cum_ref, weight_ref):
    cum = running_sum(logd_ref[...])
    cum_ref[...] = cum
    weight_ref[...] = jnp.exp(cum[:, cum.shape[1] - 1 :] - cum)


def part_columns(place_ref, size, away, cols):
    return pl.ds(pl.multiple_of(part_of(place_ref, size, away) * cols, cols), cols)


def early_kernel(size, count, width, place_ref, logd_in, key_in, value_in, *refs):
    pay_refs = refs[: size - 1]
    key_ref, value_ref, logd_ref, cum_ref, weight_ref, logd_sem, sems = refs[size - 1 :]
    logd = pltpu.make_async_copy(logd_in, logd_ref, logd_sem)
    keys, values = copies_of(key_in, key_ref, sems.at[0]), copies_of(value_in, value_ref, sems.at[1])
    for copy in (logd, *keys, *values):
        copy.start()
    logd.wait()
    put_sums(logd_ref, cum_ref, weight_ref)
    for copy in keys + values:
        copy.wait()
    for away in range(1, size):
        part = part_of(place_ref, size, away)
        here = part_columns(place_ref, size, away, count * width)
        turned = turned_keys(part, count, width, key_ref[:, here], weight_ref)
        put_states(part, count, width, turned, value_ref[:, here], cum_ref, pay_refs[away - 1])


def early_states(place, logd, key, value, size, count, width):
    heads, rows = logd.shape
    *pays, key, value = pl.pallas_call(
        functools.partial(early_kernel, size, count, width),
        in_specs=[SMEM] + [ANY] * 3,
        out_specs=[VMEM] * (size + 1),
        out_shape=[pay_shape(count, width, BF16)] * (size - 1) + [held(key.shape, BF16)] * 2,
        scratch_shapes=[pltpu.VMEM((heads, rows), F32)] * 3
        + [pltpu.SemaphoreType.DMA, pltpu.SemaphoreType.DMA((2, 2))],
        compiler_params=PACKED,
        name="early_states",
    )(place, outside(logd), outside(key), outside(value))
    return pays, key, value


def load_kernel(size, count, width, place_ref, logd_in, query_in, weight_in, key_ref, value_ref, hold_ref, *refs):
    pay_ref, query_ref, cum_ref, head_ref, logd_ref, weight_ref, logd_sem, sems, head_sems = refs
    logd = pltpu.make_async_copy(logd_in, logd_ref, logd_sem)
    logd.start()
    copies = copies_of(query_in, query_ref, sems) + copies_of(weight_in, head_ref, head_sems)
    for copy in copies:
        copy.start()
    logd.wait()
    put_sums(logd_ref, cum_ref, weight_ref)
    here = part_columns(place_ref, size, 0, count * width)
    part = part_of(place_ref, size, 0)
    keyed = turned_keys(part, count, width, key_ref[:, here], weight_ref)
    put_states(part, count, width, keyed, value_ref[:, here], cum_ref, pay_ref)
    for copy in copies:
        copy.wait()


def load(place, logd, key, value, query, weight, columns, hold, size, count, width):
    heads, rows = logd.shape
    return pl.pallas_call(
        functools.partial(load_kernel, size, count, width),
        in_specs=[SMEM, ANY, ANY, ANY, VMEM, VMEM, ANY],
        out_specs=[VMEM] * 4,
        out_shape=[
            pay_shape(count, width, F32),
            held(query.shape, BF16),
            held((heads, rows), F32),
            held((weight.shape[0], columns), BF16),
        ],
        scratch_shapes=[pltpu.VMEM((heads, rows), F32)] * 2
        + [
            pltpu.SemaphoreType.DMA,
            pltpu.SemaphoreType.DMA((2,)),
            pltpu.SemaphoreType.DMA((8,)),
        ],
        compiler_params=PACKED,
        name="load",
    )(place, outside(logd), outside(query), outside(weight), near(key), near(value), hold)


def decay_row(pay, j, count, width):
    at = count * width + j
    pad = pad_rows(count)
    return pay[at : at + 1, :].astype(F32) + pay[at + pad : at + pad + 1, :].astype(F32)


def put_decays(ref, rows, count, width):
    pad = pad_rows(count)
    blank = [jnp.zeros((1, width), F32)] * (pad - count)
    if ref.dtype == BF16:
        highs = [row.astype(BF16).astype(F32) for row in rows]
        lows = [row - high for row, high in zip(rows, highs)]
    else:
        highs, lows = rows, [jnp.zeros_like(row) for row in rows]
    tail = jnp.concatenate(highs + blank + lows + blank, axis=0)
    ref[count * width :, :] = tail.astype(ref.dtype)


def picked(values, index):
    found = values[0]
    for i in range(1, len(values)):
        found = jnp.where(index == i, values[i], found)
    return found


def gather_kernel(size, count, width, place_ref, *refs):
    in_refs, pay_ref, past_refs = refs[:size], refs[size], refs[size + 1 : 2 * size]
    window_refs = refs[2 * size :]
    decays = [[] for _ in range(size)]
    for j in range(count):
        rows = slice(j * width, (j + 1) * width)
        found = [ref[rows, :].astype(F32) for ref in in_refs]
        found_decays = [decay_row(ref, j, count, width) for ref in in_refs]
        total, total_decay = None, None
        for b in range(size):
            index = part_of(place_ref, size, b)
            state, decay = picked(found, index), picked(found_decays, index)
            if b:
                past_refs[b - 1][rows, :] = total
                decays[b - 1].append(total_decay)
                total, total_decay = total * decay + state, total_decay * decay
            else:
                total, total_decay = state, decay
        for ref in (pay_ref, *window_refs):
            ref[rows, :] = total.astype(ref.dtype)
        decays[-1].append(total_decay)
    for ref, rows in zip(past_refs, decays):
        put_decays(ref, rows, count, width)
    for ref in (pay_ref, *window_refs):
        put_decays(ref, decays[-1], count, width)


def gather(place, own, met, size, count, width, keep):
    shape = own.shape
    pay, *past = pl.pallas_call(
        functools.partial(gather_kernel, size, count, width),
        in_specs=[SMEM] + [VMEM] * size,
        out_specs=[VMEM] * (size + keep),
        out_shape=[held(shape, BF16)] + [held(shape, F32)] * (size - 1 + keep),
        compiler_params=PARAMS,
        name="gather",
    )(place, near(own), *map(near, met))
    return pay, past[: size - 1], past[-1]


def widen_kernel(count, width, bit, opening, keep, place_ref, got_ref, window_ref, before_ref, pay_ref, past_ref, *refs):
    is_later = (place_ref[0] & bit) != 0
    decays, pasts = [], []
    for j in range(count):
        rows = slice(j * width, (j + 1) * width)
        got, window = got_ref[rows, :].astype(F32), window_ref[rows, :]
        got_decay = decay_row(got_ref, j, count, width)
        window_decay = decay_row(window_ref, j, count, width)
        wide = jnp.where(is_later, got, window) * jnp.where(
            is_later, window_decay, got_decay
        ) + jnp.where(is_later, window, got)
        pay_ref[rows, :] = wide.astype(pay_ref.dtype)
        if keep:
            refs[0][rows, :] = wide
        decays.append(got_decay * window_decay)
        if opening:
            past_ref[rows, :] = jnp.where(is_later, got, jnp.zeros_like(got))
            pasts.append(jnp.where(is_later, got_decay, jnp.ones_like(got_decay)))
        else:
            before = before_ref[rows, :]
            before_decay = decay_row(before_ref, j, count, width)
            past_ref[rows, :] = jnp.where(is_later, got * before_decay + before, before)
            pasts.append(jnp.where(is_later, got_decay * before_decay, before_decay))
    put_decays(pay_ref, decays, count, width)
    if keep:
        put_decays(refs[0], decays, count, width)
    put_decays(past_ref, pasts, count, width)


def widen(place, got, window, before, count, width, bit, keep):
    shape = got.shape
    opening = before is None
    before = window if before is None else before
    done = pl.pallas_call(
        functools.partial(widen_kernel, count, width, bit, opening, keep),
        in_specs=[SMEM, VMEM, VMEM, VMEM],
        out_specs=[VMEM] * (2 + keep),
        out_shape=[held(shape, BF16), held(shape, F32)] + [held(shape, F32)] * keep,
        compiler_params=PARAMS,
        name="widen",
    )(place, near(got), near(window), near(before))
    return done if keep else (*done, None)


def enter_kernel(size, count, width, bit, opening, place_ref, got_ref, before_ref, *refs):
    past_refs, out_refs = refs[: size - 1], refs[size - 1 :]
    is_later = (place_ref[0] & bit) != 0
    for j in range(count):
        rows = slice(j * width, (j + 1) * width)
        before = jnp.zeros((width, width), F32)
        if bit:
            got = got_ref[rows, :].astype(F32)
            if not opening:
                before = before_ref[rows, :]
                got = got * decay_row(before_ref, j, count, width) + before
            before = jnp.where(is_later, got, before)
        entering = [before] + [
            before * decay_row(ref, j, count, width) + ref[rows, :] for ref in past_refs
        ]
        for away in range(size):
            index = part_of(place_ref, size, away)
            out_refs[away][rows, :] = picked(entering, index).astype(BF16)


def enter(place, got, before, past, size, count, width, bit):
    opening = before is None
    got = past[0] if got is None else got
    before = past[0] if opening else before
    return pl.pallas_call(
        functools.partial(enter_kernel, size, count, width, bit, opening),
        in_specs=[SMEM] + [VMEM] * (size + 1),
        out_specs=[VMEM] * size,
        out_shape=[held((count * width, width), BF16)] * size,
        compiler_params=PARAMS,
        name="enter",
    )(place, near(got), near(before), *map(near, past))


def local_kernel(size, count, width, away, place_ref, cum_ref, q_ref, k_ref, v_ref, out_ref, decayed_ref):
    part = part_of(place_ref, size, away)
    sums = [cum_ref[pl.ds(part * count + j, 1), :] for j in range(count)]
    rows = cum_ref.shape[1]
    tile = tile_of(rows, 2 * width)
    causal = lax.broadcasted_iota(jnp.int32, (tile, tile), 0) >= lax.broadcasted_iota(
        jnp.int32, (tile, tile), 1
    )

    def downward(row):
        turned = jnp.broadcast_to(row, (width, tile)).T
        return jnp.concatenate([turned] * (tile // width), axis=1)

    def columns(j):
        return pl.ds(pl.multiple_of((part * count + j) * width, width), width)

    def scores(j, i):
        return lax.dot_general(
            q_ref[i * tile : (i + 1) * tile, columns(j)],
            k_ref[: (i + 1) * tile, columns(j)],
            (((1,), (1,)), ((), ())),
            preferred_element_type=F32,
        )

    def weighted(j, i, found):
        cum = sums[j]
        here = slice(i * tile, (i + 1) * tile)
        across = cum[:, here]
        down = downward(across)
        weight = jnp.exp(jnp.where(causal, down - across, -jnp.inf))
        near_part = (found[:, i * tile :] * weight).astype(BF16)
        if i == 0:
            return near_part, None, None, jnp.exp(down)
        edge = cum[:, i * tile - 1 : i * tile]
        since = jnp.exp(down - edge)
        far_part = (found[:, : i * tile] * jnp.exp(edge - cum[:, : i * tile])).astype(BF16)
        return near_part, far_part, since, since * jnp.exp(edge)

    def finish(j, i, near_part, far_part, since, decay):
        cols = slice(j * width, (j + 1) * width)
        from_cols = columns(j)
        here = slice(i * tile, (i + 1) * tile)
        out = jnp.dot(near_part, v_ref[here, from_cols], preferred_element_type=F32)
        if far_part is not None:
            out = out + since[:, :width] * jnp.dot(
                far_part, v_ref[: i * tile, from_cols], preferred_element_type=F32
            )
        out_ref[here, cols] = out
        decayed_ref[here, cols] = (
            q_ref[here, columns(j)].astype(F32) * decay[:, :width]
        ).astype(BF16)

    units = [(j, i) for i in range(rows // tile) for j in range(count)]
    found, held_parts = {}, {}
    for step in range(len(units) + 3):
        if step < len(units):
            found[step] = scores(*units[step])
        if 0 <= step - 2 < len(units):
            held_parts[step - 2] = weighted(*units[step - 2], found.pop(step - 2))
        if 0 <= step - 3:
            finish(*units[step - 3], *held_parts.pop(step - 3))


def local(place, cum, query, key, value, size, count, width, away):
    rows = cum.shape[1]
    cols = count * width
    return pl.pallas_call(
        functools.partial(local_kernel, size, count, width, away),
        in_specs=[SMEM] + [VMEM] * 4,
        out_specs=[VMEM, VMEM],
        out_shape=[held((rows, cols), F32), held((rows, cols), BF16)],
        compiler_params=PARAMS,
        name="local",
    )(place, near(cum), near(query), near(key), near(value))


def norm_kernel(size, count, width, chips, block, away, group, place_ref, chip_ref, core_ref, gain_ref, *refs):
    members = len(group)
    inside_refs, query_refs = refs[:members], refs[members : 2 * members]
    state_refs, out_ref = refs[2 * members : -1], refs[-1]
    ones = jnp.full((width, width), 1.0 / width, F32).astype(BF16)
    units = [(at, j) for at in range(members) for j in range(count)]

    def rows_of(ref, j):
        src = slice(j * width, (j + 1) * width)
        found = []
        for i in range(chips):
            spot = 2 * lax.rem(chip_ref[0] + i, chips)
            spot = spot + (1 - core_ref[0] if away else core_ref[0])
            found.append(ref[pl.ds(pl.multiple_of(spot * block, block), block), src])
        return jnp.concatenate(found, axis=0)

    def carry(at, j):
        state = state_refs[at][j * width : (j + 1) * width, :]
        return jnp.dot(rows_of(query_refs[at], j), state, preferred_element_type=F32)

    def square(at, j, carried):
        attended = rows_of(inside_refs[at], j) + carried
        return attended, jnp.dot(
            (attended * attended).astype(BF16), ones, preferred_element_type=F32
        )

    def finish_head(at, j, attended, mean):
        gain = gain_ref[pl.ds(part_of(place_ref, size, group[at]) * count + j, 1), :]
        col = (at * count + j) * width
        out_ref[:, col : col + width] = (
            attended * lax.rsqrt(mean + 1e-06) * gain
        ).astype(out_ref.dtype)

    first, second = {}, {}
    for step in range(len(units) + 2):
        if step < len(units):
            first[step] = carry(*units[step])
        if 0 <= step - 1 < len(units):
            second[step - 1] = square(*units[step - 1], first.pop(step - 1))
        if 0 <= step - 2:
            finish_head(*units[step - 2], *second.pop(step - 2))


def norm(group, scalars, gain, insides, queries, entering, size, count, width, chips, block, away):
    cols = len(group) * count * width
    parts = [a[i] for a in (insides, queries, entering) for i in group]
    return pl.pallas_call(
        functools.partial(norm_kernel, size, count, width, chips, block, away, group),
        in_specs=[SMEM] * 3 + [VMEM] * (1 + len(parts)),
        out_specs=VMEM,
        out_shape=held((chips * block, cols), BF16),
        compiler_params=PARAMS,
        name="norm_away" if away else "norm_home",
    )(*scalars, gain, *map(near, parts))


def summed(size, place_ref, terms, span, total=None):
    for ref, at, away, weight_ref in terms:
        cols = weight_ref.shape[0] // size
        rows = part_columns(place_ref, size, away, cols)
        part = jnp.dot(
            ref[:, at * cols : (at + 1) * cols], weight_ref[rows, span], preferred_element_type=F32
        )
        total = part if total is None else total + part
    return total


def begin_kernel(size, place_ref, one_ref, two_ref, met_ref, near_ref, far_ref, out_ref):
    *early, last = order_of(size)
    terms = [(one_ref, at, away, near_ref) for at, away in enumerate(early)]
    terms += [(met_ref, at, away, far_ref) for at, away in enumerate(early)]
    terms += [(two_ref, 0, last, near_ref)]
    out_ref[...] = summed(size, place_ref, terms, slice(0, out_ref.shape[1]))


def begin(place, home, met, first_weight, second_weight, count, size):
    rows = met.shape[0]
    return pl.pallas_call(
        functools.partial(begin_kernel, size),
        in_specs=[SMEM] + [VMEM] * 5,
        out_specs=VMEM,
        out_shape=held((rows, count), F32),
        compiler_params=PARAMS,
        name="begin",
    )(place, *map(near, [*home, met, first_weight, second_weight]))


def complete_kernel(block, size, place_ref, begun_ref, two_ref, far_ref, own_ref, away_ref):
    span = slice(0, own_ref.shape[1])
    total = summed(size, place_ref, [(two_ref, 0, order_of(size)[-1], far_ref)], span, begun_ref[...])
    own_ref[...] = total[:block]
    away_ref[...] = total[block:].astype(away_ref.dtype)


def complete(place, begun, two, second_weight, block, size):
    rows, count = begun.shape
    return pl.pallas_call(
        functools.partial(complete_kernel, block, size),
        in_specs=[SMEM] + [VMEM] * 3,
        out_specs=[VMEM, VMEM],
        out_shape=[held((block, count), F32), held((rows - block, count), BF16)],
        compiler_params=PARAMS,
        name="complete",
    )(place, near(begun), near(two), near(second_weight))


def project_kernel(block, first, tile, size, place_ref, *refs):
    own_ref, away_ref = refs[-2:]
    terms = []
    for one_ref, two_ref, weight_ref in ((refs[0], refs[1], refs[4]), (refs[2], refs[3], refs[5])):
        *early, last = order_of(size)
        terms += [(one_ref, at, away, weight_ref) for at, away in enumerate(early)]
        terms += [(two_ref, 0, last, weight_ref)]
    for i in range(own_ref.shape[1] // tile):
        here = slice(i * tile, (i + 1) * tile)
        span = slice(first + i * tile, first + (i + 1) * tile)
        total = summed(size, place_ref, terms, span)
        own_ref[:, here] = total[:block]
        away_ref[:, here] = total[block:].astype(away_ref.dtype)


def project(place, home, other, first_weight, second_weight, hold, block, first, count, tile, size):
    rows = home[0].shape[0]
    tile = tile_of(count, tile)
    return pl.pallas_call(
        functools.partial(project_kernel, block, first, tile, size),
        in_specs=[SMEM] + [VMEM] * 6 + [ANY],
        out_specs=[VMEM, VMEM],
        out_shape=[held((block, count), F32), held((rows - block, count), BF16)],
        compiler_params=PARAMS,
        name="project",
    )(place, *map(near, [*home, *other, first_weight, second_weight]), hold)


def finish_kernel(first, pieces, own_ref, residual_ref, *refs):
    part_refs, (out_ref, total_ref, sems) = refs[:pieces], refs[-3:]
    count = own_ref.shape[1]
    total = own_ref[...] + residual_ref[:, first : first + count].astype(F32)
    for ref in part_refs:
        total = total + ref[...].astype(F32)
    total_ref[...] = total.astype(BF16)
    rows = total_ref.shape[0] // sems.shape[0]
    copies = []
    for i in range(sems.shape[0]):
        here = pl.ds(i * rows, rows)
        copies.append(
            pltpu.make_async_copy(
                total_ref.at[here, :], out_ref.at[here, pl.ds(first, count)], sems.at[i]
            )
        )
    for copy in copies:
        copy.start()
    for copy in copies:
        copy.wait()


def finish(out, own, residual, parts, first):
    block, total = residual.shape
    earlier = [] if out is None else [outside(out)]
    return pl.pallas_call(
        functools.partial(finish_kernel, first, len(parts)),
        in_specs=[VMEM] * (2 + len(parts)) + [ANY] * len(earlier),
        out_specs=ANY,
        out_shape=pltpu.HBM((block, total), BF16),
        scratch_shapes=[
            pltpu.VMEM((block, own.shape[1]), BF16),
            pltpu.SemaphoreType.DMA((tile_of(block // 16, 4),)),
        ],
        input_output_aliases={2 + len(parts): 0} if earlier else {},
        compiler_params=PARAMS,
        name="finish",
    )(near(own), near(residual), *map(near, parts), *earlier)


def shards(blocks, group, q_spikes, k_spikes, v_spikes, log_decay, norm_gain, out_weight, residual):
    rows, heads = log_decay.shape
    width = q_spikes.shape[1] // heads
    size = 4 if heads % 4 == 0 and blocks % 4 == 0 else 2
    count = heads // size
    chips = group // 2
    block = rows // group
    place = lax.axis_index("ctx").astype(jnp.int32)
    member = lax.axis_index("exp").astype(jnp.int32)
    place, chip, core = lax.optimization_barrier(
        tuple(a.reshape(1) for a in (place, member >> 1, member & 1))
    )
    cores = [(i, i ^ 1) for i in range(group)]

    def swap(x, bit):
        return lax.ppermute(x, "ctx", [(i, i ^ bit) for i in range(blocks)])

    logd = log_decay.T
    if heads % 8:
        logd = jnp.pad(logd, ((0, pad_rows(heads) - heads), (0, 0)))
    sent, key, value = early_states(place, logd, k_spikes, v_spikes, size, count, width)
    met = [swap(a, i + 1) for i, a in enumerate(sent)]
    total = out_weight.shape[1]
    tile = tile_of(total, 512)
    kept, query, cum, head_weight = load(
        place, logd, key, value, q_spikes, out_weight, tile, sent[0], size, count, width
    )
    kept, weight = lax.optimization_barrier((kept, out_weight))
    far_weight = lax.ppermute(outside(weight), "exp", cores)
    pay, past, window = gather(place, kept, met, size, count, width, int(2 * size < blocks))
    before, got, level, bit = None, None, 0, size
    while bit < blocks:
        got = swap(pay, bit)
        if 2 * bit < blocks:
            pay, before, window = widen(
                place, got, window, before, count, width, bit, int(4 * bit < blocks)
            )
        bit, level = 2 * bit, level + 1
    own, *theirs = enter(place, got, before, past, size, count, width, bit // 2 if level else 0)
    entering = [own] + [swap(a, i + 1) for i, a in enumerate(theirs)]

    _, own_weight = lax.optimization_barrier((own, out_weight))
    insides, queries = [], []
    for away in range(size):
        inside, decayed = local(place, cum, query, key, value, size, count, width, away)
        insides.append(inside)
        queries.append(decayed)

    gain = norm_gain.reshape(heads, width)
    home, other = [], []
    for which in (order_of(size)[:-1], order_of(size)[-1:]):
        args = (
            tuple(which), (place, chip, core), gain, insides, queries, entering,
            size, count, width, chips, block,
        )
        away = norm(*args, True)
        other.append(lax.ppermute(away, "exp", cores))
        home.append(norm(*args, False))

    sizes = [tile, tile]
    while total - sum(sizes) > 2 * tile:
        sizes.append(2 * tile)
    rest = total - sum(sizes)
    sizes += [rest - tile // 2, tile // 2] if rest > tile // 2 else [rest]
    begun = begin(place, home, other[0], head_weight, far_weight, sizes[0], size)
    out, at, hold = None, 0, None
    sums = []
    for index, span in enumerate(sizes):
        if index:
            own, pieces = project(
                place, home, other, own_weight, far_weight, hold, block, at, span, tile, size
            )
        else:
            own, pieces = complete(place, begun, other[1], far_weight, block, size)
        hold = pieces
        got = []
        for d in range(1, chips):
            piece = pieces[(d - 1) * block : d * block]
            perm = [(i, 2 * ((i // 2 + d) % chips) + i % 2) for i in range(group)]
            got.append(lax.ppermute(piece, "exp", perm))
        sums.append((own, got, at))
        at += span
    for own, got, at in sums:
        out = finish(out, own, residual, got, at)
    return out


def solution(mesh):
    in_specs = (
        P("ctx", "exp"),
        P("ctx", "exp"),
        P("ctx", "exp"),
        P("ctx", "exp"),
        P("exp"),
        P("exp", None),
        P(("ctx", "exp"), None),
    )
    out_specs = P(("ctx", "exp"), None)

    def body(*args):
        return shards(mesh.shape["ctx"], mesh.shape["exp"], *args)

    return jax.shard_map(
        body, mesh=mesh, in_specs=in_specs, out_specs=out_specs, check_vma=False
    )
```

```python
import functools

import jax
import jax.numpy as jnp
from jax import lax
from jax.experimental import pallas as pl
from jax.experimental.pallas import tpu as pltpu
from jax.sharding import PartitionSpec as P


F32 = jnp.float32
BF16 = jnp.bfloat16
PARAMS = pltpu.CompilerParams(vmem_limit_bytes=16 << 20)
PACKED = pltpu.CompilerParams(vmem_limit_bytes=16 << 20)
VMEM = pl.BlockSpec(memory_space=pltpu.VMEM)
SMEM = pl.BlockSpec(memory_space=pltpu.SMEM)
ANY = pl.BlockSpec(memory_space=pl.ANY)


def held(shape, kind):
    return pltpu.VMEM(shape, kind)


def near(x):
    return pltpu.with_memory_space_constraint(x, pltpu.VMEM)


def outside(x):
    return pltpu.with_memory_space_constraint(x, pltpu.HBM)


def tile_of(size, want):
    while size % want:
        want //= 2
    return want


def pad_rows(count):
    return -(-count // 8) * 8


def running_sum(logd):
    heads, rows = logd.shape
    tile = tile_of(rows, 128)
    count = rows // tile
    tiles = jnp.concatenate([logd[:, i * tile : (i + 1) * tile] for i in range(count)], axis=0)
    one = tiles.astype(BF16).astype(F32)
    two = (tiles - one).astype(BF16).astype(F32)
    three = tiles - one - two
    parts = jnp.concatenate([one, two, three], axis=0).astype(BF16)
    upper = (
        lax.broadcasted_iota(jnp.int32, (tile, tile), 0)
        <= lax.broadcasted_iota(jnp.int32, (tile, tile), 1)
    ).astype(F32)
    sums = jnp.dot(parts, upper.astype(BF16), preferred_element_type=F32)
    size = count * heads
    sums = sums[:size] + sums[size : 2 * size] + sums[2 * size :]
    done, carry = [], None
    for i in range(count):
        part = sums[i * heads : (i + 1) * heads]
        if carry is not None:
            part = part + carry
        carry = part[:, tile - 1 : tile]
        done.append(part)
    return jnp.concatenate(done, axis=1)


def copies_of(source, target, sems, first=0):
    count = sems.shape[0]
    size = target.shape[0] // count
    return [
        pltpu.make_async_copy(
            source.at[pl.ds(i * size, size), pl.ds(first, target.shape[1])],
            target.at[pl.ds(i * size, size), :],
            sems.at[i],
        )
        for i in range(count)
    ]


def pay_shape(count, width, kind):
    return held((count * width + 2 * pad_rows(count), width), kind)


def order_of(size):
    return [0, *range(size - 1, 0, -1)]


def part_of(place_ref, size, away):
    return (place_ref[0] & (size - 1)) ^ away


def turned_keys(part, count, width, key, weight_ref):
    turned = [key[:, j * width : (j + 1) * width].T for j in range(count)]
    return [
        turned[j] * weight_ref[pl.ds(part * count + j, 1), :].astype(BF16) for j in range(count)
    ]


def put_states(part, count, width, keyed, value, cum_ref, pay_ref):
    rows = cum_ref.shape[1]
    decays = []
    for j in range(count):
        state = jnp.dot(
            keyed[j], value[:, j * width : (j + 1) * width], preferred_element_type=F32
        )
        pay_ref[j * width : (j + 1) * width, :] = state.astype(pay_ref.dtype)
        total = cum_ref[pl.ds(part * count + j, 1), :][:, rows - 1 : rows]
        decays.append(jnp.broadcast_to(jnp.exp(total), (1, width)))
    put_decays(pay_ref, decays, count, width)


def put_sums(logd_ref, cum_ref, weight_ref):
    cum = running_sum(logd_ref[...])
    cum_ref[...] = cum
    weight_ref[...] = jnp.exp(cum[:, cum.shape[1] - 1 :] - cum)


def part_columns(place_ref, size, away, cols):
    return pl.ds(pl.multiple_of(part_of(place_ref, size, away) * cols, cols), cols)


def early_kernel(size, count, width, place_ref, logd_in, key_in, value_in, *refs):
    pay_refs = refs[: size - 1]
    key_ref, value_ref, logd_ref, cum_ref, weight_ref, logd_sem, sems = refs[size - 1 :]
    logd = pltpu.make_async_copy(logd_in, logd_ref, logd_sem)
    keys, values = copies_of(key_in, key_ref, sems.at[0]), copies_of(value_in, value_ref, sems.at[1])
    for copy in (logd, *keys, *values):
        copy.start()
    logd.wait()
    put_sums(logd_ref, cum_ref, weight_ref)
    for copy in keys + values:
        copy.wait()
    for away in range(1, size):
        part = part_of(place_ref, size, away)
        here = part_columns(place_ref, size, away, count * width)
        turned = turned_keys(part, count, width, key_ref[:, here], weight_ref)
        put_states(part, count, width, turned, value_ref[:, here], cum_ref, pay_refs[away - 1])


def early_states(place, logd, key, value, size, count, width):
    heads, rows = logd.shape
    *pays, key, value = pl.pallas_call(
        functools.partial(early_kernel, size, count, width),
        in_specs=[SMEM] + [ANY] * 3,
        out_specs=[VMEM] * (size + 1),
        out_shape=[pay_shape(count, width, BF16)] * (size - 1) + [held(key.shape, BF16)] * 2,
        scratch_shapes=[pltpu.VMEM((heads, rows), F32)] * 3
        + [pltpu.SemaphoreType.DMA, pltpu.SemaphoreType.DMA((2, 1))],
        compiler_params=PACKED,
        name="early_states",
    )(place, outside(logd), outside(key), outside(value))
    return pays, key, value


def load_kernel(size, count, width, place_ref, logd_in, query_in, key_ref, value_ref, hold_ref, *refs):
    pay_ref, query_ref, cum_ref, logd_ref, weight_ref, logd_sem, sems = refs
    logd = pltpu.make_async_copy(logd_in, logd_ref, logd_sem)
    logd.start()
    copies = copies_of(query_in, query_ref, sems)
    for copy in copies:
        copy.start()
    logd.wait()
    put_sums(logd_ref, cum_ref, weight_ref)
    here = part_columns(place_ref, size, 0, count * width)
    part = part_of(place_ref, size, 0)
    keyed = turned_keys(part, count, width, key_ref[:, here], weight_ref)
    put_states(part, count, width, keyed, value_ref[:, here], cum_ref, pay_ref)
    for copy in copies:
        copy.wait()


def load(place, logd, key, value, query, hold, size, count, width):
    heads, rows = logd.shape
    return pl.pallas_call(
        functools.partial(load_kernel, size, count, width),
        in_specs=[SMEM, ANY, ANY, VMEM, VMEM, ANY],
        out_specs=[VMEM] * 3,
        out_shape=[
            pay_shape(count, width, F32),
            held(query.shape, BF16),
            held((heads, rows), F32),
        ],
        scratch_shapes=[pltpu.VMEM((heads, rows), F32)] * 2
        + [pltpu.SemaphoreType.DMA, pltpu.SemaphoreType.DMA((2,))],
        compiler_params=PACKED,
        name="load",
    )(place, outside(logd), outside(query), near(key), near(value), hold)


def decay_row(pay, j, count, width):
    at = count * width + j
    pad = pad_rows(count)
    return pay[at : at + 1, :].astype(F32) + pay[at + pad : at + pad + 1, :].astype(F32)


def put_decays(ref, rows, count, width):
    pad = pad_rows(count)
    blank = [jnp.zeros((1, width), F32)] * (pad - count)
    if ref.dtype == BF16:
        highs = [row.astype(BF16).astype(F32) for row in rows]
        lows = [row - high for row, high in zip(rows, highs)]
    else:
        highs, lows = rows, [jnp.zeros_like(row) for row in rows]
    tail = jnp.concatenate(highs + blank + lows + blank, axis=0)
    ref[count * width :, :] = tail.astype(ref.dtype)


def picked(values, index):
    found = values[0]
    for i in range(1, len(values)):
        found = jnp.where(index == i, values[i], found)
    return found


def gather_kernel(size, count, width, place_ref, *refs):
    in_refs, pay_ref, past_refs = refs[:size], refs[size], refs[size + 1 : 2 * size]
    window_refs = refs[2 * size :]
    decays = [[] for _ in range(size)]
    for j in range(count):
        rows = slice(j * width, (j + 1) * width)
        found = [ref[rows, :].astype(F32) for ref in in_refs]
        found_decays = [decay_row(ref, j, count, width) for ref in in_refs]
        total, total_decay = None, None
        for b in range(size):
            index = part_of(place_ref, size, b)
            state, decay = picked(found, index), picked(found_decays, index)
            if b:
                past_refs[b - 1][rows, :] = total
                decays[b - 1].append(total_decay)
                total, total_decay = total * decay + state, total_decay * decay
            else:
                total, total_decay = state, decay
        for ref in (pay_ref, *window_refs):
            ref[rows, :] = total.astype(ref.dtype)
        decays[-1].append(total_decay)
    for ref, rows in zip(past_refs, decays):
        put_decays(ref, rows, count, width)
    for ref in (pay_ref, *window_refs):
        put_decays(ref, decays[-1], count, width)


def gather(place, own, met, size, count, width, keep):
    shape = own.shape
    pay, *past = pl.pallas_call(
        functools.partial(gather_kernel, size, count, width),
        in_specs=[SMEM] + [VMEM] * size,
        out_specs=[VMEM] * (size + keep),
        out_shape=[held(shape, BF16)] + [held(shape, F32)] * (size - 1 + keep),
        compiler_params=PARAMS,
        name="gather",
    )(place, near(own), *map(near, met))
    return pay, past[: size - 1], past[-1]


def widen_kernel(count, width, bit, opening, keep, place_ref, got_ref, window_ref, before_ref, pay_ref, past_ref, *refs):
    is_later = (place_ref[0] & bit) != 0
    decays, pasts = [], []
    for j in range(count):
        rows = slice(j * width, (j + 1) * width)
        got, window = got_ref[rows, :].astype(F32), window_ref[rows, :]
        got_decay = decay_row(got_ref, j, count, width)
        window_decay = decay_row(window_ref, j, count, width)
        wide = jnp.where(is_later, got, window) * jnp.where(
            is_later, window_decay, got_decay
        ) + jnp.where(is_later, window, got)
        pay_ref[rows, :] = wide.astype(pay_ref.dtype)
        if keep:
            refs[0][rows, :] = wide
        decays.append(got_decay * window_decay)
        if opening:
            past_ref[rows, :] = jnp.where(is_later, got, jnp.zeros_like(got))
            pasts.append(jnp.where(is_later, got_decay, jnp.ones_like(got_decay)))
        else:
            before = before_ref[rows, :]
            before_decay = decay_row(before_ref, j, count, width)
            past_ref[rows, :] = jnp.where(is_later, got * before_decay + before, before)
            pasts.append(jnp.where(is_later, got_decay * before_decay, before_decay))
    put_decays(pay_ref, decays, count, width)
    if keep:
        put_decays(refs[0], decays, count, width)
    put_decays(past_ref, pasts, count, width)


def widen(place, got, window, before, count, width, bit, keep):
    shape = got.shape
    opening = before is None
    before = window if before is None else before
    done = pl.pallas_call(
        functools.partial(widen_kernel, count, width, bit, opening, keep),
        in_specs=[SMEM, VMEM, VMEM, VMEM],
        out_specs=[VMEM] * (2 + keep),
        out_shape=[held(shape, BF16), held(shape, F32)] + [held(shape, F32)] * keep,
        compiler_params=PARAMS,
        name="widen",
    )(place, near(got), near(window), near(before))
    return done if keep else (*done, None)


def enter_kernel(size, count, width, bit, opening, place_ref, got_ref, before_ref, *refs):
    past_refs, out_refs = refs[: size - 1], refs[size - 1 :]
    is_later = (place_ref[0] & bit) != 0
    for j in range(count):
        rows = slice(j * width, (j + 1) * width)
        before = jnp.zeros((width, width), F32)
        if bit:
            got = got_ref[rows, :].astype(F32)
            if not opening:
                before = before_ref[rows, :]
                got = got * decay_row(before_ref, j, count, width) + before
            before = jnp.where(is_later, got, before)
        entering = [before] + [
            before * decay_row(ref, j, count, width) + ref[rows, :] for ref in past_refs
        ]
        for away in range(size):
            index = part_of(place_ref, size, away)
            out_refs[away][rows, :] = picked(entering, index).astype(BF16)


def enter(place, got, before, past, size, count, width, bit):
    opening = before is None
    got = past[0] if got is None else got
    before = past[0] if opening else before
    return pl.pallas_call(
        functools.partial(enter_kernel, size, count, width, bit, opening),
        in_specs=[SMEM] + [VMEM] * (size + 1),
        out_specs=[VMEM] * size,
        out_shape=[held((count * width, width), BF16)] * size,
        compiler_params=PARAMS,
        name="enter",
    )(place, near(got), near(before), *map(near, past))


def local_kernel(size, count, width, away, place_ref, cum_ref, q_ref, k_ref, v_ref, out_ref, decayed_ref):
    part = part_of(place_ref, size, away)
    sums = [cum_ref[pl.ds(part * count + j, 1), :] for j in range(count)]
    rows = cum_ref.shape[1]
    tile = tile_of(rows, 2 * width)
    causal = lax.broadcasted_iota(jnp.int32, (tile, tile), 0) >= lax.broadcasted_iota(
        jnp.int32, (tile, tile), 1
    )

    def downward(row):
        turned = jnp.broadcast_to(row, (width, tile)).T
        return jnp.concatenate([turned] * (tile // width), axis=1)

    def columns(j):
        return pl.ds(pl.multiple_of((part * count + j) * width, width), width)

    def scores(j, i):
        return lax.dot_general(
            q_ref[i * tile : (i + 1) * tile, columns(j)],
            k_ref[: (i + 1) * tile, columns(j)],
            (((1,), (1,)), ((), ())),
            preferred_element_type=F32,
        )

    def weighted(j, i, found):
        cum = sums[j]
        here = slice(i * tile, (i + 1) * tile)
        across = cum[:, here]
        down = downward(across)
        weight = jnp.exp(jnp.where(causal, down - across, -jnp.inf))
        near_part = (found[:, i * tile :] * weight).astype(BF16)
        if i == 0:
            return near_part, None, None, jnp.exp(down)
        edge = cum[:, i * tile - 1 : i * tile]
        since = jnp.exp(down - edge)
        far_part = (found[:, : i * tile] * jnp.exp(edge - cum[:, : i * tile])).astype(BF16)
        return near_part, far_part, since, since * jnp.exp(edge)

    def finish(j, i, near_part, far_part, since, decay):
        cols = slice(j * width, (j + 1) * width)
        from_cols = columns(j)
        here = slice(i * tile, (i + 1) * tile)
        out = jnp.dot(near_part, v_ref[here, from_cols], preferred_element_type=F32)
        if far_part is not None:
            out = out + since[:, :width] * jnp.dot(
                far_part, v_ref[: i * tile, from_cols], preferred_element_type=F32
            )
        out_ref[here, cols] = out
        decayed_ref[here, cols] = (
            q_ref[here, columns(j)].astype(F32) * decay[:, :width]
        ).astype(BF16)

    units = [(j, i) for i in range(rows // tile) for j in range(count)]
    found, held_parts = {}, {}
    for step in range(len(units) + 3):
        if step < len(units):
            found[step] = scores(*units[step])
        if 0 <= step - 2 < len(units):
            held_parts[step - 2] = weighted(*units[step - 2], found.pop(step - 2))
        if 0 <= step - 3:
            finish(*units[step - 3], *held_parts.pop(step - 3))


def local(place, cum, query, key, value, size, count, width, away):
    rows = cum.shape[1]
    cols = count * width
    return pl.pallas_call(
        functools.partial(local_kernel, size, count, width, away),
        in_specs=[SMEM] + [VMEM] * 4,
        out_specs=[VMEM, VMEM],
        out_shape=[held((rows, cols), F32), held((rows, cols), BF16)],
        compiler_params=PARAMS,
        name="local",
    )(place, near(cum), near(query), near(key), near(value))


def norm_kernel(size, count, width, chips, block, away, group, place_ref, chip_ref, core_ref, gain_ref, *refs):
    members = len(group)
    inside_refs, query_refs = refs[:members], refs[members : 2 * members]
    state_refs, out_ref = refs[2 * members : -1], refs[-1]
    ones = jnp.full((width, width), 1.0 / width, F32).astype(BF16)
    units = [(at, j) for at in range(members) for j in range(count)]

    def rows_of(ref, j):
        src = slice(j * width, (j + 1) * width)
        found = []
        for i in range(chips):
            spot = 2 * lax.rem(chip_ref[0] + i, chips)
            spot = spot + (1 - core_ref[0] if away else core_ref[0])
            found.append(ref[pl.ds(pl.multiple_of(spot * block, block), block), src])
        return jnp.concatenate(found, axis=0)

    def carry(at, j):
        state = state_refs[at][j * width : (j + 1) * width, :]
        return jnp.dot(rows_of(query_refs[at], j), state, preferred_element_type=F32)

    def square(at, j, carried):
        attended = rows_of(inside_refs[at], j) + carried
        return attended, jnp.dot(
            (attended * attended).astype(BF16), ones, preferred_element_type=F32
        )

    def finish_head(at, j, attended, mean):
        gain = gain_ref[pl.ds(part_of(place_ref, size, group[at]) * count + j, 1), :]
        col = (at * count + j) * width
        out_ref[:, col : col + width] = (
            attended * lax.rsqrt(mean + 1e-06) * gain
        ).astype(out_ref.dtype)

    first, second = {}, {}
    for step in range(len(units) + 2):
        if step < len(units):
            first[step] = carry(*units[step])
        if 0 <= step - 1 < len(units):
            second[step - 1] = square(*units[step - 1], first.pop(step - 1))
        if 0 <= step - 2:
            finish_head(*units[step - 2], *second.pop(step - 2))


def norm(group, scalars, gain, insides, queries, entering, size, count, width, chips, block, away):
    cols = len(group) * count * width
    parts = [a[i] for a in (insides, queries, entering) for i in group]
    return pl.pallas_call(
        functools.partial(norm_kernel, size, count, width, chips, block, away, group),
        in_specs=[SMEM] * 3 + [VMEM] * (1 + len(parts)),
        out_specs=VMEM,
        out_shape=held((chips * block, cols), BF16),
        compiler_params=PARAMS,
        name="norm_away" if away else "norm_home",
    )(*scalars, gain, *map(near, parts))


def summed(size, place_ref, terms, span, total=None):
    for ref, at, away, weight_ref in terms:
        cols = weight_ref.shape[0] // size
        rows = part_columns(place_ref, size, away, cols)
        part = jnp.dot(
            ref[:, at * cols : (at + 1) * cols], weight_ref[rows, span], preferred_element_type=F32
        )
        total = part if total is None else total + part
    return total


def begin_kernel(size, place_ref, home_ref, met_ref, near_ref, far_ref, out_ref):
    order = order_of(size)
    terms = [(met_ref, at, away, far_ref) for at, away in enumerate(order[:-1])]
    terms += [(home_ref, at, away, near_ref) for at, away in enumerate(order)]
    out_ref[...] = summed(size, place_ref, terms, slice(0, out_ref.shape[1]))


def begin(place, home, met, first_weight, second_weight, count, size):
    rows = met.shape[0]
    return pl.pallas_call(
        functools.partial(begin_kernel, size),
        in_specs=[SMEM] + [VMEM] * 4,
        out_specs=VMEM,
        out_shape=held((rows, count), F32),
        compiler_params=PARAMS,
        name="begin",
    )(place, *map(near, [home, met, first_weight, second_weight]))


def complete_kernel(block, size, place_ref, begun_ref, two_ref, far_ref, own_ref, away_ref):
    span = slice(0, own_ref.shape[1])
    total = summed(size, place_ref, [(two_ref, 0, order_of(size)[-1], far_ref)], span, begun_ref[...])
    own_ref[...] = total[:block]
    away_ref[...] = total[block:].astype(away_ref.dtype)


def complete(place, begun, two, second_weight, block, size):
    rows, count = begun.shape
    return pl.pallas_call(
        functools.partial(complete_kernel, block, size),
        in_specs=[SMEM] + [VMEM] * 3,
        out_specs=[VMEM, VMEM],
        out_shape=[held((block, count), F32), held((rows - block, count), BF16)],
        compiler_params=PARAMS,
        name="complete",
    )(place, near(begun), near(two), near(second_weight))


def project_kernel(block, first, tile, size, place_ref, *refs):
    own_ref, away_ref = refs[-2:]
    home_ref, one_ref, two_ref, near_ref, far_ref = refs[:5]
    order = order_of(size)
    terms = [(home_ref, at, away, near_ref) for at, away in enumerate(order)]
    terms += [(one_ref, at, away, far_ref) for at, away in enumerate(order[:-1])]
    terms += [(two_ref, 0, order[-1], far_ref)]
    for i in range(own_ref.shape[1] // tile):
        here = slice(i * tile, (i + 1) * tile)
        span = slice(first + i * tile, first + (i + 1) * tile)
        total = summed(size, place_ref, terms, span)
        own_ref[:, here] = total[:block]
        away_ref[:, here] = total[block:].astype(away_ref.dtype)


def project(place, home, other, first_weight, second_weight, hold, block, first, count, tile, size):
    rows = home.shape[0]
    tile = tile_of(count, tile)
    return pl.pallas_call(
        functools.partial(project_kernel, block, first, tile, size),
        in_specs=[SMEM] + [VMEM] * 5 + [ANY],
        out_specs=[VMEM, VMEM],
        out_shape=[held((block, count), F32), held((rows - block, count), BF16)],
        compiler_params=PARAMS,
        name="project",
    )(place, *map(near, [home, *other, first_weight, second_weight]), hold)


def finish_kernel(first, pieces, own_ref, residual_ref, *refs):
    part_refs, (out_ref, total_ref, sems) = refs[:pieces], refs[-3:]
    count = own_ref.shape[1]
    total = own_ref[...] + residual_ref[:, first : first + count].astype(F32)
    for ref in part_refs:
        total = total + ref[...].astype(F32)
    total_ref[...] = total.astype(BF16)
    rows = total_ref.shape[0] // sems.shape[0]
    copies = []
    for i in range(sems.shape[0]):
        here = pl.ds(i * rows, rows)
        copies.append(
            pltpu.make_async_copy(
                total_ref.at[here, :], out_ref.at[here, pl.ds(first, count)], sems.at[i]
            )
        )
    for copy in copies:
        copy.start()
    for copy in copies:
        copy.wait()


def finish(out, own, residual, parts, first):
    block, total = residual.shape
    earlier = [] if out is None else [outside(out)]
    return pl.pallas_call(
        functools.partial(finish_kernel, first, len(parts)),
        in_specs=[VMEM] * (2 + len(parts)) + [ANY] * len(earlier),
        out_specs=ANY,
        out_shape=pltpu.HBM((block, total), BF16),
        scratch_shapes=[
            pltpu.VMEM((block, own.shape[1]), BF16),
            pltpu.SemaphoreType.DMA((1,)),
        ],
        input_output_aliases={2 + len(parts): 0} if earlier else {},
        compiler_params=PARAMS,
        name="finish",
    )(near(own), near(residual), *map(near, parts), *earlier)


def shards(blocks, group, q_spikes, k_spikes, v_spikes, log_decay, norm_gain, out_weight, residual):
    rows, heads = log_decay.shape
    width = q_spikes.shape[1] // heads
    size = 4 if heads % 4 == 0 and blocks % 4 == 0 else 2
    count = heads // size
    chips = group // 2
    block = rows // group
    place = lax.axis_index("ctx").astype(jnp.int32)
    member = lax.axis_index("exp").astype(jnp.int32)
    place, chip, core = lax.optimization_barrier(
        tuple(a.reshape(1) for a in (place, member >> 1, member & 1))
    )
    cores = [(i, i ^ 1) for i in range(group)]

    def swap(x, bit):
        return lax.ppermute(x, "ctx", [(i, i ^ bit) for i in range(blocks)])

    logd = log_decay.T
    if heads % 8:
        logd = jnp.pad(logd, ((0, pad_rows(heads) - heads), (0, 0)))
    sent, key, value = early_states(place, logd, k_spikes, v_spikes, size, count, width)
    met = [swap(a, i + 1) for i, a in enumerate(sent)]
    kept, query, cum = load(place, logd, key, value, q_spikes, sent[0], size, count, width)
    kept, weight = lax.optimization_barrier((kept, out_weight))
    far_weight = lax.ppermute(outside(weight), "exp", cores)
    total = out_weight.shape[1]
    tile = tile_of(total, 512)

    pay, past, window = gather(place, kept, met, size, count, width, int(2 * size < blocks))
    _, own_weight = lax.optimization_barrier((pay, out_weight))
    before, got, level, bit = None, None, 0, size
    while bit < blocks:
        got = swap(pay, bit)
        if 2 * bit < blocks:
            pay, before, window = widen(
                place, got, window, before, count, width, bit, int(4 * bit < blocks)
            )
        bit, level = 2 * bit, level + 1
    own, *theirs = enter(place, got, before, past, size, count, width, bit // 2 if level else 0)
    entering = [own] + [swap(a, i + 1) for i, a in enumerate(theirs)]

    insides, queries = [], []
    for away in range(size):
        inside, decayed = local(place, cum, query, key, value, size, count, width, away)
        insides.append(inside)
        queries.append(decayed)

    gain = norm_gain.reshape(heads, width)
    order = order_of(size)
    other = []

    def normed(which, away):
        return norm(
            tuple(which), (place, chip, core), gain, insides, queries, entering,
            size, count, width, chips, block, away,
        )

    for which in (order[:-1], order[-1:]):
        away = normed(which, True)
        other.append(lax.ppermute(away, "exp", cores))
    home = normed(order, False)

    sizes = [tile, tile]
    while total - sum(sizes) > 2 * tile:
        sizes.append(2 * tile)
    rest = total - sum(sizes)
    sizes += [rest - tile // 2, tile // 2] if rest > tile // 2 else [rest]
    begun = begin(place, home, other[0], own_weight, far_weight, sizes[0], size)
    out, at, hold = None, 0, None
    sums = []
    for index, span in enumerate(sizes):
        if index:
            own, pieces = project(
                place, home, other, own_weight, far_weight, hold, block, at, span, tile, size
            )
        else:
            own, pieces = complete(place, begun, other[1], far_weight, block, size)
        hold = pieces
        got = []
        for d in range(1, chips):
            piece = pieces[(d - 1) * block : d * block]
            perm = [(i, 2 * ((i // 2 + d) % chips) + i % 2) for i in range(group)]
            got.append(lax.ppermute(piece, "exp", perm))
        sums.append((own, got, at))
        at += span
    for own, got, at in sums:
        out = finish(out, own, residual, got, at)
    return out


def solution(mesh):
    in_specs = (
        P("ctx", "exp"),
        P("ctx", "exp"),
        P("ctx", "exp"),
        P("ctx", "exp"),
        P("exp"),
        P("exp", None),
        P(("ctx", "exp"), None),
    )
    out_specs = P(("ctx", "exp"), None)

    def body(*args):
        return shards(mesh.shape["ctx"], mesh.shape["exp"], *args)

    return jax.shard_map(
        body, mesh=mesh, in_specs=in_specs, out_specs=out_specs, check_vma=False
    )
```
